32 devices in a mesh: rep: 8 (over z, x), shard: 4 (over y, core).
Axes of the slice: x: 2, y: 2, z: 4, core: 2. Of those that a mesh axis runs over, the one named last changes fastest.
Arguments:
- tokens: bfloat16 [16384, 1024], P(('rep', 'shard')), may hold values from -6 to 6
- seq_lengths: int32 [8, 8], P('rep'), may hold values from 128 to 384, as said below
- owner_order: int32 [8, 8], P('rep'), may hold values from 0 to 7, as said below
- gain_attn: bfloat16 [1024], P('shard'), may hold values from 0.5 to 1.5
- w_input: bfloat16 [1024, 4096], P('shard'), may hold values from -0.1875 to 0.1875
- w_step: bfloat16 [1024, 24], P('shard'), may hold values from -0.046875 to 0.046875
- step_bias: bfloat16 [24], P('shard'), may hold values from -4 to -1
- decay_log: bfloat16 [24], P('shard'), may hold values from 0 to 2.6875
- skip_scale: bfloat16 [24], P('shard'), may hold values from 0.5 to 1.5
- conv_weight: bfloat16 [4, 1792], P(None, 'shard'), may hold values from -3 to 3
- conv_bias: bfloat16 [1792], P('shard'), may hold values from -1.5 to 1.5
- gain_ssm: bfloat16 [1536], P('shard'), may hold values from 0.5 to 1.5
- w_output: bfloat16 [2048, 1024], P('shard'), may hold values from -0.1875 to 0.1875
- gain_ffn: bfloat16 [1024], P('shard'), may hold values from 0.5 to 1.5
- w_gate_up: bfloat16 [1024, 4096], P('shard'), may hold values from -0.1875 to 0.1875
- w_down: bfloat16 [2048, 1024], P('shard'), may hold values from -0.125 to 0.125
- cotangent: bfloat16 [16384, 1024], P(('rep', 'shard')), may hold values from -6 to 6
Outputs:
- block_out: bfloat16 [16384, 1024], P(('rep', 'shard'))
- grad_tokens: bfloat16 [16384, 1024], P(('rep', 'shard'))
- grad_gain_attn: float32 [1024], P('shard')
- grad_w_input: float32 [1024, 4096], P('shard')
- grad_w_step: float32 [1024, 24], P('shard')
- grad_step_bias: float32 [24], P('shard')
- grad_decay_log: float32 [24], P('shard')
- grad_skip_scale: float32 [24], P('shard')
- grad_conv_weight: float32 [4, 1792], P(None, 'shard')
- grad_conv_bias: float32 [1792], P('shard')
- grad_gain_ssm: float32 [1536], P('shard')
- grad_w_output: float32 [2048, 1024], P('shard')
- grad_gain_ffn: float32 [1024], P('shard')
- grad_w_gate_up: float32 [1024, 4096], P('shard')
- grad_w_down: float32 [2048, 1024], P('shard')
The draws below stay inside these ranges and needn't reach their ends.
Inputs may be any that keep to these rules, and one draw needn't show every extreme that they name: `seq_lengths`: device d of a group (index along shard) owns the sequences at owner positions 2d and 2d+1, whose lengths sum to 512; in every group one sequence has exactly 128 tokens and its partner 512 - 128. `owner_order`: each row is a permutation of the group's 8 sequences.
All inputs are finite; a program needn't handle non-finite values.
Results may differ from the reference program's by a relative error of at most 0.012.
Values may be sent and summed in bfloat16 or wider, within the bound.
No kernel may reach another device: no remote copies, remote signals or barrier semaphores. Data moves between devices by JAX's collectives and lax.ppermute only.
A program may use at most 384 MiB of HBM per device.

```python
import math
import jax
import jax.numpy as jnp
from jax import lax

D = 1024
FF = 2048
QUERY_HEADS = 8
KEY_VALUE_HEADS = 2
HEAD_SIZE = 64
SSM_HEADS = 24
SSM_HD = 64
STATE = 128
CONV = 4
TOK_DEV = 512
INNER = 1536
QUERY_KEY_VALUE = 768
XBC = 1792
PROJ = 4096
CAT = 2048
MINLEN = 128
GROUPS = 8
GROUP_SEQS = 8
TOKENS = 16384


def pair_tables(key):
    key_len, key_force, key_perm = jax.random.split(jax.random.fold_in(key, 7), 3)
    pairs = GROUP_SEQS // 2
    first = jax.random.randint(key_len, (GROUPS, pairs), MINLEN, TOK_DEV - MINLEN + 1)
    forced = jax.random.randint(key_force, (GROUPS, 1), 0, pairs)
    first = jnp.where(jnp.arange(pairs)[None, :] == forced, MINLEN, first)
    owner_len = jnp.stack([first, TOK_DEV - first], 2).reshape(GROUPS, GROUP_SEQS)

    def shuffle(group_key):
        return jax.random.permutation(group_key, GROUP_SEQS)
    order = jax.vmap(shuffle)(jax.random.split(key_perm, GROUPS)).astype(jnp.int32)
    lengths = jnp.zeros((GROUPS, GROUP_SEQS), jnp.int32).at[jnp.arange(GROUPS)[:, None], order].set(owner_len.astype(jnp.int32))
    return (lengths, order)


def draw_seq_lengths(key, part):
    return pair_tables(key)[0]


def draw_owner_order(key, part):
    return pair_tables(key)[1]


def steps_of(own_key, shape, cuts, smallest, largest):
    level = 1.0
    for dim, blocks in cuts:
        draws = jax.random.uniform(jax.random.fold_in(jax.random.fold_in(own_key, 6), dim), (blocks,), jnp.float32, smallest / len(cuts), largest / len(cuts))
        level = level * jnp.repeat(jnp.exp(draws), shape[dim] // blocks).reshape((-1,) + (1,) * (len(shape) - 1 - dim))
    return level


def normal_values(own_key, dims, scale, reach, shards=(), kind=jnp.bfloat16):
    loudness = steps_of(own_key, dims, shards, -0.22, 0.18) if shards else 1.0
    entries = jax.random.normal(own_key, dims, jnp.float32) * scale * loudness
    return jnp.minimum(jnp.maximum(entries, -reach), reach).astype(kind)


def setup_inputs(seed: int = 0) -> dict:
    keys = jax.random.split(jax.random.key(seed), 18)
    tokens = normal_values(keys[0], (TOKENS, D), 1.0, 6.0, ((0, 32),))
    seq_lengths = draw_seq_lengths(jax.random.fold_in(keys[17], 71), 0)
    owner_order = draw_owner_order(jax.random.fold_in(keys[17], 71), 0)
    gain_attn = jnp.clip(1.0 + 0.1 * jax.random.normal(keys[3], (D,), jnp.float32), 0.5, 1.5).astype(jnp.bfloat16)
    w_input = normal_values(keys[4], (D, PROJ), D ** -0.5, 0.1875, ((0, 4),))
    w_step = normal_values(keys[5], (D, SSM_HEADS), (16 * D) ** -0.5, 0.046875, ((0, 4),))
    step_bias = jnp.clip(-4.0 + 3.0 * jax.random.uniform(keys[6], (SSM_HEADS,), jnp.float32) ** steps_of(keys[6], (SSM_HEADS,), ((0, 4),), -0.2, 0.2), -4.0, -1.0).astype(jnp.bfloat16)
    decay_log = jnp.clip(2.6875 * jax.random.uniform(keys[7], (SSM_HEADS,), jnp.float32) ** steps_of(keys[7], (SSM_HEADS,), ((0, 4),), -0.2, 0.2), 0.0, 2.6875).astype(jnp.bfloat16)
    skip_scale = jnp.clip(0.5 + 1.0 * jax.random.uniform(keys[8], (SSM_HEADS,), jnp.float32) ** steps_of(keys[8], (SSM_HEADS,), ((0, 4),), -0.2, 0.2), 0.5, 1.5).astype(jnp.bfloat16)
    conv_weight = normal_values(keys[9], (CONV, XBC), CONV ** -0.5, 3.0, ((1, 4),))
    conv_bias = normal_values(keys[10], (XBC,), 0.3, 1.5, ((0, 4),))
    gain_ssm = jnp.clip(1.0 + 0.1 * jax.random.normal(keys[11], (INNER,), jnp.float32), 0.5, 1.5).astype(jnp.bfloat16)
    w_output = normal_values(keys[12], (CAT, D), (CAT // 2) ** -0.5, 0.1875, ((0, 4),))
    gain_ffn = jnp.clip(1.0 + 0.1 * jax.random.normal(keys[13], (D,), jnp.float32), 0.5, 1.5).astype(jnp.bfloat16)
    w_gate_up = normal_values(keys[14], (D, 2 * FF), D ** -0.5, 0.1875, ((0, 4),))
    w_down = normal_values(keys[15], (FF, D), FF ** -0.5, 0.125, ((0, 4),))
    cotangent = normal_values(keys[16], (TOKENS, D), 1.0, 6.0, ((0, 32),))
    return dict(tokens=tokens, seq_lengths=seq_lengths, owner_order=owner_order, gain_attn=gain_attn, w_input=w_input, w_step=w_step, step_bias=step_bias, decay_log=decay_log, skip_scale=skip_scale, conv_weight=conv_weight, conv_bias=conv_bias, gain_ssm=gain_ssm, w_output=w_output, gain_ffn=gain_ffn, w_gate_up=w_gate_up, w_down=w_down, cotangent=cotangent)


EPS = 1e-05
ROPE_BASE = 100000000000.0
FULL_PRECISION = lax.Precision.HIGHEST

@jax.custom_vjp
def reduced_precision(v):
    return lax.optimization_barrier(v.astype(jnp.bfloat16)).astype(jnp.float32)

@jax.custom_vjp
def reduced_backward(v):
    return v

def low_keep(v):
    return (reduced_precision(v), None)

def low_pass(kept, grad):
    return (grad,)

def back_keep(v):
    return (v, None)

def back_low(kept, grad):
    return (reduced_precision(grad),)
reduced_precision.defvjp(low_keep, low_pass)
reduced_backward.defvjp(back_keep, back_low)

def product(left, right):
    return jnp.dot(left, right, precision=FULL_PRECISION)

def rms_scale(values):
    return lax.rsqrt(lax.optimization_barrier(jnp.mean(values * values, axis=-1, keepdims=True)) + EPS)

def rms_norm(values, gain):
    return values * rms_scale(values) * gain

def rope_angles(position, head_dim):
    half = head_dim // 2
    ladder = jnp.arange(half, dtype=jnp.float32) * (2.0 / head_dim)
    return position.astype(jnp.float32)[:, None] * jnp.exp(-math.log(ROPE_BASE) * ladder)

def apply_rotary(values, rotary_angles):
    half = values.shape[-1] // 2
    cosine = jnp.cos(rotary_angles)[:, None, :]
    sine = jnp.sin(rotary_angles)[:, None, :]
    first = values[..., :half]
    second = values[..., half:]
    return jnp.concatenate([first * cosine - second * sine, second * cosine + first * sine], -1)

def conv_silu(conv_in, conv_weight, conv_bias, segment):
    taps = conv_weight.shape[0]
    width = conv_in.shape[1]
    mixed = conv_bias + conv_in * conv_weight[taps - 1]
    for back in range(1, taps):
        shifted = jnp.concatenate([jnp.zeros((back, width), jnp.float32), conv_in[:-back]], 0)
        same = jnp.concatenate([jnp.zeros((back,), jnp.float32), (segment[back:] == segment[:-back]).astype(jnp.float32)], 0)
        mixed = mixed + shifted * same[:, None] * conv_weight[taps - 1 - back]
    return jax.nn.silu(mixed)

def gated_norm(ssm_y, gate_z, gain):
    gated = ssm_y * jax.nn.silu(gate_z)
    return gated * rms_scale(gated) * gain

def swiglu(gate_up):
    half = gate_up.shape[1] // 2
    return jax.nn.silu(gate_up[:, :half]) * gate_up[:, half:]

def bin_forward(weights, tokens, position, segment):
    gain_attn, w_input, w_step, step_bias, decay_log, skip_scale, conv_weight, conv_bias, gain_ssm, w_output, gain_ffn, w_gate_up, w_down = weights
    input_rows = tokens.shape[0]
    normed = reduced_precision(rms_norm(tokens, gain_attn))
    projected_rows = reduced_backward(product(normed, w_input))
    step_raw = reduced_backward(product(normed, w_step))
    rotary_angles = rope_angles(position, HEAD_SIZE)
    query_rows = reduced_precision(apply_rotary(projected_rows[:, :QUERY_HEADS * HEAD_SIZE].reshape(input_rows, QUERY_HEADS, HEAD_SIZE), rotary_angles))
    key_matrix = reduced_precision(apply_rotary(projected_rows[:, QUERY_HEADS * HEAD_SIZE:QUERY_KEY_VALUE - KEY_VALUE_HEADS * HEAD_SIZE].reshape(input_rows, KEY_VALUE_HEADS, HEAD_SIZE), rotary_angles))
    value_matrix = reduced_precision(projected_rows[:, QUERY_KEY_VALUE - KEY_VALUE_HEADS * HEAD_SIZE:QUERY_KEY_VALUE].reshape(input_rows, KEY_VALUE_HEADS, HEAD_SIZE))
    gate_z = projected_rows[:, QUERY_KEY_VALUE:QUERY_KEY_VALUE + INNER]
    conv_out = conv_silu(projected_rows[:, QUERY_KEY_VALUE + INNER:], conv_weight, conv_bias, segment)
    inner_x = conv_out[:, :INNER].reshape(input_rows, SSM_HEADS, SSM_HD)
    b_low = reduced_precision(conv_out[:, INNER:INNER + STATE])
    c_low = reduced_precision(conv_out[:, INNER + STATE:])
    step = jax.nn.softplus(step_raw + step_bias)
    cumulative = jnp.cumsum(step * -jnp.exp(decay_log), axis=0)
    places = jnp.arange(input_rows)
    mask = ((places[None, :] <= places[:, None]) & (segment[None, :] == segment[:, None])).astype(jnp.float32)
    intersection = reduced_backward(product(c_low, b_low.T))
    log_gap = cumulative[:, None, :] - cumulative[None, :, :]
    decay = jnp.exp(jnp.where(mask[:, :, None] > 0, log_gap, 0.0)) * mask[:, :, None]
    mixer = reduced_precision(intersection[:, :, None] * (decay * step[None, :, :]))
    ssd_out = reduced_backward(jnp.einsum('ijh,jhd->ihd', mixer, reduced_precision(inner_x), precision=FULL_PRECISION))
    ssm_y = (ssd_out + skip_scale[None, :, None] * inner_x).reshape(input_rows, INNER)
    ssm_out = reduced_precision(gated_norm(ssm_y, gate_z, gain_ssm))
    head_group = QUERY_HEADS // KEY_VALUE_HEADS
    score_matrix = reduced_backward(jnp.einsum('mytl,byl->ytmb', query_rows.reshape(input_rows, KEY_VALUE_HEADS, head_group, HEAD_SIZE), key_matrix, precision=FULL_PRECISION)) * HEAD_SIZE ** (-0.5)
    score_matrix = jnp.where(mask[None, None] > 0, score_matrix, -1e+30)
    attn_weights = reduced_precision(jax.nn.softmax(score_matrix, axis=-1))
    attn_out = reduced_precision(reduced_backward(jnp.einsum('kgij,jkd->ikgd', attn_weights, value_matrix, precision=FULL_PRECISION))).reshape(input_rows, QUERY_HEADS * HEAD_SIZE)
    joined = jnp.concatenate([attn_out, ssm_out], 1)
    middle = tokens + reduced_backward(product(joined, w_output))
    normed_ffn = reduced_precision(rms_norm(middle, gain_ffn))
    hidden = reduced_precision(swiglu(reduced_backward(product(normed_ffn, w_gate_up))))
    return middle + reduced_backward(product(hidden, w_down))

def owner_maps(lengths, order):
    starts = (jnp.cumsum(lengths) - lengths).astype(jnp.int32)
    owner_len = lengths[order]
    first_len = owner_len[0::2]
    first_src = starts[order[0::2]]
    second_src = starts[order[1::2]]
    local = jnp.arange(TOK_DEV, dtype=jnp.int32)
    segment = (local[None, :] >= first_len[:, None]).astype(jnp.int32)
    position = (local[None, :] - segment * first_len[:, None]).astype(jnp.int32)
    source = (jnp.where(segment > 0, second_src[:, None], first_src[:, None]) + position).astype(jnp.int32)
    return (source, position, segment)

def reference(tokens, seq_lengths, owner_order, gain_attn, w_input, w_step, step_bias, decay_log, skip_scale, conv_weight, conv_bias, gain_ssm, w_output, gain_ffn, w_gate_up, w_down, cotangent):
    source, position, segment = jax.vmap(owner_maps)(seq_lengths, owner_order)
    base = jnp.arange(GROUPS, dtype=jnp.int32)[:, None, None] * (GROUP_SEQS // 2 * TOK_DEV)
    given_rows = (source + base).reshape(-1).astype(jnp.int32)
    bin_count = given_rows.shape[0] // TOK_DEV
    own_tokens = tokens.astype(jnp.float32)[given_rows].reshape(bin_count, TOK_DEV, D)
    own_cot = cotangent.astype(jnp.float32)[given_rows].reshape(bin_count, TOK_DEV, D)
    position = position.reshape(bin_count, TOK_DEV)
    segment = segment.reshape(bin_count, TOK_DEV)
    weights = (gain_attn, w_input, w_step, step_bias, decay_log, skip_scale, conv_weight, conv_bias, gain_ssm, w_output, gain_ffn, w_gate_up, w_down)
    weights = tuple((weight.astype(jnp.float32) for weight in weights))

    def forward(weight_set, inputs):

        def one_bin(packed):
            return jax.checkpoint(bin_forward)(weight_set, packed[0], packed[1], packed[2])
        return lax.map(one_bin, (inputs, position, segment))
    outputs, pullback = jax.vjp(forward, weights, own_tokens)
    grads, grad_own = pullback(own_cot)
    block_out = jnp.zeros((tokens.shape[0], D), jnp.float32).at[given_rows].set(outputs.reshape(-1, D))
    grad_tokens = jnp.zeros((tokens.shape[0], D), jnp.float32).at[given_rows].set(grad_own.reshape(-1, D))
    return (block_out.astype(jnp.bfloat16), grad_tokens.astype(jnp.bfloat16), grads[0], grads[1], grads[2], grads[3], grads[4], grads[5], grads[6], grads[7], grads[8], grads[9], grads[10], grads[11], grads[12])
```

```python
from functools import partial
import math

import jax
import jax.numpy as jnp
from jax import lax
from jax.sharding import PartitionSpec as P

QUERY_HEADS = 8
KEY_VALUE_HEADS = 2
HEAD_SIZE = 64
SSM_HEADS = 24
SSM_HD = 64
STATE = 128
INNER = 1536
QUERY_KEY_VALUE = 768


EPS = 1e-05
ROPE_BASE = 100000000000.0


def rms_scale(values):
    return lax.rsqrt(jnp.mean(values * values, axis=-1, keepdims=True) + EPS)


def rms_norm(values, gain):
    return values * rms_scale(values) * gain


def rope_angles(position, head_dim):
    half = head_dim // 2
    ladder = jnp.arange(half, dtype=jnp.float32) * (2.0 / head_dim)
    return position.astype(jnp.float32)[:, None] * jnp.exp(-math.log(ROPE_BASE) * ladder)


def apply_rotary(values, rotary_angles):
    half = values.shape[-1] // 2
    cosine = jnp.cos(rotary_angles)[:, None, :]
    sine = jnp.sin(rotary_angles)[:, None, :]
    first = values[..., :half]
    second = values[..., half:]
    return jnp.concatenate([first * cosine - second * sine, second * cosine + first * sine], -1)


def conv_silu(conv_in, conv_weight, conv_bias, segment):
    taps = conv_weight.shape[0]
    width = conv_in.shape[1]
    mixed = conv_bias + conv_in * conv_weight[taps - 1]
    for back in range(1, taps):
        shifted = jnp.concatenate([jnp.zeros((back, width), jnp.float32), conv_in[:-back]], 0)
        same = jnp.concatenate(
            [
                jnp.zeros((back,), jnp.float32),
                (segment[back:] == segment[:-back]).astype(jnp.float32),
            ],
            0,
        )
        mixed = mixed + shifted * same[:, None] * conv_weight[taps - 1 - back]
    return jax.nn.silu(mixed)


def gated_norm(ssm_y, gate_z, gain):
    gated = ssm_y * jax.nn.silu(gate_z)
    return gated * rms_scale(gated) * gain


def swiglu(gate_up):
    half = gate_up.shape[1] // 2
    return jax.nn.silu(gate_up[:, :half]) * gate_up[:, half:]


def group_tables(lengths, order, input_rows, device):
    count = lengths.shape[0]
    slots = jnp.arange(count, dtype=jnp.int32)
    starts = jnp.cumsum(lengths) - lengths
    pick = (order[:, None] == slots[None, :]).astype(jnp.int32)
    owner_len = jnp.sum(pick * lengths[None, :], 1)
    owner_start = jnp.cumsum(owner_len) - owner_len
    owner_src = jnp.sum(pick * starts[None, :], 1)
    first_len = jnp.sum(jnp.where(slots == 2 * device, owner_len, 0))
    first_src = jnp.sum(jnp.where(slots == 2 * device, owner_src, 0))
    second_src = jnp.sum(jnp.where(slots == 2 * device + 1, owner_src, 0))
    local = jnp.arange(input_rows, dtype=jnp.int32)
    segment = (local >= first_len).astype(jnp.int32)
    position = local - segment * first_len
    source = jnp.where(segment > 0, second_src, first_src) + position
    given = device * input_rows + local
    seq_id = jnp.sum((starts[None, :] <= given[:, None]).astype(jnp.int32), 1) - 1
    member = (seq_id[:, None] == slots[None, :]).astype(jnp.int32)
    seq_start = jnp.sum(member * starts[None, :], 1)
    seq_owner_start = jnp.sum(pick * owner_start[:, None], 0)
    target = jnp.sum(member * seq_owner_start[None, :], 1) + given - seq_start
    return (source, position, segment, target)


def block_mask(segment, count):
    places = jnp.arange(segment.shape[0])
    here = jnp.arange(count)
    return ((places[None, :] <= here[:, None]) & (segment[None, :] == segment[:, None])).astype(
        jnp.float32
    )


def attention_scores(grouped_heads, key_matrix, mask):
    score_matrix = jnp.einsum(
        "mytl,byl->ytmb", grouped_heads, key_matrix, preferred_element_type=jnp.float32
    ) * HEAD_SIZE ** (-0.5)
    return jnp.where(mask[None, None] > 0, score_matrix, -1e30)


def attention_forward(query_rows, key_matrix, value_matrix, segment):
    input_rows = query_rows.shape[0]
    hybrid_block = min(512, input_rows)
    head_group = QUERY_HEADS // KEY_VALUE_HEADS
    mask = block_mask(segment, hybrid_block)
    grouped_heads = query_rows.reshape(hybrid_block, KEY_VALUE_HEADS, head_group, HEAD_SIZE)
    score_matrix = attention_scores(grouped_heads, key_matrix, mask)
    largest = jnp.max(score_matrix, -1, keepdims=True)
    raised = jnp.exp(score_matrix - largest)
    total = jnp.sum(raised, -1, keepdims=True)
    attn_weights = (raised / total).astype(jnp.bfloat16)
    mixed = jnp.einsum(
        "kgij,jkd->ikgd", attn_weights, value_matrix, preferred_element_type=jnp.float32
    )
    outputs = mixed.reshape(hybrid_block, QUERY_HEADS * HEAD_SIZE).astype(jnp.bfloat16)
    totals = largest + jnp.log(total)
    return (outputs, totals)


def attention_backward(query_rows, key_matrix, value_matrix, segment, log_total, output_gradient):
    input_rows = query_rows.shape[0]
    hybrid_block = min(512, input_rows)
    head_group = QUERY_HEADS // KEY_VALUE_HEADS
    mask = block_mask(segment, hybrid_block)
    grouped_heads = query_rows.reshape(hybrid_block, KEY_VALUE_HEADS, head_group, HEAD_SIZE)
    score_matrix = attention_scores(grouped_heads, key_matrix, mask)
    attn_weights = jnp.exp(score_matrix - log_total)
    weights_low = attn_weights.astype(jnp.bfloat16)
    gradient_rows = output_gradient.reshape(hybrid_block, KEY_VALUE_HEADS, head_group, HEAD_SIZE)
    grad_weights = jnp.einsum(
        "mytl,byl->ytmb", gradient_rows, value_matrix, preferred_element_type=jnp.float32
    )
    value_gradient = jnp.einsum(
        "kgij,ikgd->jkd", weights_low, gradient_rows, preferred_element_type=jnp.float32
    )
    inner = jnp.sum(grad_weights * attn_weights, -1, keepdims=True)
    grad_scores = (attn_weights * (grad_weights - inner) * HEAD_SIZE ** (-0.5)).astype(jnp.bfloat16)
    grad_query_parts = jnp.einsum(
        "kgij,jkd->ikgd", grad_scores, key_matrix, preferred_element_type=jnp.float32
    ).reshape(hybrid_block, QUERY_HEADS, HEAD_SIZE)
    grad_keys = jnp.einsum(
        "kgij,ikgd->jkd", grad_scores, grouped_heads, preferred_element_type=jnp.float32
    )
    return (grad_query_parts, grad_keys, value_gradient)


def decay_weights(cumulative, step, mask, lower, count, first, each):
    cum_rows = cumulative[lower : lower + count, first : first + each]
    cum_all = cumulative[:, first : first + each]
    log_gap = cum_rows.T[:, :, None] - cum_all.T[:, None, :]
    decay = jnp.exp(jnp.where(mask[None] > 0, log_gap, 0.0)) * mask[None]
    return (decay, decay * step[:, first : first + each].T[:, None, :])


def ssd_forward(c_low, b_low, x_low, step, cumulative, segment):
    input_rows = c_low.shape[0]
    hybrid_block = min(512, input_rows)
    heads = x_low.shape[1]
    each = min(8, heads)
    mask = block_mask(segment, hybrid_block)
    intersection = jnp.einsum("is,js->ij", c_low, b_low, preferred_element_type=jnp.float32)
    parts = []
    for first in range(0, heads, each):
        decay, weighted = decay_weights(cumulative, step, mask, 0, hybrid_block, first, each)
        mixer = (intersection[None] * weighted).astype(jnp.bfloat16)
        parts.append(
            jnp.einsum(
                "hij,jhd->ihd",
                mixer,
                x_low[:, first : first + each],
                preferred_element_type=jnp.float32,
            )
        )
    outputs = jnp.concatenate(parts, 1)
    return outputs


def ssd_backward(c_low, b_low, x_low, step, cumulative, segment, grad_y):
    input_rows = c_low.shape[0]
    hybrid_block = min(512, input_rows)
    heads = x_low.shape[1]
    each = min(8, heads)
    grad_x = jnp.zeros(x_low.shape, jnp.float32)
    grad_cum = jnp.zeros((input_rows, heads), jnp.float32)
    grad_step = jnp.zeros((input_rows, heads), jnp.float32)
    mask = block_mask(segment, hybrid_block)
    intersection = jnp.einsum("is,js->ij", c_low, b_low, preferred_element_type=jnp.float32)
    grad_intersection = jnp.zeros((hybrid_block, input_rows), jnp.float32)
    for first in range(0, heads, each):
        decay, weighted = decay_weights(cumulative, step, mask, 0, hybrid_block, first, each)
        mixer = (intersection[None] * weighted).astype(jnp.bfloat16)
        gradient_rows = grad_y[0:hybrid_block, first : first + each]
        grad_mixer = jnp.einsum(
            "ihd,jhd->hij",
            gradient_rows,
            x_low[:, first : first + each],
            preferred_element_type=jnp.float32,
        )
        grad_x = grad_x.at[:, first : first + each].add(
            jnp.einsum("hij,ihd->jhd", mixer, gradient_rows, preferred_element_type=jnp.float32)
        )
        grad_intersection = grad_intersection + jnp.sum(grad_mixer * weighted, 0)
        grad_weighted = grad_mixer * intersection[None]
        grad_step = grad_step.at[:, first : first + each].add(jnp.sum(grad_weighted * decay, 1).T)
        grad_gap = grad_weighted * weighted
        grad_cum = grad_cum.at[0:hybrid_block, first : first + each].add(jnp.sum(grad_gap, 2).T)
        grad_cum = grad_cum.at[:, first : first + each].add(-jnp.sum(grad_gap, 1).T)
    intersection_low = grad_intersection.astype(jnp.bfloat16)
    grad_c_parts = jnp.dot(intersection_low, b_low, preferred_element_type=jnp.float32)
    grad_b = jnp.einsum("ij,is->js", intersection_low, c_low, preferred_element_type=jnp.float32)
    return (grad_x, grad_cum, grad_step, grad_b, grad_c_parts)


def layer_forward(weights, own_tokens, position, segment):
    (
        gain_attn,
        w_input,
        w_step,
        step_bias,
        decay_log,
        skip_scale,
        conv_weight,
        conv_bias,
        gain_ssm,
        w_output,
        gain_ffn,
        w_gate_up,
        w_down,
    ) = weights
    input_rows = own_tokens.shape[0]
    tokens_full = own_tokens.astype(jnp.float32)
    normed = rms_norm(tokens_full, gain_attn.astype(jnp.float32)).astype(jnp.bfloat16)
    projected_rows = jnp.dot(normed, w_input, preferred_element_type=jnp.float32)
    step_raw = jnp.dot(normed, w_step, preferred_element_type=jnp.float32)
    rotary_angles = rope_angles(position, HEAD_SIZE)
    query_rows = apply_rotary(
        projected_rows[:, : QUERY_HEADS * HEAD_SIZE].reshape(input_rows, QUERY_HEADS, HEAD_SIZE),
        rotary_angles,
    ).astype(jnp.bfloat16)
    key_matrix = apply_rotary(
        projected_rows[
            :, QUERY_HEADS * HEAD_SIZE : QUERY_KEY_VALUE - KEY_VALUE_HEADS * HEAD_SIZE
        ].reshape(input_rows, KEY_VALUE_HEADS, HEAD_SIZE),
        rotary_angles,
    ).astype(jnp.bfloat16)
    value_matrix = (
        projected_rows[:, QUERY_KEY_VALUE - KEY_VALUE_HEADS * HEAD_SIZE : QUERY_KEY_VALUE]
        .reshape(input_rows, KEY_VALUE_HEADS, HEAD_SIZE)
        .astype(jnp.bfloat16)
    )
    gate_z = projected_rows[:, QUERY_KEY_VALUE : QUERY_KEY_VALUE + INNER]
    conv_in = projected_rows[:, QUERY_KEY_VALUE + INNER :]
    conv_out = conv_silu(
        conv_in, conv_weight.astype(jnp.float32), conv_bias.astype(jnp.float32), segment
    )
    inner_x = conv_out[:, :INNER].reshape(input_rows, SSM_HEADS, SSM_HD)
    b_low = conv_out[:, INNER : INNER + STATE].astype(jnp.bfloat16)
    c_low = conv_out[:, INNER + STATE :].astype(jnp.bfloat16)
    step_pre = step_raw + step_bias.astype(jnp.float32)
    step = jax.nn.softplus(step_pre)
    rate = -jnp.exp(decay_log.astype(jnp.float32))
    cumulative = jnp.cumsum(step * rate, axis=0)
    x_low = inner_x.astype(jnp.bfloat16)
    ssd_out = ssd_forward(c_low, b_low, x_low, step, cumulative, segment)
    ssm_y = (ssd_out + skip_scale.astype(jnp.float32)[None, :, None] * inner_x).reshape(
        input_rows, INNER
    )
    ssm_out = gated_norm(ssm_y, gate_z, gain_ssm.astype(jnp.float32)).astype(jnp.bfloat16)
    attn_out, log_total = attention_forward(query_rows, key_matrix, value_matrix, segment)
    joined = jnp.concatenate([attn_out, ssm_out], 1)
    middle = tokens_full + jnp.dot(joined, w_output, preferred_element_type=jnp.float32)
    normed_ffn = rms_norm(middle, gain_ffn.astype(jnp.float32)).astype(jnp.bfloat16)
    gate_up = jnp.dot(normed_ffn, w_gate_up, preferred_element_type=jnp.float32)
    hidden = swiglu(gate_up).astype(jnp.bfloat16)
    block_out = middle + jnp.dot(hidden, w_down, preferred_element_type=jnp.float32)
    saved = {
        "tokens": tokens_full,
        "normed": normed,
        "projected": projected_rows,
        "angles": rotary_angles,
        "queries": query_rows,
        "key_rows": key_matrix,
        "value_rows": value_matrix,
        "gate_z": gate_z,
        "conv_in": conv_in,
        "inner_x": inner_x,
        "b_low": b_low,
        "c_low": c_low,
        "x_low": x_low,
        "step_pre": step_pre,
        "step": step,
        "rate": rate,
        "cumulative": cumulative,
        "ssm_y": ssm_y,
        "log_total": log_total,
        "joined": joined,
        "middle": middle,
        "normed_ffn": normed_ffn,
        "gate_up": gate_up,
        "hidden": hidden,
    }
    return (block_out.astype(jnp.bfloat16), saved)


def layer_backward(weights, saved, segment, cot_rows):
    (
        gain_attn,
        w_input,
        w_step,
        step_bias,
        decay_log,
        skip_scale,
        conv_weight,
        conv_bias,
        gain_ssm,
        w_output,
        gain_ffn,
        w_gate_up,
        w_down,
    ) = weights
    input_rows = cot_rows.shape[0]
    grad_w_down = jnp.einsum(
        "ti,td->id", saved["hidden"], cot_rows, preferred_element_type=jnp.float32
    )
    grad_hidden = jnp.einsum("td,id->ti", cot_rows, w_down, preferred_element_type=jnp.float32)
    swiglu_back = jax.vjp(swiglu, saved["gate_up"])[1]
    grad_gate_up = swiglu_back(grad_hidden)[0].astype(jnp.bfloat16)
    grad_w_gate_up = jnp.einsum(
        "ti,tj->ij", saved["normed_ffn"], grad_gate_up, preferred_element_type=jnp.float32
    )
    grad_normed_ffn = jnp.einsum(
        "tj,ij->ti", grad_gate_up, w_gate_up, preferred_element_type=jnp.float32
    )
    ffn_back = jax.vjp(rms_norm, saved["middle"], gain_ffn.astype(jnp.float32))[1]
    grad_middle_norm, grad_gain_ffn = ffn_back(grad_normed_ffn)
    grad_middle = cot_rows.astype(jnp.float32) + grad_middle_norm
    middle_low = grad_middle.astype(jnp.bfloat16)
    grad_w_output = jnp.einsum(
        "ti,td->id", saved["joined"], middle_low, preferred_element_type=jnp.float32
    )
    grad_joined = jnp.einsum("td,id->ti", middle_low, w_output, preferred_element_type=jnp.float32)
    grad_attn = grad_joined[:, : QUERY_HEADS * HEAD_SIZE].astype(jnp.bfloat16)
    grad_ssm_out = grad_joined[:, QUERY_HEADS * HEAD_SIZE :]
    gated_back = jax.vjp(gated_norm, saved["ssm_y"], saved["gate_z"], gain_ssm.astype(jnp.float32))[
        1
    ]
    grad_ssm_y, grad_gate_z, grad_gain_ssm = gated_back(grad_ssm_out)
    grad_ssm_y = grad_ssm_y.reshape(input_rows, SSM_HEADS, SSM_HD)
    grad_skip_scale = jnp.sum(grad_ssm_y * saved["inner_x"], (0, 2))
    grad_x, grad_cum, grad_step, grad_b, grad_c = ssd_backward(
        saved["c_low"],
        saved["b_low"],
        saved["x_low"],
        saved["step"],
        saved["cumulative"],
        segment,
        grad_ssm_y.astype(jnp.bfloat16),
    )
    grad_x = grad_x + skip_scale.astype(jnp.float32)[None, :, None] * grad_ssm_y
    grad_inc = lax.cumsum(grad_cum, axis=0, reverse=True)
    grad_step = grad_step + grad_inc * saved["rate"]
    grad_decay_log = jnp.sum(grad_inc * saved["step"], 0) * saved["rate"]
    grad_step_pre = grad_step * jax.nn.sigmoid(saved["step_pre"])
    grad_step_bias = jnp.sum(grad_step_pre, 0)
    step_low = grad_step_pre.astype(jnp.bfloat16)
    grad_w_step = jnp.einsum(
        "ti,th->ih", saved["normed"], step_low, preferred_element_type=jnp.float32
    )
    grad_conv_out = jnp.concatenate([grad_x.reshape(input_rows, INNER), grad_b, grad_c], 1)
    conv_back = jax.vjp(
        partial(conv_silu, segment=segment),
        saved["conv_in"],
        conv_weight.astype(jnp.float32),
        conv_bias.astype(jnp.float32),
    )[1]
    grad_conv_in, grad_conv_weight, grad_conv_bias = conv_back(grad_conv_out)
    grad_queries, grad_keys, value_gradient = attention_backward(
        saved["queries"],
        saved["key_rows"],
        saved["value_rows"],
        segment,
        saved["log_total"],
        grad_attn,
    )
    projected_rows = saved["projected"]
    query_back = jax.vjp(
        partial(apply_rotary, rotary_angles=saved["angles"]),
        projected_rows[:, : QUERY_HEADS * HEAD_SIZE].reshape(input_rows, QUERY_HEADS, HEAD_SIZE),
    )[1]
    key_back = jax.vjp(
        partial(apply_rotary, rotary_angles=saved["angles"]),
        projected_rows[
            :, QUERY_HEADS * HEAD_SIZE : QUERY_KEY_VALUE - KEY_VALUE_HEADS * HEAD_SIZE
        ].reshape(input_rows, KEY_VALUE_HEADS, HEAD_SIZE),
    )[1]
    grad_query_raw = query_back(grad_queries)[0]
    unrotated_key_gradient = key_back(grad_keys)[0]
    grad_projected = jnp.concatenate(
        [
            grad_query_raw.reshape(input_rows, QUERY_HEADS * HEAD_SIZE),
            unrotated_key_gradient.reshape(input_rows, KEY_VALUE_HEADS * HEAD_SIZE),
            value_gradient.reshape(input_rows, KEY_VALUE_HEADS * HEAD_SIZE),
            grad_gate_z,
            grad_conv_in,
        ],
        1,
    ).astype(jnp.bfloat16)
    grad_w_input = jnp.einsum(
        "ti,tj->ij", saved["normed"], grad_projected, preferred_element_type=jnp.float32
    )
    grad_normed = jnp.einsum(
        "tj,ij->ti", grad_projected, w_input, preferred_element_type=jnp.float32
    )
    grad_normed = grad_normed + jnp.einsum(
        "th,ih->ti", step_low, w_step, preferred_element_type=jnp.float32
    )
    attn_norm_back = jax.vjp(rms_norm, saved["tokens"], gain_attn.astype(jnp.float32))[1]
    grad_tokens_norm, grad_gain_attn = attn_norm_back(grad_normed)
    grad_tokens = grad_middle + grad_tokens_norm
    grads = (
        grad_gain_attn,
        grad_w_input,
        grad_w_step,
        grad_step_bias,
        grad_decay_log,
        grad_skip_scale,
        grad_conv_weight,
        grad_conv_bias,
        grad_gain_ssm,
        grad_w_output,
        grad_gain_ffn,
        grad_w_gate_up,
        grad_w_down,
    )
    return (grad_tokens.astype(jnp.bfloat16), grads)


def bit_of(axis, bit):
    return (lax.axis_index(axis) >> bit) & 1


def bit_count(axis):
    return lax.axis_size(axis).bit_length() - 1


def swap(values, axis, bit):
    count = lax.axis_size(axis)
    return lax.ppermute(values, axis, [(i, i ^ (1 << bit)) for i in range(count)])


def join(values, other, axis, bit, dim):
    flag = bit_of(axis, bit)
    return jnp.stack([jnp.where(flag == 0, values, other), jnp.where(flag == 0, other, values)], dim)


def gather_rows(piece):
    rows, width = piece.shape
    for bit in range(bit_count("shard")):
        piece = join(piece, swap(piece, "shard", bit), "shard", bit, 0)
    return piece.reshape(-1, width)


def gather_weight(piece):
    rows, width = piece.shape
    near = bit_of("rep", 0)
    held = piece
    for bit in reversed(range(1, bit_count("shard"))):
        lead = held.shape[:-2]
        flat = held.reshape(-1, width)
        halves = flat.reshape(2, -1, width)
        mine = lax.dynamic_index_in_dim(halves, near, 0, keepdims=False)
        direct = swap(mine, "shard", bit)
        passed = swap(direct, "rep", 0)
        other = join(direct, passed, "rep", 0, 0).reshape(lead + (rows, width))
        held = join(held, other, "shard", bit, len(lead))
    lead = held.shape[:-2]
    held = join(held, swap(held, "shard", 0), "shard", 0, len(lead))
    parts = len(lead)
    order = tuple(range(parts)) [::-1]
    return held.reshape(-1, width)


def gather_small(pieces, dims):
    flat = jnp.concatenate([piece.reshape(-1) for piece in pieces])
    every = lax.all_gather(flat, "shard", axis=0, tiled=False)
    parts = every.shape[0]
    outputs = []
    offset = 0
    for piece, dim in zip(pieces, dims):
        length = math.prod(piece.shape)
        block = every[:, offset : offset + length].reshape((parts,) + piece.shape)
        offset += length
        if dim == 0:
            outputs.append(block.reshape((-1,) + piece.shape[1:]))
        else:
            outputs.append(jnp.swapaxes(block, 0, 1).reshape(piece.shape[0], -1))
    return outputs


def reduce_grad(grad, order):
    rows_all, width = grad.shape
    shard_bits, rep_bits = bit_count("shard"), bit_count("rep")
    rows = rows_all >> (shard_bits + rep_bits)
    left = [("shard", b) for b in reversed(range(shard_bits))]
    left += [("rep", b) for b in reversed(range(rep_bits))]
    total = grad.reshape((2,) * (shard_bits + rep_bits) + (rows, width))
    for stage in order:
        dim = left.index(stage)
        left.pop(dim)
        flag = bit_of(*stage)
        away = lax.dynamic_index_in_dim(total, 1 - flag, dim, keepdims=False)
        keep = lax.dynamic_index_in_dim(total, flag, dim, keepdims=False)
        came = swap(away, *stage)
        total = (keep.astype(jnp.float32) + came.astype(jnp.float32)).astype(jnp.bfloat16)
    have = []
    for stage in reversed(order):
        if stage[0] == "shard":
            continue
        have.append(stage)
        have.sort(key=lambda s: -s[1])
        total = join(total, swap(total, *stage), *stage, have.index(stage))
    return total.reshape(rows_all >> shard_bits, width).astype(jnp.float32)


def reduce_small(grads):
    flat = jnp.concatenate([grad.reshape(-1) for grad in grads])
    extra = -flat.shape[0] % 1024
    total = jnp.pad(flat, (0, extra)).reshape(-1, 128)
    for axis in ("shard", "rep"):
        for bit in range(bit_count(axis)):
            total = total + swap(total, axis, bit)
    total = total.reshape(-1)
    outputs = []
    offset = 0
    for grad in grads:
        length = math.prod(grad.shape)
        outputs.append(total[offset : offset + length].reshape(grad.shape))
        offset += length
    return outputs


def own_block(values, dim):
    size = values.shape[dim] // lax.axis_size("shard")
    return lax.dynamic_slice_in_dim(values, lax.axis_index("shard") * size, size, dim)


def take_rows(values, wanted):
    places = jnp.arange(values.shape[0], dtype=jnp.int32)
    choice = (wanted[:, None] == places[None, :]).astype(jnp.bfloat16)
    return jnp.dot(choice, values, preferred_element_type=jnp.float32).astype(jnp.bfloat16)


def on_device(
    tokens,
    seq_lengths,
    owner_order,
    gain_attn,
    w_input,
    w_step,
    step_bias,
    decay_log,
    skip_scale,
    conv_weight,
    conv_bias,
    gain_ssm,
    w_output,
    gain_ffn,
    w_gate_up,
    w_down,
    cotangent,
):
    input_rows = tokens.shape[0]
    device = lax.axis_index("shard")
    source, position, segment, target = group_tables(
        seq_lengths[0], owner_order[0], input_rows, device
    )
    own_tokens = take_rows(gather_rows(tokens), source)
    own_cot = take_rows(gather_rows(cotangent), source)
    small = gather_small(
        (gain_attn, w_step, step_bias, decay_log, skip_scale, conv_weight, conv_bias, gain_ssm, gain_ffn),
        (0, 0, 0, 0, 0, 1, 0, 0, 0),
    )
    weights_full = (
        small[0],
        gather_weight(w_input),
        *small[1:8],
        gather_weight(w_output),
        small[8],
        gather_weight(w_gate_up),
        gather_weight(w_down),
    )
    out_low, saved = layer_forward(weights_full, own_tokens, position, segment)
    grad_low, grads = layer_backward(weights_full, saved, segment, own_cot)
    core = [("shard", 0)]
    far = [("shard", b) for b in range(1, bit_count("shard"))]
    near = [("rep", 0)]
    rest = [("rep", b) for b in range(1, bit_count("rep"))]
    first = core + far + near + rest
    second = core + near + far + rest
    places = (0, 2, 3, 4, 5, 6, 7, 8, 10)
    summed = reduce_small([grads[i] for i in places])
    outs = [None] * 13
    for i, grad in zip(places, summed):
        outs[i] = own_block(grad, 1 if i == 6 else 0)
    outs[12] = reduce_grad(grads[12].astype(jnp.bfloat16), first)
    outs[11] = reduce_grad(grads[11].astype(jnp.bfloat16), second)
    outs[9] = reduce_grad(grads[9].astype(jnp.bfloat16), first)
    outs[1] = reduce_grad(grads[1].astype(jnp.bfloat16), second)
    block_out = take_rows(gather_rows(out_low), target)
    grad_tokens = take_rows(gather_rows(grad_low), target)
    return (block_out, grad_tokens, *outs)


def solution(mesh):
    placed = (
        P(("rep", "shard"), None),
        P("rep", None),
        P("rep", None),
        P("shard"),
        P("shard", None),
        P("shard", None),
        P("shard"),
        P("shard"),
        P("shard"),
        P(None, "shard"),
        P("shard"),
        P("shard"),
        P("shard", None),
        P("shard"),
        P("shard", None),
        P("shard", None),
        P(("rep", "shard"), None),
    )
    return jax.shard_map(
        on_device,
        mesh=mesh,
        in_specs=placed,
        out_specs=(
            P(("rep", "shard"), None),
            P(("rep", "shard"), None),
            P("shard"),
            P("shard", None),
            P("shard", None),
            P("shard"),
            P("shard"),
            P("shard"),
            P(None, "shard"),
            P("shard"),
            P("shard"),
            P("shard", None),
            P("shard"),
            P("shard", None),
            P("shard", None),
        ),
        check_vma=False,
    )
```

```python
import math

import jax
import jax.numpy as jnp
from jax import lax
from jax.experimental import pallas as pl
from jax.experimental.pallas import tpu as pltpu
from jax.sharding import PartitionSpec as P

QUERY_HEADS = 8
KEY_VALUE_HEADS = 2
HEAD_SIZE = 64
SSM_HEADS = 24
SSM_HD = 64
STATE = 128
INNER = 1536
QUERY_KEY_VALUE = 768
TAPS = 4

EPS = 1e-05
ROPE_BASE = 100000000000.0
SIDE = 128
QUAD = 4
LOW = -1e30


def causal_bias(limit, rows, row0, cols):
    i = lax.broadcasted_iota(jnp.int32, (rows, cols), 0) + row0
    j = lax.broadcasted_iota(jnp.int32, (rows, cols), 1)
    seen = (j <= i) & ((j >= limit) | (i < limit))
    return jnp.where(seen, 0.0, LOW)


def contract_last(left, right):
    return lax.dot_general(left, right, (((1,), (1,)), ((), ())), preferred_element_type=jnp.float32)


def contract_first(left, right):
    return lax.dot_general(left, right, (((0,), (0,)), ((), ())), preferred_element_type=jnp.float32)


def halves(pair):
    lane = lax.broadcasted_iota(jnp.int32, pair.shape, 1)
    zero = jnp.zeros_like(pair)
    return (jnp.where(lane < HEAD_SIZE, pair, zero), jnp.where(lane >= HEAD_SIZE, pair, zero))


def ssd_forward_kernel(limit_ref, c_ref, b_ref, x_ref, cum_col_ref, cum_row_ref, out_ref, inter, bias):
    count = c_ref.shape[0]

    @pl.when(pl.program_id(0) == 0)
    def _():
        inter[...] = contract_last(c_ref[...], b_ref[...])
        bias[...] = causal_bias(limit_ref[0], count, 0, count)

    for pair in range(QUAD // 2):
        lanes = slice(pair * SIDE, (pair + 1) * SIDE)
        sides = halves(x_ref[:, lanes])
        for top in range(0, count, SIDE):
            rows = slice(top, top + SIDE)
            seen = top + SIDE
            total = None
            for half in range(2):
                h = pair * 2 + half
                gap = cum_col_ref[0, rows, h : h + 1] - cum_row_ref[0, h : h + 1, :seen]
                mixer = (inter[rows, :seen] * jnp.exp(gap + bias[rows, :seen])).astype(jnp.bfloat16)
                part = jnp.dot(mixer, sides[half][:seen], preferred_element_type=jnp.float32)
                total = part if total is None else total + part
            out_ref[rows, lanes] = total


def ssd_forward(limit, c_low, b_low, x_step, cum):
    count, heads = cum.shape
    steps = heads // QUAD
    whole = lambda width: pl.BlockSpec((count, width), lambda i: (0, 0))
    return pl.pallas_call(
        ssd_forward_kernel,
        grid=(steps,),
        out_shape=jax.ShapeDtypeStruct(x_step.shape, jnp.float32),
        in_specs=[
            pl.BlockSpec(memory_space=pltpu.SMEM),
            whole(c_low.shape[1]),
            whole(b_low.shape[1]),
            pl.BlockSpec((count, QUAD * HEAD_SIZE), lambda i: (0, i)),
            pl.BlockSpec((1, count, QUAD), lambda i: (i, 0, 0)),
            pl.BlockSpec((1, QUAD, count), lambda i: (i, 0, 0)),
        ],
        out_specs=pl.BlockSpec((count, QUAD * HEAD_SIZE), lambda i: (0, i)),
        scratch_shapes=[pltpu.VMEM((count, count), jnp.float32)] * 2,
        name="ssd_forward",
    )(
        limit,
        c_low,
        b_low,
        x_step,
        cum.reshape(count, steps, QUAD).transpose(1, 0, 2),
        cum.T.reshape(steps, QUAD, count),
    )


def ssd_backward_kernel(
    limit_ref, c_ref, b_ref, x_ref, dy_ref, cum_col_ref, cum_row_ref, z_ref, gc_ref, gb_ref, inter, bias, total
):
    count = c_ref.shape[0]

    @pl.when(pl.program_id(0) == 0)
    def _():
        inter[...] = contract_last(c_ref[...], b_ref[...])
        bias[...] = causal_bias(limit_ref[0], count, 0, count)
        total[...] = jnp.zeros_like(total)

    for pair in range(QUAD // 2):
        lanes = slice(pair * SIDE, (pair + 1) * SIDE)
        x_pair = x_ref[:, lanes]
        sides = halves(dy_ref[:, lanes])
        for top in reversed(range(0, count, SIDE)):
            rows = slice(top, top + SIDE)
            seen = top + SIDE
            grad = None
            back = None
            for half in range(2):
                h = pair * 2 + half
                gap = cum_col_ref[0, rows, h : h + 1] - cum_row_ref[0, h : h + 1, :seen]
                decay = jnp.exp(gap + bias[rows, :seen])
                mixer = (inter[rows, :seen] * decay).astype(jnp.bfloat16)
                grad_mixer = contract_last(sides[half][rows], x_pair[:seen])
                part = grad_mixer * decay
                grad = part if grad is None else grad + part
                part = contract_first(mixer, sides[half][rows])
                back = part if back is None else back + part
            total[rows, :seen] += grad
            if seen == count:
                z_ref[:, lanes] = back
            else:
                z_ref[:seen, lanes] += back

    @pl.when(pl.program_id(0) == pl.num_programs(0) - 1)
    def _():
        low = total[...].astype(jnp.bfloat16)
        gc_ref[...] = jnp.dot(low, b_ref[...], preferred_element_type=jnp.float32)
        gb_ref[...] = contract_first(low, c_ref[...])


def ssd_backward(limit, c_low, b_low, x_step, grad_y, cum):
    count, heads = cum.shape
    steps = heads // QUAD
    state = c_low.shape[1]
    whole = pl.BlockSpec((count, state), lambda i: (0, 0))
    quad = pl.BlockSpec((count, QUAD * HEAD_SIZE), lambda i: (0, i))
    return pl.pallas_call(
        ssd_backward_kernel,
        grid=(steps,),
        out_shape=(
            jax.ShapeDtypeStruct(x_step.shape, jnp.float32),
            jax.ShapeDtypeStruct((count, state), jnp.float32),
            jax.ShapeDtypeStruct((count, state), jnp.float32),
        ),
        in_specs=[
            pl.BlockSpec(memory_space=pltpu.SMEM),
            whole,
            whole,
            quad,
            quad,
            pl.BlockSpec((1, count, QUAD), lambda i: (i, 0, 0)),
            pl.BlockSpec((1, QUAD, count), lambda i: (i, 0, 0)),
        ],
        out_specs=(quad, whole, whole),
        scratch_shapes=[pltpu.VMEM((count, count), jnp.float32)] * 3,
        name="ssd_backward",
    )(
        limit,
        c_low,
        b_low,
        x_step,
        grad_y,
        cum.reshape(count, steps, QUAD).transpose(1, 0, 2),
        cum.T.reshape(steps, QUAD, count),
    )


def turn(values, cosine, sine):
    lane = lax.broadcasted_iota(jnp.int32, values.shape, 1) % HEAD_SIZE
    width = values.shape[1]
    ahead = pltpu.roll(values, width - HEAD_SIZE // 2, 1)
    behind = pltpu.roll(values, HEAD_SIZE // 2, 1)
    other = jnp.where(lane < HEAD_SIZE // 2, ahead, behind)
    return values * cosine + other * sine


def both_sides(pair, step):
    lane = lax.broadcasted_iota(jnp.int32, pair.shape, 1)
    mine = jnp.where((lane >= HEAD_SIZE) == (step > 0), pair, jnp.zeros_like(pair))
    return (mine + pltpu.roll(mine, HEAD_SIZE, 1)).astype(jnp.bfloat16)


def attention_forward_kernel(limit_ref, q_ref, k_ref, v_ref, cos_ref, sin_ref, out_ref, log_ref, bias):
    count = k_ref.shape[0]
    step = pl.program_id(0)

    @pl.when(step == 0)
    def _():
        bias[...] = causal_bias(limit_ref[0], count, 0, count)

    cosine, sine = cos_ref[...], sin_ref[...]
    key = both_sides(turn(k_ref[...], cosine, sine), step)
    value_sides = halves(both_sides(v_ref[...], step))
    for pair in range(2):
        lanes = slice(pair * SIDE, (pair + 1) * SIDE)
        sides = halves(turn(q_ref[:, lanes], cosine, sine).astype(jnp.bfloat16))
        for top in range(0, count, SIDE):
            rows = slice(top, top + SIDE)
            seen = top + SIDE
            total = None
            for half in range(2):
                score = contract_last(sides[half][rows], key[:seen]) * HEAD_SIZE ** (-0.5)
                score = score + bias[rows, :seen]
                largest = jnp.max(score, -1, keepdims=True)
                raised = jnp.exp(score - largest)
                mass = jnp.sum(raised, -1, keepdims=True)
                weights = (raised * (1.0 / mass)).astype(jnp.bfloat16)
                part = jnp.dot(weights, value_sides[half][:seen], preferred_element_type=jnp.float32)
                total = part if total is None else total + part
                h = pair * 2 + half
                log_ref[0, rows, h : h + 1] = largest + jnp.log(mass)
            out_ref[rows, lanes] = total.astype(jnp.bfloat16)


def attention_specs(count):
    wide = pl.BlockSpec((count, 2 * SIDE), lambda i: (0, i))
    whole = pl.BlockSpec((count, SIDE), lambda i: (0, 0))
    keys = pl.BlockSpec((count, SIDE), lambda i: (0, QUERY_HEADS * HEAD_SIZE // SIDE))
    values = pl.BlockSpec((count, SIDE), lambda i: (0, QUERY_HEADS * HEAD_SIZE // SIDE + 1))
    logs = pl.BlockSpec((1, count, QUAD), lambda i: (i, 0, 0))
    return wide, whole, keys, values, logs


def attention_forward(limit, projected, cosine, sine):
    count = projected.shape[0]
    wide, whole, keys, values, logs = attention_specs(count)
    return pl.pallas_call(
        attention_forward_kernel,
        grid=(KEY_VALUE_HEADS,),
        out_shape=(
            jax.ShapeDtypeStruct((count, QUERY_HEADS * HEAD_SIZE), jnp.bfloat16),
            jax.ShapeDtypeStruct((KEY_VALUE_HEADS, count, QUAD), jnp.float32),
        ),
        in_specs=[pl.BlockSpec(memory_space=pltpu.SMEM), wide, keys, values, whole, whole],
        out_specs=(wide, logs),
        scratch_shapes=[pltpu.VMEM((count, count), jnp.float32)],
        name="attention_forward",
    )(limit, projected, projected, projected, cosine, sine)


def attention_backward_kernel(
    limit_ref, q_ref, k_ref, v_ref, cos_ref, sin_ref, go_ref, log_ref, gq_ref, gkv_ref, bias, gk, gv
):
    count = k_ref.shape[0]
    step = pl.program_id(0)

    @pl.when(step == 0)
    def _():
        bias[...] = causal_bias(limit_ref[0], count, 0, count)

    cosine, sine = cos_ref[...], sin_ref[...]
    key = both_sides(turn(k_ref[...], cosine, sine), step)
    value = both_sides(v_ref[...], step)
    key_sides = halves(key)
    gk[...] = jnp.zeros_like(gk)
    gv[...] = jnp.zeros_like(gv)
    for pair in range(2):
        lanes = slice(pair * SIDE, (pair + 1) * SIDE)
        q_sides = halves(turn(q_ref[:, lanes], cosine, sine).astype(jnp.bfloat16))
        go_sides = halves(go_ref[:, lanes])
        for top in range(0, count, SIDE):
            rows = slice(top, top + SIDE)
            seen = top + SIDE
            total = None
            for half in range(2):
                h = pair * 2 + half
                score = contract_last(q_sides[half][rows], key[:seen]) * HEAD_SIZE ** (-0.5)
                weights = jnp.exp(score + bias[rows, :seen] - log_ref[0, rows, h : h + 1])
                grad = contract_last(go_sides[half][rows], value[:seen])
                inner = jnp.sum(grad * weights, -1, keepdims=True)
                low = (weights * (grad - inner) * HEAD_SIZE ** (-0.5)).astype(jnp.bfloat16)
                part = jnp.dot(low, key_sides[half][:seen], preferred_element_type=jnp.float32)
                total = part if total is None else total + part
                gk[:seen, :] += contract_first(low, q_sides[half][rows])
                gv[:seen, :] += contract_first(weights.astype(jnp.bfloat16), go_sides[half][rows])
            gq_ref[rows, lanes] = turn(total, cosine[rows], -sine[rows]).astype(jnp.bfloat16)
    lane = lax.broadcasted_iota(jnp.int32, (count, SIDE), 1)
    mine = (lane >= HEAD_SIZE) == (step > 0)
    for place, part in enumerate((gk, gv)):
        summed = part[...] + pltpu.roll(part[...], HEAD_SIZE, 1)
        if place == 0:
            summed = turn(summed, cosine, -sine)
        lanes = slice(place * SIDE, (place + 1) * SIDE)
        @pl.when(step == 0)
        def _():
            gkv_ref[:, lanes] = summed.astype(jnp.bfloat16)

        @pl.when(step > 0)
        def _():
            gkv_ref[:, lanes] = jnp.where(mine, summed, gkv_ref[:, lanes].astype(jnp.float32)).astype(jnp.bfloat16)


def attention_backward(limit, projected, cosine, sine, grad_out, logs_in):
    count = projected.shape[0]
    wide, whole, keys, values, logs = attention_specs(count)
    return pl.pallas_call(
        attention_backward_kernel,
        grid=(KEY_VALUE_HEADS,),
        out_shape=(
            jax.ShapeDtypeStruct((count, QUERY_HEADS * HEAD_SIZE), jnp.bfloat16),
            jax.ShapeDtypeStruct((count, 2 * SIDE), jnp.bfloat16),
        ),
        in_specs=[pl.BlockSpec(memory_space=pltpu.SMEM), wide, keys, values, whole, whole, wide, logs],
        out_specs=(wide, pl.BlockSpec((count, 2 * SIDE), lambda i: (0, 0))),
        scratch_shapes=[
            pltpu.VMEM((count, count), jnp.float32),
            pltpu.VMEM((count, SIDE), jnp.float32),
            pltpu.VMEM((count, SIDE), jnp.float32),
        ],
        name="attention_backward",
    )(limit, projected, projected, projected, cosine, sine, grad_out, logs_in)


def pick_kernel(shift_ref, wanted_ref, *refs):
    out_ref = refs[-1]
    pieces = refs[:-1]
    count = pieces[0].shape[0]
    place = lax.broadcasted_iota(jnp.int32, (out_ref.shape[0], count), 1)
    total = None
    for n, piece in enumerate(pieces):
        choice = (wanted_ref[...] - shift_ref[n] == place).astype(jnp.bfloat16)
        part = jnp.dot(choice, piece[...], preferred_element_type=jnp.float32)
        total = part if total is None else total + part
    out_ref[...] = total.astype(out_ref.dtype)


def pick_rows(pieces, shifts, wanted):
    vmem = pl.BlockSpec(memory_space=pltpu.VMEM)
    return pl.pallas_call(
        pick_kernel,
        out_shape=jax.ShapeDtypeStruct((wanted.shape[0], pieces[0].shape[1]), pieces[0].dtype),
        in_specs=[pl.BlockSpec(memory_space=pltpu.SMEM), vmem] + [vmem] * len(pieces),
        out_specs=vmem,
        name="pick_rows",
    )(shifts, wanted[:, None], *pieces)


def lay_rows_kernel(place_ref, *refs):
    sems = refs[-1]
    out_ref = refs[-2]
    pieces = refs[:-2]
    copies = []
    for n, piece in enumerate(pieces):
        rows = piece.shape[0]
        start = pl.multiple_of(place_ref[n] * 16, 16)
        copies.append(pltpu.make_async_copy(piece, out_ref.at[pl.ds(start, rows)], sems.at[n]))
    for copy in copies:
        copy.start()
    for copy in copies:
        copy.wait()


def lay_rows(pieces, places):
    rows = sum(piece.shape[0] for piece in pieces)
    hbm = pl.BlockSpec(memory_space=pl.ANY)
    return pl.pallas_call(
        lay_rows_kernel,
        out_shape=jax.ShapeDtypeStruct((rows, pieces[0].shape[1]), pieces[0].dtype),
        in_specs=[pl.BlockSpec(memory_space=pltpu.SMEM)] + [hbm] * len(pieces),
        out_specs=pl.BlockSpec(memory_space=pltpu.VMEM),
        scratch_shapes=[pltpu.SemaphoreType.DMA((len(pieces),))],
        name="lay_rows",
    )(places // 16, *pieces)


def sum_pieces_kernel(place_ref, *refs):
    out_ref = refs[-1]
    for n, piece in enumerate(refs[:-1]):
        rows = piece.shape[0]
        start = pl.multiple_of(place_ref[n] * 8, 8)
        out_ref[pl.ds(start, rows), :] = piece[...].astype(jnp.float32)


def widen_rows(pieces, places):
    rows = sum(piece.shape[0] for piece in pieces)
    vmem = pl.BlockSpec(memory_space=pltpu.VMEM)
    return pl.pallas_call(
        sum_pieces_kernel,
        out_shape=jax.ShapeDtypeStruct((rows, pieces[0].shape[1]), jnp.float32),
        in_specs=[pl.BlockSpec(memory_space=pltpu.SMEM)] + [vmem] * len(pieces),
        out_specs=vmem,
        name="widen_rows",
    )(places // 8, *pieces)


def swap(values, axis, mask):
    count = lax.axis_size(axis)
    return lax.ppermute(values, axis, [(i, i ^ mask) for i in range(count)])


def take(values, index, dim):
    return lax.dynamic_index_in_dim(values, index, dim, keepdims=False)


def add(first, *others):
    total = first.astype(jnp.float32)
    for other in others:
        total = total + other.astype(jnp.float32)
    return total.astype(jnp.bfloat16)


class Flow:
    def __init__(self):
        self.live = []

    def add(self, stream):
        slot = {"stream": stream, "sent": None, "result": None, "done": False}
        self.live.append(slot)
        self._advance(slot, None)
        return slot

    def _advance(self, slot, value):
        try:
            slot["sent"] = slot["stream"].send(value)
        except StopIteration as stop:
            slot["result"] = stop.value
            slot["sent"] = None
            slot["done"] = True
            self.live.remove(slot)

    def step(self, values=None, slots=None):
        slots = [slot for slot in (self.live if slots is None else slots) if not slot["done"]]
        values, sent = lax.optimization_barrier((values, [slot["sent"] for slot in slots]))
        for slot, came in zip(slots, sent):
            self._advance(slot, came)
        return values

    def until(self, slots, values=None):
        while any(not slot["done"] for slot in slots):
            values = self.step(values)
        return values


def rows_stream(piece):
    shard = lax.axis_index("shard")
    held = [(0, piece)]
    mask = lax.axis_size("shard") // 2
    first = True
    near = None
    while mask > 1:
        send = [swap(p, "shard", mask) for _, p in held]
        if first:
            send.append(swap(piece, "shard", 1))
        came = yield send
        if first:
            near = came[-1]
            first = False
        held = held + [(k ^ mask, p) for (k, _), p in zip(held, came)]
        mask //= 2
    came = yield [swap(p, "shard", 1) for k, p in held[1:]]
    held = held + [(1, near)] + [(k ^ 1, p) for (k, _), p in zip(held[1:], came)]
    keys = [k for k, _ in held]
    return [p for _, p in held], jnp.stack([shard ^ k for k in keys]).astype(jnp.int32)


def weight_stream(piece):
    rows, width = piece.shape
    shard, near = lax.axis_index("shard"), lax.axis_index("rep") & 1
    part = lax.dynamic_slice_in_dim(piece, near * (rows // 2), rows // 2, 0)
    held = [(0, part)]
    both = []
    mask = lax.axis_size("shard") // 2
    beside = None
    while mask > 1:
        send = [swap(p, "shard", mask) for _, p in held]
        if beside is None:
            send.append(swap(piece, "shard", 1))
        came = yield send
        if beside is None:
            beside = came[-1]
        fresh = [(k ^ mask, p) for (k, _), p in zip(held, came)]
        passed = yield [swap(p, "rep", 1) for _, p in fresh] + [swap(p, "shard", 1) for _, p in fresh]
        count = len(fresh)
        for n, (k, p) in enumerate(fresh):
            both.append((k, 0, p))
            both.append((k ^ 1, 0, passed[count + n]))
            both.append((k, 1, passed[n]))
        held = held + fresh
        mask //= 2
    late = [(k, p) for k, side, p in both if side == 1]
    came = yield [swap(p, "shard", 1) for _, p in late]
    both = both + [(k ^ 1, 1, p) for (k, _), p in zip(late, came)]
    pieces = [piece, beside] + [p for _, _, p in both]
    places = [shard * rows, (shard ^ 1) * rows]
    places += [(shard ^ k) * rows + (near ^ side) * (rows // 2) for k, side, _ in both]
    return lay_rows(pieces, jnp.stack(places).astype(jnp.int32))


def reduce_stream(grad, far_first):
    rows_all, width = grad.shape
    shards, replicas = lax.axis_size("shard"), lax.axis_size("rep")
    rows = rows_all // shards // replicas
    shard, replica = lax.axis_index("shard"), lax.axis_index("rep")
    core, far = shard & 1, shard >> 1
    near, rest = replica & 1, replica >> 1
    total = grad.reshape(shards // 2, 2, replicas // 2, 2, rows, width)
    away, keep = take(total, 1 - core, 1), take(total, core, 1)
    came = yield [swap(away, "shard", 1)]
    total = add(keep, came[0])

    def over_near(total):
        away, keep = take(total, 1 - near, total.ndim - 3), take(total, near, total.ndim - 3)
        came = yield [swap(away, "rep", 1)]
        return add(keep, came[0])

    def over_far(total):
        count = shards // 2
        while count > 1:
            count //= 2
            flag = (far // count) % 2
            total = total.reshape((2, count) + total.shape[1:])
            away, keep = take(total, 1 - flag, 0), take(total, flag, 0)
            came = yield [swap(away, "shard", 2 * count)]
            total = add(keep, came[0])
        return total[0]

    if far_first:
        total = yield from over_far(total)
        total = yield from over_near(total)
    else:
        total = yield from over_near(total)
        total = yield from over_far(total)
    others = range(1, replicas // 2)
    came = yield [swap(take(total, rest ^ k, 0), "rep", 2 * k) for k in others]
    total = add(take(total, rest, 0), *came)
    came = yield [swap(total, "rep", 2 * k) for k in others]
    mine = jnp.concatenate([total, *came], 0)
    came = yield [swap(mine, "rep", 1)]
    pieces = [mine[k * rows : (k + 1) * rows] for k in range(replicas // 2)]
    pieces += [came[0][k * rows : (k + 1) * rows] for k in range(replicas // 2)]
    places = [((rest ^ k) * 2 + (near ^ side)) * rows for side in range(2) for k in range(replicas // 2)]
    return pieces, jnp.stack(places).astype(jnp.int32)


def butterfly_stream(total):
    for axis in ("shard", "rep"):
        mask = 1
        while mask < lax.axis_size(axis):
            came = yield [swap(total, axis, mask)]
            total = total + came[0]
            mask *= 2
    return total


def small_stream(flat):
    held = flat[None]
    mask = 1
    shard = lax.axis_index("shard")
    while mask < lax.axis_size("shard"):
        came = yield [swap(held, "shard", mask)]
        flag = (shard & mask) == 0
        held = jnp.concatenate([jnp.where(flag, held, came[0]), jnp.where(flag, came[0], held)], 0)
        mask *= 2
    return held


def unpack_small(every, shapes, dims):
    parts = every.shape[0]
    outputs = []
    offset = 0
    for shape, dim in zip(shapes, dims):
        length = math.prod(shape)
        block = every[:, offset : offset + length].reshape((parts,) + shape)
        offset += length
        if dim == 0:
            outputs.append(block.reshape((-1,) + shape[1:]))
        else:
            outputs.append(jnp.swapaxes(block, 0, 1).reshape(shape[0], -1))
    return outputs


def own_block(values, dim):
    size = values.shape[dim] // lax.axis_size("shard")
    return lax.dynamic_slice_in_dim(values, lax.axis_index("shard") * size, size, dim)


def group_tables(lengths, order, input_rows, device):
    count = lengths.shape[0]
    slots = jnp.arange(count, dtype=jnp.int32)
    starts = jnp.cumsum(lengths) - lengths
    pick = (order[:, None] == slots[None, :]).astype(jnp.int32)
    owner_len = jnp.sum(pick * lengths[None, :], 1)
    owner_start = jnp.cumsum(owner_len) - owner_len
    owner_src = jnp.sum(pick * starts[None, :], 1)
    first_len = jnp.sum(jnp.where(slots == 2 * device, owner_len, 0))
    first_src = jnp.sum(jnp.where(slots == 2 * device, owner_src, 0))
    second_src = jnp.sum(jnp.where(slots == 2 * device + 1, owner_src, 0))
    local = jnp.arange(input_rows, dtype=jnp.int32)
    segment = (local >= first_len).astype(jnp.int32)
    position = local - segment * first_len
    source = jnp.where(segment > 0, second_src, first_src) + position
    given = device * input_rows + local
    seq_id = jnp.sum((starts[None, :] <= given[:, None]).astype(jnp.int32), 1) - 1
    member = (seq_id[:, None] == slots[None, :]).astype(jnp.int32)
    seq_start = jnp.sum(member * starts[None, :], 1)
    seq_owner_start = jnp.sum(pick * owner_start[:, None], 0)
    target = jnp.sum(member * seq_owner_start[None, :], 1) + given - seq_start
    return (source, position, first_len.reshape(1), target)


def rms_scale(values):
    return lax.rsqrt(jnp.mean(values * values, axis=-1, keepdims=True) + EPS)


def rms_norm(values, gain):
    return values * rms_scale(values) * gain


def rope_tables(position):
    half = HEAD_SIZE // 2
    lane = jnp.arange(SIDE, dtype=jnp.int32)
    ladder = (lane % half).astype(jnp.float32) * (2.0 / HEAD_SIZE)
    angles = position.astype(jnp.float32)[:, None] * jnp.exp(-math.log(ROPE_BASE) * ladder)
    sign = jnp.where(lane % HEAD_SIZE < half, -1.0, 1.0)
    return jnp.cos(angles), jnp.sin(angles) * sign


def conv_mixed(conv_in, conv_weight, conv_bias, position):
    width = conv_in.shape[1]
    mixed = conv_bias + conv_in * conv_weight[TAPS - 1]
    for back in range(1, TAPS):
        shifted = jnp.concatenate([jnp.zeros((back, width), jnp.float32), conv_in[:-back]], 0)
        same = (position >= back).astype(jnp.float32)[:, None]
        mixed = mixed + shifted * same * conv_weight[TAPS - 1 - back]
    return mixed


def gated_norm(ssm_y, gate_z, gain):
    gated = ssm_y * jax.nn.silu(gate_z)
    return gated * rms_scale(gated) * gain


def swiglu(gate_up):
    half = gate_up.shape[1] // 2
    return jax.nn.silu(gate_up[:, :half]) * gate_up[:, half:]


def dot(left, right):
    return jnp.dot(left, right, preferred_element_type=jnp.float32)


def head_lanes():
    head = lax.broadcasted_iota(jnp.int32, (SSM_HEADS, INNER), 0)
    lane = lax.broadcasted_iota(jnp.int32, (SSM_HEADS, INNER), 1)
    return (lane // SSM_HD == head).astype(jnp.float32)


def spread_heads(values):
    return jnp.dot(values, head_lanes(), precision=lax.Precision.HIGHEST)


def sum_heads(values):
    return lax.dot_general(
        values, head_lanes(), (((1,), (1,)), ((), ())), precision=lax.Precision.HIGHEST
    )


def on_device(
    tokens,
    seq_lengths,
    owner_order,
    gain_attn,
    w_input,
    w_step,
    step_bias,
    decay_log,
    skip_scale,
    conv_weight,
    conv_bias,
    gain_ssm,
    w_output,
    gain_ffn,
    w_gate_up,
    w_down,
    cotangent,
):
    input_rows = tokens.shape[0]
    shard = lax.axis_index("shard")
    flow = Flow()

    slot_tokens = flow.add(rows_stream(tokens))
    slot_input = flow.add(weight_stream(w_input))
    small_args = (gain_attn, w_step, step_bias, decay_log, skip_scale, conv_weight, conv_bias, gain_ssm, gain_ffn)
    small_dims = (0, 0, 0, 0, 0, 1, 0, 0, 0)
    slot_small = flow.add(small_stream(jnp.concatenate([a.reshape(-1) for a in small_args])))
    source, position, limit, target = group_tables(seq_lengths[0], owner_order[0], input_rows, shard)
    cosine, sine = rope_tables(position)
    source, position, limit, target, cosine, sine = flow.step((source, position, limit, target, cosine, sine))
    slot_output = flow.add(weight_stream(w_output))
    source, position = flow.step((source, position))
    slot_gate_up = flow.add(weight_stream(w_gate_up))
    source, position = flow.until([slot_tokens, slot_input, slot_small], (source, position))

    gain_attn_all, w_step_all, step_bias_all, decay_all, skip_all, conv_w_all, conv_b_all, gain_ssm_all, gain_ffn_all = (
        unpack_small(slot_small["result"], [a.shape for a in small_args], small_dims)
    )
    f32 = lambda v: v.astype(jnp.float32)
    gain_attn_f, gain_ssm_f, gain_ffn_f = f32(gain_attn_all), f32(gain_ssm_all), f32(gain_ffn_all)
    conv_w_f, conv_b_f = f32(conv_w_all), f32(conv_b_all)
    skip_lanes = jnp.repeat(f32(skip_all), SSM_HD)[None]
    pieces, owners = slot_tokens["result"]
    own_low = pick_rows(pieces, owners * input_rows, source)
    own = f32(own_low)
    w_input_all = slot_input["result"]

    normed = rms_norm(own, gain_attn_f).astype(jnp.bfloat16)
    projected = dot(normed, w_input_all)
    step_raw = dot(normed, w_step_all)
    projected, step_raw = flow.step((projected, step_raw))
    slot_down = flow.add(weight_stream(w_down))
    conv_in = projected[:, QUERY_KEY_VALUE + INNER :]
    gate_z = projected[:, QUERY_KEY_VALUE : QUERY_KEY_VALUE + INNER]
    conv_out = jax.nn.silu(conv_mixed(conv_in, conv_w_f, conv_b_f, position))
    inner_x = conv_out[:, :INNER]
    b_low = conv_out[:, INNER : INNER + STATE].astype(jnp.bfloat16)
    c_low = conv_out[:, INNER + STATE :].astype(jnp.bfloat16)
    step_pre = step_raw + f32(step_bias_all)
    step = jax.nn.softplus(step_pre)
    rate = -jnp.exp(f32(decay_all))
    cum = jnp.cumsum(step * rate, axis=0)
    step_lanes = spread_heads(step)
    x_step = (inner_x * step_lanes).astype(jnp.bfloat16)
    x_step, cum, b_low, c_low, inner_x, step_lanes = flow.step((x_step, cum, b_low, c_low, inner_x, step_lanes))
    ssd_out = ssd_forward(limit, c_low, b_low, x_step, cum)
    ssd_out, projected = flow.step((ssd_out, projected))
    attn_out, logs = attention_forward(limit, projected, cosine, sine)
    ssm_y = ssd_out + skip_lanes * inner_x
    gate_z = projected[:, QUERY_KEY_VALUE : QUERY_KEY_VALUE + INNER]
    ssm_out = gated_norm(ssm_y, gate_z, gain_ssm_f).astype(jnp.bfloat16)
    joined = jnp.concatenate([attn_out, ssm_out], 1)
    joined = flow.until([slot_output], joined)
    w_output_all = slot_output["result"]
    slot_cot = flow.add(rows_stream(cotangent))
    middle = own + dot(joined, w_output_all)
    normed_ffn = rms_norm(middle, gain_ffn_f).astype(jnp.bfloat16)
    normed_ffn, middle = flow.until([slot_gate_up], flow.step((normed_ffn, middle)))
    w_gate_up_all = slot_gate_up["result"]
    gate_up = dot(normed_ffn, w_gate_up_all)
    hidden = swiglu(gate_up).astype(jnp.bfloat16)
    gate_up, hidden = flow.until([slot_cot, slot_down], (gate_up, hidden))
    w_down_all = slot_down["result"]
    pieces, owners = slot_cot["result"]
    cot = pick_rows(pieces, owners * input_rows, source)

    def weight_grad(left, right):
        return lax.dot_general(
            left, right, (((0,), (0,)), ((), ())), preferred_element_type=jnp.float32
        ).astype(jnp.bfloat16)

    def back(left, weight):
        return lax.dot_general(left, weight, (((1,), (1,)), ((), ())), preferred_element_type=jnp.float32)

    grad_slots = {}
    grad_slots["down"] = [flow.add(reduce_stream(weight_grad(hidden, cot), True))]
    grad_hidden = back(cot, w_down_all)
    grad_gate_up = jax.vjp(swiglu, gate_up)[1](grad_hidden)[0].astype(jnp.bfloat16)
    grad_gate_up = flow.step(grad_gate_up)
    half = grad_gate_up.shape[1] // 2
    grad_slots["gate_up"] = [flow.add(reduce_stream(weight_grad(normed_ffn, grad_gate_up[:, :half]), True))]
    grad_normed_ffn = back(grad_gate_up, w_gate_up_all)
    grad_middle_norm, grad_gain_ffn = jax.vjp(rms_norm, middle, gain_ffn_f)[1](grad_normed_ffn)
    grad_middle = f32(cot) + grad_middle_norm
    grad_gate_up, grad_middle = flow.step((grad_gate_up, grad_middle))
    grad_slots["gate_up"].append(flow.add(reduce_stream(weight_grad(normed_ffn, grad_gate_up[:, half:]), False)))
    middle_low = grad_middle.astype(jnp.bfloat16)
    grad_joined = back(middle_low, w_output_all)
    grad_attn = grad_joined[:, : QUERY_HEADS * HEAD_SIZE].astype(jnp.bfloat16)
    grad_ssm_out = grad_joined[:, QUERY_HEADS * HEAD_SIZE :]
    grad_ssm_y, grad_z, grad_gain_ssm = jax.vjp(gated_norm, ssm_y, gate_z, gain_ssm_f)[1](grad_ssm_out)
    grad_z_low = grad_z.astype(jnp.bfloat16)
    grad_y_low = grad_ssm_y.astype(jnp.bfloat16)
    grad_ssm_y, grad_z_low, grad_attn, middle_low, grad_y_low = flow.step(
        (grad_ssm_y, grad_z_low, grad_attn, middle_low, grad_y_low)
    )
    grad_slots["output"] = [flow.add(reduce_stream(weight_grad(joined, middle_low), True))]
    grad_q, grad_kv = attention_backward(limit, projected, cosine, sine, grad_attn, logs)
    grad_q, grad_kv, grad_y_low = flow.step((grad_q, grad_kv, grad_y_low))
    grad_slots["input"] = [flow.add(reduce_stream(weight_grad(normed, grad_z_low), False))]
    back_x, grad_c, grad_b = ssd_backward(limit, c_low, b_low, x_step, grad_y_low, cum)
    back_x, grad_c, grad_b = flow.step((back_x, grad_c, grad_b))
    qkv = jnp.concatenate([grad_q, grad_kv], 1)
    grad_slots["input"].insert(0, flow.add(reduce_stream(weight_grad(normed, qkv), True)))
    grad_skip = jnp.sum(sum_heads(grad_ssm_y * inner_x), 0)
    grad_cum = sum_heads(f32(grad_y_low) * ssd_out - f32(x_step) * back_x)
    grad_step = sum_heads(back_x * inner_x)
    grad_x = back_x * step_lanes + skip_lanes * grad_ssm_y
    grad_inc = lax.cumsum(grad_cum, axis=0, reverse=True)
    grad_step = grad_step + grad_inc * rate
    grad_decay = jnp.sum(grad_inc * step, 0) * rate
    grad_step_pre = grad_step * jax.nn.sigmoid(step_pre)
    grad_step_bias = jnp.sum(grad_step_pre, 0)
    step_low = grad_step_pre.astype(jnp.bfloat16)
    grad_w_step = lax.dot_general(normed, step_low, (((0,), (0,)), ((), ())), preferred_element_type=jnp.float32)
    grad_conv = jnp.concatenate([grad_x, grad_b, grad_c], 1)
    mixed_back = jax.vjp(
        lambda u, w, b: jax.nn.silu(conv_mixed(u, w, b, position)), conv_in, conv_w_f, conv_b_f
    )[1]
    grad_u, grad_conv_w, grad_conv_b = mixed_back(grad_conv)
    grad_u_low = grad_u.astype(jnp.bfloat16)
    grad_u_low, step_low = flow.step((grad_u_low, step_low))
    grad_slots["input"].append(flow.add(reduce_stream(weight_grad(normed, grad_u_low), True)))
    grad_projected = jnp.concatenate([qkv, grad_z_low, grad_u_low], 1)
    grad_normed = back(grad_projected, w_input_all) + back(step_low, w_step_all)
    grad_tokens_norm, grad_gain_attn = jax.vjp(rms_norm, own, gain_attn_f)[1](grad_normed)
    grad_low = (grad_middle + grad_tokens_norm).astype(jnp.bfloat16)
    small_grads = (
        grad_gain_attn,
        grad_w_step,
        grad_step_bias,
        grad_decay,
        grad_skip,
        grad_conv_w,
        grad_conv_b,
        grad_gain_ssm,
        grad_gain_ffn,
    )
    flat = jnp.concatenate([g.reshape(-1) for g in small_grads])
    flat = jnp.pad(flat, (0, -flat.shape[0] % 1024)).reshape(-1, SIDE)
    grad_low, flat = flow.step((grad_low, flat))
    slot_grad = flow.add(rows_stream(grad_low))
    slot_flat = flow.add(butterfly_stream(flat))
    block_low = (middle + dot(hidden, w_down_all)).astype(jnp.bfloat16)
    slot_block = flow.add(rows_stream(block_low))
    target = flow.until(list(flow.live), target)

    pieces, owners = slot_block["result"]
    block_out = pick_rows(pieces, owners * input_rows, target)
    pieces, owners = slot_grad["result"]
    grad_tokens = pick_rows(pieces, owners * input_rows, target)
    outs = [None] * 13
    summed = slot_flat["result"].reshape(-1)
    offset = 0
    for i, grad in zip((0, 2, 3, 4, 5, 6, 7, 8, 10), small_grads):
        block = summed[offset : offset + grad.size].reshape(grad.shape)
        offset += grad.size
        outs[i] = own_block(block, 1 if i == 6 else 0)
    for i, name in ((1, "input"), (9, "output"), (11, "gate_up"), (12, "down")):
        parts = [widen_rows(*slot["result"]) for slot in grad_slots[name]]
        outs[i] = parts[0] if len(parts) == 1 else jnp.concatenate(parts, 1)
    return (block_out, grad_tokens, *outs)


def solution(mesh):
    placed = (
        P(("rep", "shard"), None),
        P("rep", None),
        P("rep", None),
        P("shard"),
        P("shard", None),
        P("shard", None),
        P("shard"),
        P("shard"),
        P("shard"),
        P(None, "shard"),
        P("shard"),
        P("shard"),
        P("shard", None),
        P("shard"),
        P("shard", None),
        P("shard", None),
        P(("rep", "shard"), None),
    )
    return jax.shard_map(
        on_device,
        mesh=mesh,
        in_specs=placed,
        out_specs=(
            P(("rep", "shard"), None),
            P(("rep", "shard"), None),
            P("shard"),
            P("shard", None),
            P("shard", None),
            P("shard"),
            P("shard"),
            P("shard"),
            P(None, "shard"),
            P("shard"),
            P("shard"),
            P("shard", None),
            P("shard"),
            P("shard", None),
            P("shard", None),
        ),
        check_vma=False,
    )
```

```python
from functools import partial
import math

import jax
import jax.numpy as jnp
from jax import lax
from jax.experimental import pallas as pl
from jax.experimental.pallas import tpu as pltpu
from jax.sharding import PartitionSpec as P

QUERY_HEADS = 8
KEY_VALUE_HEADS = 2
HEAD_SIZE = 64
SSM_HEADS = 24
SSM_HD = 64
STATE = 128
INNER = 1536
QUERY_KEY_VALUE = 768
TAPS = 4

EPS = 1e-05
ROPE_BASE = 100000000000.0
SIDE = 128
QUAD = 4
LOW = -1e30
SCALE = HEAD_SIZE ** (-0.5)


def causal_bias(limit, rows, row0, cols):
    i = lax.broadcasted_iota(jnp.int32, (rows, cols), 0) + row0
    j = lax.broadcasted_iota(jnp.int32, (rows, cols), 1)
    seen = (j <= i) & ((j >= limit) | (i < limit))
    return jnp.where(seen, 0.0, LOW)


def contract_last(left, right):
    return lax.dot_general(left, right, (((1,), (1,)), ((), ())), preferred_element_type=jnp.float32)


def contract_first(left, right):
    return lax.dot_general(left, right, (((0,), (0,)), ((), ())), preferred_element_type=jnp.float32)


def halves(pair):
    lane = lax.broadcasted_iota(jnp.int32, pair.shape, 1)
    zero = jnp.zeros_like(pair)
    return (jnp.where(lane < HEAD_SIZE, pair, zero), jnp.where(lane >= HEAD_SIZE, pair, zero))


def four_lanes(values, step):
    return pltpu.roll(values, lax.rem(SIDE - QUAD * step, SIDE), 1)


def ssd_forward_kernel(limit_ref, c_ref, b_ref, x_ref, cum_col_ref, cum_row_ref, out_ref, inter, bias):
    count = c_ref.shape[0]

    @pl.when(pl.program_id(0) == 0)
    def _():
        inter[...] = contract_last(c_ref[...], b_ref[...])
        bias[...] = causal_bias(limit_ref[0], count, 0, count)

    step = pl.program_id(0)
    cum_col = four_lanes(cum_col_ref[...], step)
    cum_row = cum_row_ref[pl.ds(pl.multiple_of(step // 2 * 8, 8), 8), :]
    cum_row = jnp.where(step % 2 == 0, cum_row[:QUAD], cum_row[QUAD:])
    for pair in range(QUAD // 2):
        lanes = slice(pair * SIDE, (pair + 1) * SIDE)
        sides = halves(x_ref[:, lanes])
        for top in range(0, count, SIDE):
            rows = slice(top, top + SIDE)
            seen = top + SIDE
            total = None
            for half in range(2):
                h = pair * 2 + half
                gap = cum_col[rows, h : h + 1] - cum_row[h : h + 1, :seen]
                mixer = (inter[rows, :seen] * jnp.exp(gap + bias[rows, :seen])).astype(jnp.bfloat16)
                part = jnp.dot(mixer, sides[half][:seen], preferred_element_type=jnp.float32)
                total = part if total is None else total + part
            out_ref[rows, lanes] = total


def ssd_forward(limit, low, tables):
    count = low.shape[0]
    steps = SSM_HEADS // QUAD
    b_spec = pl.BlockSpec((count, STATE), lambda i: (0, INNER // STATE))
    c_spec = pl.BlockSpec((count, STATE), lambda i: (0, INNER // STATE + 1))
    return pl.pallas_call(
        ssd_forward_kernel,
        grid=(steps,),
        out_shape=jax.ShapeDtypeStruct((count, INNER), jnp.float32),
        in_specs=[
            pl.BlockSpec(memory_space=pltpu.SMEM),
            c_spec,
            b_spec,
            pl.BlockSpec((count, QUAD * HEAD_SIZE), lambda i: (0, i)),
            pl.BlockSpec((count, SIDE), lambda i: (0, 0)),
            pl.BlockSpec((SIDE, count), lambda i: (0, 0)),
        ],
        out_specs=pl.BlockSpec((count, QUAD * HEAD_SIZE), lambda i: (0, i)),
        scratch_shapes=[pltpu.VMEM((count, count), jnp.float32)] * 2,
        name="ssd_forward",
    )(limit, low, low, low, *tables)


def ssd_backward_kernel(
    limit_ref, c_ref, b_ref, x_ref, dy_ref, cum_col_ref, cum_row_ref, z_ref, gbc_ref, inter, bias, total
):
    count = c_ref.shape[0]

    @pl.when(pl.program_id(0) == 0)
    def _():
        inter[...] = contract_last(c_ref[...], b_ref[...])
        bias[...] = causal_bias(limit_ref[0], count, 0, count)
        total[...] = jnp.zeros_like(total)

    step = pl.program_id(0)
    cum_col = four_lanes(cum_col_ref[...], step)
    cum_row = cum_row_ref[pl.ds(pl.multiple_of(step // 2 * 8, 8), 8), :]
    cum_row = jnp.where(step % 2 == 0, cum_row[:QUAD], cum_row[QUAD:])
    for pair in range(QUAD // 2):
        lanes = slice(pair * SIDE, (pair + 1) * SIDE)
        x_pair = x_ref[:, lanes]
        sides = halves(dy_ref[:, lanes])
        for top in reversed(range(0, count, SIDE)):
            rows = slice(top, top + SIDE)
            seen = top + SIDE
            grad = None
            back = None
            for half in range(2):
                h = pair * 2 + half
                gap = cum_col[rows, h : h + 1] - cum_row[h : h + 1, :seen]
                decay = jnp.exp(gap + bias[rows, :seen])
                mixer = (inter[rows, :seen] * decay).astype(jnp.bfloat16)
                grad_mixer = contract_last(sides[half][rows], x_pair[:seen])
                part = grad_mixer * decay
                grad = part if grad is None else grad + part
                part = contract_first(mixer, sides[half][rows])
                back = part if back is None else back + part
            total[rows, :seen] += grad
            if seen == count:
                z_ref[:, lanes] = back
            else:
                z_ref[:seen, lanes] += back

    @pl.when(pl.program_id(0) == pl.num_programs(0) - 1)
    def _():
        low = total[...].astype(jnp.bfloat16)
        gbc_ref[:, :STATE] = contract_first(low, c_ref[...])
        gbc_ref[:, STATE:] = jnp.dot(low, b_ref[...], preferred_element_type=jnp.float32)


def ssd_backward(limit, low, grad_y, tables):
    count = low.shape[0]
    steps = SSM_HEADS // QUAD
    b_spec = pl.BlockSpec((count, STATE), lambda i: (0, INNER // STATE))
    c_spec = pl.BlockSpec((count, STATE), lambda i: (0, INNER // STATE + 1))
    quad = pl.BlockSpec((count, QUAD * HEAD_SIZE), lambda i: (0, i))
    return pl.pallas_call(
        ssd_backward_kernel,
        grid=(steps,),
        out_shape=(
            jax.ShapeDtypeStruct((count, INNER), jnp.float32),
            jax.ShapeDtypeStruct((count, 2 * STATE), jnp.float32),
        ),
        in_specs=[
            pl.BlockSpec(memory_space=pltpu.SMEM),
            c_spec,
            b_spec,
            quad,
            quad,
            pl.BlockSpec((count, SIDE), lambda i: (0, 0)),
            pl.BlockSpec((SIDE, count), lambda i: (0, 0)),
        ],
        out_specs=(quad, pl.BlockSpec((count, 2 * STATE), lambda i: (0, 0))),
        scratch_shapes=[pltpu.VMEM((count, count), jnp.float32)] * 3,
        name="ssd_backward",
    )(limit, low, low, low, grad_y, *tables)


def turn(values, cosine, sine):
    lane = lax.broadcasted_iota(jnp.int32, values.shape, 1) % HEAD_SIZE
    width = values.shape[1]
    ahead = pltpu.roll(values, width - HEAD_SIZE // 2, 1)
    behind = pltpu.roll(values, HEAD_SIZE // 2, 1)
    other = jnp.where(lane < HEAD_SIZE // 2, ahead, behind)
    return values * cosine + other * sine


def both_sides(pair, step):
    lane = lax.broadcasted_iota(jnp.int32, pair.shape, 1)
    mine = jnp.where((lane >= HEAD_SIZE) == (step > 0), pair, jnp.zeros_like(pair))
    return (mine + pltpu.roll(mine, HEAD_SIZE, 1)).astype(jnp.bfloat16)


def attention_forward_kernel(limit_ref, q_ref, k_ref, v_ref, cos_ref, sin_ref, out_ref, log_ref, bias):
    count = k_ref.shape[0]
    step = pl.program_id(0)

    @pl.when(step == 0)
    def _():
        bias[...] = causal_bias(limit_ref[0], count, 0, count)

    cosine, sine = cos_ref[...], sin_ref[...]
    key = both_sides(turn(k_ref[...], cosine, sine), step)
    value_sides = halves(both_sides(v_ref[...], step))
    for pair in range(2):
        lanes = slice(pair * SIDE, (pair + 1) * SIDE)
        sides = halves(turn(q_ref[:, lanes], cosine, sine).astype(jnp.bfloat16) * SCALE)
        for top in range(0, count, SIDE):
            rows = slice(top, top + SIDE)
            seen = top + SIDE
            total = None
            for half in range(2):
                score = contract_last(sides[half][rows], key[:seen]) + bias[rows, :seen]
                largest = jnp.max(score, -1, keepdims=True)
                raised = jnp.exp(score - largest)
                mass = jnp.sum(raised, -1, keepdims=True)
                weights = (raised * (1.0 / mass)).astype(jnp.bfloat16)
                part = jnp.dot(weights, value_sides[half][:seen], preferred_element_type=jnp.float32)
                total = part if total is None else total + part
                h = pair * 2 + half
                log_ref[0, rows, h : h + 1] = largest + jnp.log(mass)
            out_ref[rows, lanes] = total.astype(jnp.bfloat16)


def attention_specs(count):
    wide = pl.BlockSpec((count, 2 * SIDE), lambda i: (0, i))
    whole = pl.BlockSpec((count, SIDE), lambda i: (0, 0))
    keys = pl.BlockSpec((count, SIDE), lambda i: (0, QUERY_HEADS * HEAD_SIZE // SIDE))
    values = pl.BlockSpec((count, SIDE), lambda i: (0, QUERY_HEADS * HEAD_SIZE // SIDE + 1))
    logs = pl.BlockSpec((1, count, QUAD), lambda i: (i, 0, 0))
    return wide, whole, keys, values, logs


def attention_forward(limit, projected, cosine, sine):
    count = projected.shape[0]
    wide, whole, keys, values, logs = attention_specs(count)
    return pl.pallas_call(
        attention_forward_kernel,
        grid=(KEY_VALUE_HEADS,),
        out_shape=(
            jax.ShapeDtypeStruct((count, QUERY_HEADS * HEAD_SIZE), jnp.bfloat16),
            jax.ShapeDtypeStruct((KEY_VALUE_HEADS, count, QUAD), jnp.float32),
        ),
        in_specs=[pl.BlockSpec(memory_space=pltpu.SMEM), wide, keys, values, whole, whole],
        out_specs=(wide, logs),
        scratch_shapes=[pltpu.VMEM((count, count), jnp.float32)],
        name="attention_forward",
    )(limit, projected, projected, projected, cosine, sine)


def attention_backward_kernel(
    limit_ref, q_ref, k_ref, v_ref, cos_ref, sin_ref, go_ref, log_ref, gq_ref, gkv_ref, bias, gk, gv
):
    count = k_ref.shape[0]
    step = pl.program_id(0)

    @pl.when(step == 0)
    def _():
        bias[...] = causal_bias(limit_ref[0], count, 0, count)

    cosine, sine = cos_ref[...], sin_ref[...]
    key = both_sides(turn(k_ref[...], cosine, sine), step)
    value = both_sides(v_ref[...], step)
    key_sides = halves(key)
    gk[...] = jnp.zeros_like(gk)
    gv[...] = jnp.zeros_like(gv)
    for pair in range(2):
        lanes = slice(pair * SIDE, (pair + 1) * SIDE)
        q_sides = halves(turn(q_ref[:, lanes], cosine, sine).astype(jnp.bfloat16) * SCALE)
        go_sides = halves(go_ref[:, lanes])
        for top in range(0, count, SIDE):
            rows = slice(top, top + SIDE)
            seen = top + SIDE
            total = None
            for half in range(2):
                h = pair * 2 + half
                score = contract_last(q_sides[half][rows], key[:seen])
                weights = jnp.exp(score + bias[rows, :seen] - log_ref[0, rows, h : h + 1])
                grad = contract_last(go_sides[half][rows], value[:seen])
                inner = jnp.sum(grad * weights, -1, keepdims=True)
                low = (weights * (grad - inner)).astype(jnp.bfloat16)
                part = jnp.dot(low, key_sides[half][:seen], preferred_element_type=jnp.float32)
                total = part if total is None else total + part
                gk[:seen, :] += contract_first(low, q_sides[half][rows])
                gv[:seen, :] += contract_first(weights.astype(jnp.bfloat16), go_sides[half][rows])
            gq_ref[rows, lanes] = turn(total * SCALE, cosine[rows], -sine[rows]).astype(jnp.bfloat16)
    lane = lax.broadcasted_iota(jnp.int32, (count, SIDE), 1)
    mine = (lane >= HEAD_SIZE) == (step > 0)
    for place, part in enumerate((gk, gv)):
        summed = part[...] + pltpu.roll(part[...], HEAD_SIZE, 1)
        if place == 0:
            summed = turn(summed, cosine, -sine)
        lanes = slice(place * SIDE, (place + 1) * SIDE)
        @pl.when(step == 0)
        def _():
            gkv_ref[:, lanes] = summed.astype(jnp.bfloat16)

        @pl.when(step > 0)
        def _():
            gkv_ref[:, lanes] = jnp.where(mine, summed, gkv_ref[:, lanes].astype(jnp.float32)).astype(jnp.bfloat16)


def attention_backward(limit, projected, cosine, sine, grad_out, logs_in):
    count = projected.shape[0]
    wide, whole, keys, values, logs = attention_specs(count)
    return pl.pallas_call(
        attention_backward_kernel,
        grid=(KEY_VALUE_HEADS,),
        out_shape=(
            jax.ShapeDtypeStruct((count, QUERY_HEADS * HEAD_SIZE), jnp.bfloat16),
            jax.ShapeDtypeStruct((count, 2 * SIDE), jnp.bfloat16),
        ),
        in_specs=[pl.BlockSpec(memory_space=pltpu.SMEM), wide, keys, values, whole, whole, wide, logs],
        out_specs=(wide, pl.BlockSpec((count, 2 * SIDE), lambda i: (0, 0))),
        scratch_shapes=[
            pltpu.VMEM((count, count), jnp.float32),
            pltpu.VMEM((count, SIDE), jnp.float32),
            pltpu.VMEM((count, SIDE), jnp.float32),
        ],
        name="attention_backward",
    )(limit, projected, projected, projected, cosine, sine, grad_out, logs_in)


BLOCK = QUAD * HEAD_SIZE


TILE = 128
HALO = 8


def conv_taps(u_ref, top, place, weight_ref, bias_ref, lanes):
    mixed = bias_ref[:, lanes] + u_ref[HALO + top : HALO + top + TILE, lanes] * weight_ref[TAPS - 1 : TAPS, lanes]
    for back in range(1, TAPS):
        shifted = u_ref[HALO + top - back : HALO + top - back + TILE, lanes]
        mixed = mixed + jnp.where(place >= back, shifted, 0.0) * weight_ref[TAPS - 1 - back : TAPS - back, lanes]
    return mixed


def conv_forward_kernel(u_ref, place_ref, weight_ref, bias_ref, step_ref, out_ref, low_ref, held):
    count = u_ref.shape[0]
    held[:HALO, :] = jnp.zeros((HALO, BLOCK), jnp.float32)
    held[HALO:, :] = u_ref[...]
    lane = lax.broadcasted_iota(jnp.int32, (TILE, SIDE), 1)
    scale = four_lanes(step_ref[...], pl.program_id(0))
    for side in range(BLOCK // SIDE):
        lanes = slice(side * SIDE, (side + 1) * SIDE)
        for top in range(0, count, TILE):
            rows = slice(top, top + TILE)
            mixed = conv_taps(held, top, place_ref[rows], weight_ref, bias_ref, lanes)
            out = mixed / (1.0 + jnp.exp(-mixed))
            out_ref[rows, lanes] = out
            first, second = scale[rows, 2 * side : 2 * side + 1], scale[rows, 2 * side + 1 : 2 * side + 2]
            low_ref[rows, lanes] = (out * jnp.where(lane < HEAD_SIZE, first, second)).astype(jnp.bfloat16)


def conv_specs(count, width):
    column = lambda i: (0, i)
    first = (QUERY_KEY_VALUE + INNER) // BLOCK
    return (
        pl.BlockSpec((count, BLOCK), lambda i: (0, first + i)),
        pl.BlockSpec((count, 1), lambda i: (0, 0)),
        pl.BlockSpec((TAPS, BLOCK), column),
        pl.BlockSpec((1, BLOCK), column),
        pl.BlockSpec((count, SIDE), lambda i: (0, 0)),
        pl.BlockSpec((count, BLOCK), column),
    )


def conv_forward(projected, position, weight, bias, step_quads):
    count, width = projected.shape[0], weight.shape[1]
    u, place, taps, row, quads, block = conv_specs(count, width)
    return pl.pallas_call(
        conv_forward_kernel,
        grid=(width // BLOCK,),
        out_shape=(
            jax.ShapeDtypeStruct((count, width), jnp.float32),
            jax.ShapeDtypeStruct((count, width), jnp.bfloat16),
        ),
        in_specs=[u, place, taps, row, quads],
        out_specs=(block, block),
        scratch_shapes=[pltpu.VMEM((HALO + count, BLOCK), jnp.float32)],
        name="conv_forward",
    )(projected, position[:, None], weight, bias[None], step_quads)


def head_sums(values, chosen):
    high = values.astype(jnp.bfloat16)
    rest = values - high.astype(jnp.float32)
    middle = rest.astype(jnp.bfloat16)
    low = (rest - middle.astype(jnp.float32)).astype(jnp.bfloat16)
    total = jnp.dot(high, chosen, preferred_element_type=jnp.float32)
    total = total + jnp.dot(middle, chosen, preferred_element_type=jnp.float32)
    return total + jnp.dot(low, chosen, preferred_element_type=jnp.float32)


def conv_backward_kernel(
    u_ref, place_ref, weight_ref, bias_ref, step_ref, skip_ref, z_ref, gy_ref, y_ref, low_ref, gbc_ref,
    gu_ref, gw_ref, heads_ref, held, grads,
):
    count = u_ref.shape[0]
    step = pl.program_id(0)
    inner = step < pl.num_programs(0) - 1
    scale = four_lanes(step_ref[...], step)
    held[:HALO, :] = jnp.zeros((HALO, BLOCK), jnp.float32)
    held[HALO:, :] = u_ref[...]
    lane = lax.broadcasted_iota(jnp.int32, (TILE, SIDE), 1)

    @pl.when(step == 0)
    def _():
        heads_ref[...] = jnp.zeros_like(heads_ref)

    for side in range(BLOCK // SIDE):
        lanes = slice(side * SIDE, (side + 1) * SIDE)
        sums = [None] * (TAPS + 1)
        head = lax.broadcasted_iota(jnp.int32, (SIDE, SIDE), 0) // HEAD_SIZE + 2 * side + QUAD * step
        column = lax.broadcasted_iota(jnp.int32, (SIDE, SIDE), 1)
        chosen = [(head + offset == column).astype(jnp.bfloat16) for offset in (0, 32, 64)]
        for back in range(1, TAPS):
            grads[back - 1, count:, lanes] = jnp.zeros((HALO, SIDE), jnp.float32)
        for top in range(0, count, TILE):
            rows = slice(top, top + TILE)
            place = place_ref[rows]
            mixed = conv_taps(held, top, place, weight_ref, bias_ref, lanes)
            gate = 1.0 / (1.0 + jnp.exp(-mixed))
            out = mixed * gate
            z, gy = z_ref[rows, lanes], gy_ref[rows, lanes]
            first, second = scale[rows, 2 * side : 2 * side + 1], scale[rows, 2 * side + 1 : 2 * side + 2]
            grad = z * jnp.where(lane < HEAD_SIZE, first, second) + skip_ref[:, lanes] * gy
            grad = jnp.where(inner, grad, gbc_ref[rows, lanes])
            gy_low = gy.astype(jnp.bfloat16).astype(jnp.float32)
            cum = gy_low * y_ref[rows, lanes] - low_ref[rows, lanes].astype(jnp.float32) * z
            part = head_sums(z * out, chosen[0]) + head_sums(cum, chosen[1]) + head_sums(gy * out, chosen[2])
            heads_ref[rows, :] += jnp.where(inner, part, 0.0)
            grad = grad * (gate + out * (1.0 - gate))
            parts = [jnp.sum(grad, 0, keepdims=True)]
            parts.append(jnp.sum(grad * held[HALO + top : HALO + top + TILE, lanes], 0, keepdims=True))
            grads[TAPS - 1, rows, lanes] = grad * weight_ref[TAPS - 1 : TAPS, lanes]
            for back in range(1, TAPS):
                seen = jnp.where(place >= back, grad, 0.0)
                shifted = held[HALO + top - back : HALO + top - back + TILE, lanes]
                parts.append(jnp.sum(seen * shifted, 0, keepdims=True))
                grads[back - 1, rows, lanes] = seen * weight_ref[TAPS - 1 - back : TAPS - back, lanes]
            sums = [p if s is None else s + p for s, p in zip(sums, parts)]
        gw_ref[:, lanes] = jnp.zeros((8, SIDE), jnp.float32)
        gw_ref[TAPS : TAPS + 1, lanes] = sums[0]
        for back in range(TAPS):
            gw_ref[TAPS - 1 - back : TAPS - back, lanes] = sums[1 + back]
        for top in range(0, count, TILE):
            total = grads[TAPS - 1, top : top + TILE, lanes]
            for back in range(1, TAPS):
                total = total + grads[back - 1, top + back : top + back + TILE, lanes]
            gu_ref[top : top + TILE, lanes] = total.astype(jnp.bfloat16)


def conv_backward(projected, position, weight, bias, step_quads, skip, z, grad_y, y, low, grad_bc):
    count, width = projected.shape[0], weight.shape[1]
    u, place, taps, row, quads, block = conv_specs(count, width)
    last = INNER // BLOCK - 1
    inner = pl.BlockSpec((count, BLOCK), lambda i: (0, jnp.minimum(i, last)))
    skip_row = pl.BlockSpec((1, BLOCK), lambda i: (0, jnp.minimum(i, last)))
    return pl.pallas_call(
        conv_backward_kernel,
        grid=(width // BLOCK,),
        out_shape=(
            jax.ShapeDtypeStruct((count, width), jnp.bfloat16),
            jax.ShapeDtypeStruct((8, width), jnp.float32),
            jax.ShapeDtypeStruct((count, SIDE), jnp.float32),
        ),
        in_specs=[u, place, taps, row, quads, skip_row, inner, inner, inner, block, pl.BlockSpec((count, BLOCK), lambda i: (0, 0))],
        out_specs=(block, pl.BlockSpec((8, BLOCK), lambda i: (0, i)), pl.BlockSpec((count, SIDE), lambda i: (0, 0))),
        scratch_shapes=[
            pltpu.VMEM((HALO + count, BLOCK), jnp.float32),
            pltpu.VMEM((TAPS, count + HALO, BLOCK), jnp.float32),
        ],
        name="conv_backward",
    )(projected, position[:, None], weight, bias[None], step_quads, skip, z, grad_y, y, low, grad_bc)


def pick_kernel(shift_ref, wanted_ref, *refs):
    out_ref = refs[-1]
    pieces = refs[:-1]
    count = pieces[0].shape[0]
    place = lax.broadcasted_iota(jnp.int32, (out_ref.shape[0], count), 1)
    total = None
    for n, piece in enumerate(pieces):
        choice = (wanted_ref[...] - shift_ref[n] == place).astype(jnp.bfloat16)
        part = jnp.dot(choice, piece[...], preferred_element_type=jnp.float32)
        total = part if total is None else total + part
    out_ref[...] = total.astype(out_ref.dtype)


def pick_rows(pieces, shifts, wanted):
    vmem = pl.BlockSpec(memory_space=pltpu.VMEM)
    return pl.pallas_call(
        pick_kernel,
        out_shape=jax.ShapeDtypeStruct((wanted.shape[0], pieces[0].shape[1]), pieces[0].dtype),
        in_specs=[pl.BlockSpec(memory_space=pltpu.SMEM), vmem] + [vmem] * len(pieces),
        out_specs=vmem,
        name="pick_rows",
    )(shifts, wanted[:, None], *pieces)


def lay_rows_kernel(place_ref, *refs):
    sems = refs[-1]
    out_ref = refs[-2]
    pieces = refs[:-2]
    copies = []
    for n, piece in enumerate(pieces):
        rows = piece.shape[0]
        start = pl.multiple_of(place_ref[n] * 16, 16)
        copies.append(pltpu.make_async_copy(piece, out_ref.at[pl.ds(start, rows)], sems.at[n]))
    for copy in copies:
        copy.start()
    for copy in copies:
        copy.wait()


def lay_rows(pieces, places):
    rows = sum(piece.shape[0] for piece in pieces)
    hbm = pl.BlockSpec(memory_space=pl.ANY)
    return pl.pallas_call(
        lay_rows_kernel,
        out_shape=jax.ShapeDtypeStruct((rows, pieces[0].shape[1]), pieces[0].dtype),
        in_specs=[pl.BlockSpec(memory_space=pltpu.SMEM)] + [hbm] * len(pieces),
        out_specs=pl.BlockSpec(memory_space=pltpu.VMEM),
        scratch_shapes=[pltpu.SemaphoreType.DMA((len(pieces),))],
        name="lay_rows",
    )(places // 16, *pieces)


def widen_kernel(parts, columns, place_ref, *refs):
    out_ref = refs[-1]
    for n, block in enumerate(refs[:-1]):
        rows = block.shape[0] // parts
        left = columns[n // 2]
        for k in range(parts):
            start = pl.multiple_of(place_ref[(n % 2) * parts + k] * rows, rows)
            piece = block[k * rows : (k + 1) * rows, :].astype(jnp.float32)
            out_ref[pl.ds(start, rows), left : left + block.shape[1]] = piece


def widen_rows(chunks, places):
    flat = [block for chunk in chunks for block in chunk]
    columns, left = [], 0
    for chunk in chunks:
        columns.append(left)
        left += chunk[0].shape[1]
    rows = 2 * chunks[0][0].shape[0]
    vmem = pl.BlockSpec(memory_space=pltpu.VMEM)
    return pl.pallas_call(
        partial(widen_kernel, places.shape[0] // 2, tuple(columns)),
        out_shape=jax.ShapeDtypeStruct((rows, left), jnp.float32),
        in_specs=[pl.BlockSpec(memory_space=pltpu.SMEM)] + [vmem] * len(flat),
        out_specs=vmem,
        name="widen_rows",
    )(places, *flat)


def swap(values, axis, mask):
    count = lax.axis_size(axis)
    return lax.ppermute(values, axis, [(i, i ^ mask) for i in range(count)])


def take(values, index, dim):
    return lax.dynamic_index_in_dim(values, index, dim, keepdims=False)


def add(first, *others):
    total = first.astype(jnp.float32)
    for other in others:
        total = total + other.astype(jnp.float32)
    return total.astype(jnp.bfloat16)


class Flow:
    def __init__(self):
        self.live = []

    def add(self, stream):
        slot = {"stream": stream, "sent": None, "result": None, "done": False}
        self.live.append(slot)
        self._advance(slot, None)
        return slot

    def _advance(self, slot, value):
        try:
            slot["sent"] = slot["stream"].send(value)
        except StopIteration as stop:
            slot["result"] = stop.value
            slot["sent"] = None
            slot["done"] = True
            self.live.remove(slot)

    def step(self, values=None, slots=None):
        slots = [slot for slot in (self.live if slots is None else slots) if not slot["done"]]
        values, sent = lax.optimization_barrier((values, [slot["sent"] for slot in slots]))
        for slot, came in zip(slots, sent):
            self._advance(slot, came)
        return values

    def until(self, slots, values=None, alone=False):
        while any(not slot["done"] for slot in slots):
            values = self.step(values, slots if alone else None)
        return values


def rows_stream(piece):
    shard = lax.axis_index("shard")
    held = [(0, piece)]
    mask = lax.axis_size("shard") // 2
    first = True
    near = None
    while mask > 1:
        send = [swap(p, "shard", mask) for _, p in held]
        if first:
            send.append(swap(piece, "shard", 1))
        came = yield send
        if first:
            near = came[-1]
            first = False
        held = held + [(k ^ mask, p) for (k, _), p in zip(held, came)]
        mask //= 2
    came = yield [swap(p, "shard", 1) for k, p in held[1:]]
    held = held + [(1, near)] + [(k ^ 1, p) for (k, _), p in zip(held[1:], came)]
    keys = [k for k, _ in held]
    return [p for _, p in held], jnp.stack([shard ^ k for k in keys]).astype(jnp.int32)


def weight_stream(piece):
    rows, width = piece.shape
    shard, near = lax.axis_index("shard"), lax.axis_index("rep") & 1
    part = lax.dynamic_slice_in_dim(piece, near * (rows // 2), rows // 2, 0)
    held = [(0, part)]
    both = []
    mask = lax.axis_size("shard") // 2
    beside = None
    while mask > 1:
        send = [swap(p, "shard", mask) for _, p in held]
        if beside is None:
            send.append(swap(piece, "shard", 1))
        came = yield send
        if beside is None:
            beside = came[-1]
        fresh = [(k ^ mask, p) for (k, _), p in zip(held, came)]
        passed = yield [swap(p, "rep", 1) for _, p in fresh] + [swap(p, "shard", 1) for _, p in fresh]
        count = len(fresh)
        for n, (k, p) in enumerate(fresh):
            both.append((k, 0, p))
            both.append((k ^ 1, 0, passed[count + n]))
            both.append((k, 1, passed[n]))
        held = held + fresh
        mask //= 2
    late = [(k, p) for k, side, p in both if side == 1]
    came = yield [swap(p, "shard", 1) for _, p in late]
    both = both + [(k ^ 1, 1, p) for (k, _), p in zip(late, came)]
    pieces = [piece, beside] + [p for _, _, p in both]
    places = [shard * rows, (shard ^ 1) * rows]
    places += [(shard ^ k) * rows + (near ^ side) * (rows // 2) for k, side, _ in both]
    return lay_rows(pieces, jnp.stack(places).astype(jnp.int32))


def transposed_dot(left, right):
    return lax.dot_general(left, right, (((0,), (0,)), ((), ())), preferred_element_type=jnp.float32)


def reduce_stream(left, right, direct=False):
    shards, replicas = lax.axis_size("shard"), lax.axis_size("rep")
    block = left.shape[1] // shards
    rows = block // replicas
    width = right.shape[1]
    shard, replica = lax.axis_index("shard"), lax.axis_index("rep")
    core, far = shard & 1, shard >> 1
    near, rest = replica & 1, replica >> 1

    def product(r, c, extras=(), half=None):
        start, size = ((far ^ r) * 2 + c) * block, block
        if half is not None:
            size = block // 2
            start = start + half * size
            extras = [x if x.shape[0] == size else lax.dynamic_slice_in_dim(x, half * size, size, 0) for x in extras]
        total = transposed_dot(lax.dynamic_slice_in_dim(left, start, size, 1), right)
        for extra in extras:
            total = total + extra.astype(jnp.float32)
        return total.astype(jnp.bfloat16)

    count = shards // 2
    came = yield [swap(product(r, 1 - core), "shard", 1) for r in range(count)]
    extras = [[c] for c in came]
    while count > 1:
        count //= 2
        came = yield [swap(product(r, core, extras[r]), "shard", 2 * count) for r in range(count, 2 * count)]
        for n, c in enumerate(came):
            extras[n].append(c)
    came = yield [swap(product(0, core, extras[0], 1 - near), "rep", 1)]
    total = product(0, core, [*extras[0], came[0]], near)
    if direct:
        others = merge_order()[1:]
        total = total.reshape(replicas // 2, rows, width)
        came = yield [swap(take(total, rest ^ k, 0), "rep", 2 * k) for k in others]
        total = add(take(total, rest, 0), *came)
        came = yield [swap(total, "rep", 2 * k) for k in others]
        mine = jnp.concatenate([total, *came], 0)
        came = yield [swap(mine, "rep", 1)]
        return mine, came[0]
    mask = 1
    while mask < replicas // 2:
        flag = (rest // mask) % 2
        total = total.reshape(-1, 2, rows, width)
        came = yield [swap(take(total, 1 - flag, 1), "rep", 2 * mask)]
        total = add(take(total, flag, 1), came[0])
        mask *= 2
    mine = total.reshape(rows, width)
    while mask > 1:
        mask //= 2
        came = yield [swap(mine, "rep", 2 * mask)]
        mine = jnp.concatenate([mine, came[0]], 0)
    came = yield [swap(mine, "rep", 1)]
    return mine, came[0]


def merge_order():
    order = [0]
    mask = lax.axis_size("rep") // 2
    while mask > 1:
        mask //= 2
        order = order + [k ^ mask for k in order]
    return order


def piece_places():
    replica = lax.axis_index("rep")
    near, rest = replica & 1, replica >> 1
    order = merge_order()
    places = [(near ^ side) * len(order) + (rest ^ k) for side in range(2) for k in order]
    return jnp.stack(places).astype(jnp.int32)


def butterfly_stream(total):
    for axis in ("shard", "rep"):
        mask = 1
        while mask < lax.axis_size(axis):
            came = yield [swap(total, axis, mask)]
            total = total + came[0]
            mask *= 2
    return total


def small_stream(flat):
    held = flat[None]
    mask = 1
    shard = lax.axis_index("shard")
    while mask < lax.axis_size("shard"):
        came = yield [swap(held, "shard", mask)]
        flag = (shard & mask) == 0
        held = jnp.concatenate([jnp.where(flag, held, came[0]), jnp.where(flag, came[0], held)], 0)
        mask *= 2
    return held


def unpack_small(every, shapes, dims):
    parts = every.shape[0]
    outputs = []
    offset = 0
    for shape, dim in zip(shapes, dims):
        length = math.prod(shape)
        block = every[:, offset : offset + length].reshape((parts,) + shape)
        offset += length
        if dim == 0:
            outputs.append(block.reshape((-1,) + shape[1:]))
        else:
            outputs.append(jnp.swapaxes(block, 0, 1).reshape(shape[0], -1))
    return outputs


def own_block(values, dim):
    size = values.shape[dim] // lax.axis_size("shard")
    return lax.dynamic_slice_in_dim(values, lax.axis_index("shard") * size, size, dim)


def group_tables(lengths, order, input_rows, device):
    count = lengths.shape[0]
    slots = jnp.arange(count, dtype=jnp.int32)
    starts = jnp.cumsum(lengths) - lengths
    pick = (order[:, None] == slots[None, :]).astype(jnp.int32)
    owner_len = jnp.sum(pick * lengths[None, :], 1)
    owner_start = jnp.cumsum(owner_len) - owner_len
    owner_src = jnp.sum(pick * starts[None, :], 1)
    first_len = jnp.sum(jnp.where(slots == 2 * device, owner_len, 0))
    first_src = jnp.sum(jnp.where(slots == 2 * device, owner_src, 0))
    second_src = jnp.sum(jnp.where(slots == 2 * device + 1, owner_src, 0))
    local = jnp.arange(input_rows, dtype=jnp.int32)
    segment = (local >= first_len).astype(jnp.int32)
    position = local - segment * first_len
    source = jnp.where(segment > 0, second_src, first_src) + position
    given = device * input_rows + local
    seq_id = jnp.sum((starts[None, :] <= given[:, None]).astype(jnp.int32), 1) - 1
    member = (seq_id[:, None] == slots[None, :]).astype(jnp.int32)
    seq_start = jnp.sum(member * starts[None, :], 1)
    seq_owner_start = jnp.sum(pick * owner_start[:, None], 0)
    target = jnp.sum(member * seq_owner_start[None, :], 1) + given - seq_start
    return (source, position, first_len.reshape(1), target)


def rms_scale(values):
    return lax.rsqrt(jnp.mean(values * values, axis=-1, keepdims=True) + EPS)


def rms_norm(values, gain):
    return values * rms_scale(values) * gain


def rope_tables(position):
    half = HEAD_SIZE // 2
    lane = jnp.arange(SIDE, dtype=jnp.int32)
    ladder = (lane % half).astype(jnp.float32) * (2.0 / HEAD_SIZE)
    angles = position.astype(jnp.float32)[:, None] * jnp.exp(-math.log(ROPE_BASE) * ladder)
    sign = jnp.where(lane % HEAD_SIZE < half, -1.0, 1.0)
    return jnp.cos(angles), jnp.sin(angles) * sign


def gated_norm(ssm_y, gate_z, gain):
    gated = ssm_y * jax.nn.silu(gate_z)
    return gated * rms_scale(gated) * gain


def swiglu(gate_up):
    half = gate_up.shape[1] // 2
    return jax.nn.silu(gate_up[:, :half]) * gate_up[:, half:]


def dot(left, right):
    return jnp.dot(left, right, preferred_element_type=jnp.float32)


def running_sum(values, reverse):
    count = values.shape[0]
    i = lax.broadcasted_iota(jnp.int32, (count, count), 0)
    j = lax.broadcasted_iota(jnp.int32, (count, count), 1)
    chosen = ((i <= j) if reverse else (j <= i)).astype(jnp.float32)
    return jnp.dot(chosen, values, precision=lax.Precision.HIGHEST)


def to_lanes(values, fill):
    count, width = values.shape
    return jnp.concatenate([values, jnp.full((count, SIDE - width), fill, values.dtype)], 1)


def on_device(
    tokens,
    seq_lengths,
    owner_order,
    gain_attn,
    w_input,
    w_step,
    step_bias,
    decay_log,
    skip_scale,
    conv_weight,
    conv_bias,
    gain_ssm,
    w_output,
    gain_ffn,
    w_gate_up,
    w_down,
    cotangent,
):
    input_rows = tokens.shape[0]
    shard = lax.axis_index("shard")
    flow = Flow()
    f32 = lambda v: v.astype(jnp.float32)

    slot_input = flow.add(weight_stream(w_input))
    small_args = (gain_attn, w_step, step_bias, decay_log, skip_scale, conv_weight, conv_bias, gain_ssm, gain_ffn)
    small_dims = (0, 0, 0, 0, 0, 1, 0, 0, 0)
    slot_small = flow.add(small_stream(jnp.concatenate([a.reshape(-1) for a in small_args])))
    source, position, limit, target = group_tables(seq_lengths[0], owner_order[0], input_rows, shard)
    cosine, sine = rope_tables(position)
    source, position, tokens, cosine, sine = flow.step((source, position, tokens, cosine, sine))
    slot_tokens = flow.add(rows_stream(tokens))
    source, position, w_output, w_gate_up, w_down, cotangent = flow.step(
        (source, position, w_output, w_gate_up, w_down, cotangent)
    )
    w_output_all = lax.all_gather(w_output, "shard", axis=0, tiled=True)
    w_gate_up_all = lax.all_gather(w_gate_up, "shard", axis=0, tiled=True)
    source, position, w_down, cotangent = flow.until(
        [slot_tokens, slot_input, slot_small], (source, position, w_down, cotangent)
    )
    w_down_all = lax.all_gather(w_down, "shard", axis=0, tiled=True)
    slot_cot = flow.add(rows_stream(cotangent))

    gain_attn_all, w_step_all, step_bias_all, decay_all, skip_all, conv_w_all, conv_b_all, gain_ssm_all, gain_ffn_all = (
        unpack_small(slot_small["result"], [a.shape for a in small_args], small_dims)
    )
    gain_attn_f, gain_ssm_f, gain_ffn_f = f32(gain_attn_all), f32(gain_ssm_all), f32(gain_ffn_all)
    conv_w_f, conv_b_f = f32(conv_w_all), f32(conv_b_all)
    skip_lanes = jnp.repeat(f32(skip_all), SSM_HD)[None]
    pieces, owners = slot_tokens["result"]
    own = f32(pick_rows(pieces, owners * input_rows, source))
    w_input_all = slot_input["result"]

    normed = rms_norm(own, gain_attn_f).astype(jnp.bfloat16)
    projected = dot(normed, w_input_all)
    projected, normed = flow.step((projected, normed))
    step_pre = dot(normed, w_step_all) + f32(step_bias_all)
    step = jax.nn.softplus(step_pre)
    rate = -jnp.exp(f32(decay_all))
    cum = to_lanes(running_sum(step * rate, False), 0.0)
    tables = (cum, cum.T)
    step_lanes = to_lanes(step, 1.0)
    conv_out, low = conv_forward(projected, position, conv_w_f, conv_b_f, step_lanes)
    inner_x = conv_out[:, :INNER]
    ssd_out = ssd_forward(limit, low, tables)
    attn_out, logs = attention_forward(limit, projected, cosine, sine)
    gate_z = projected[:, QUERY_KEY_VALUE : QUERY_KEY_VALUE + INNER]
    ssm_y = ssd_out + skip_lanes * inner_x
    ssm_out = gated_norm(ssm_y, gate_z, gain_ssm_f).astype(jnp.bfloat16)
    joined = jnp.concatenate([attn_out, ssm_out], 1)
    middle = own + dot(joined, w_output_all)
    normed_ffn = rms_norm(middle, gain_ffn_f).astype(jnp.bfloat16)
    gate_up = dot(normed_ffn, w_gate_up_all)
    hidden = swiglu(gate_up).astype(jnp.bfloat16)
    gate_up, hidden = flow.until([slot_cot], (gate_up, hidden))
    pieces, owners = slot_cot["result"]
    cot = pick_rows(pieces, owners * input_rows, source)

    def back(left, weight):
        return lax.dot_general(left, weight, (((1,), (1,)), ((), ())), preferred_element_type=jnp.float32)

    slots = {}
    block_low = (middle + dot(hidden, w_down_all)).astype(jnp.bfloat16)
    slots["down"] = [flow.add(reduce_stream(hidden, cot))]
    grad_hidden = back(cot, w_down_all)
    grad_gate_up = jax.vjp(swiglu, gate_up)[1](grad_hidden)[0].astype(jnp.bfloat16)
    grad_gate_up = flow.step(grad_gate_up)
    half = grad_gate_up.shape[1] // 2
    slots["gate_up"] = [flow.add(reduce_stream(normed_ffn, grad_gate_up[:, :half]))]
    grad_normed_ffn = back(grad_gate_up, w_gate_up_all)
    grad_middle_norm, grad_gain_ffn = jax.vjp(rms_norm, middle, gain_ffn_f)[1](grad_normed_ffn)
    grad_middle = f32(cot) + grad_middle_norm
    grad_middle, grad_gate_up = flow.step((grad_middle, grad_gate_up))
    slots["gate_up"].append(flow.add(reduce_stream(normed_ffn, grad_gate_up[:, half:])))
    middle_low = grad_middle.astype(jnp.bfloat16)
    grad_joined = back(middle_low, w_output_all)
    grad_attn = grad_joined[:, : QUERY_HEADS * HEAD_SIZE].astype(jnp.bfloat16)
    grad_ssm_out = grad_joined[:, QUERY_HEADS * HEAD_SIZE :]
    grad_ssm_y, grad_z, grad_gain_ssm = jax.vjp(gated_norm, ssm_y, gate_z, gain_ssm_f)[1](grad_ssm_out)
    grad_z_low = grad_z.astype(jnp.bfloat16)
    grad_y_low = grad_ssm_y.astype(jnp.bfloat16)
    grad_ssm_y, grad_z_low, grad_attn, middle_low, grad_y_low = flow.step(
        (grad_ssm_y, grad_z_low, grad_attn, middle_low, grad_y_low)
    )
    block_all = lax.all_gather(block_low, "shard", axis=0, tiled=True)
    slots["output"] = [flow.add(reduce_stream(joined, middle_low))]
    grad_q, grad_kv = attention_backward(limit, projected, cosine, sine, grad_attn, logs)
    grad_q, grad_kv, grad_y_low, grad_z_low = flow.step((grad_q, grad_kv, grad_y_low, grad_z_low))
    qkvz = jnp.concatenate([grad_q, grad_kv, grad_z_low], 1)
    slots["input"] = [flow.add(reduce_stream(normed, qkvz))]
    back_x, grad_bc = ssd_backward(limit, low, grad_y_low, tables)
    back_x, grad_bc = flow.step((back_x, grad_bc))
    grad_u_low, grad_taps, head_parts = conv_backward(
        projected, position, conv_w_f, conv_b_f, step_lanes, skip_lanes, back_x, grad_ssm_y, ssd_out, low, grad_bc
    )
    grad_u_low, head_parts = flow.step((grad_u_low, head_parts))
    slots["input"].append(flow.add(reduce_stream(normed, grad_u_low, True)))
    grad_projected = jnp.concatenate([qkvz, grad_u_low], 1)
    heads_of = lambda offset: head_parts[:, offset : offset + SSM_HEADS]
    grad_skip = jnp.sum(heads_of(64), 0)
    grad_inc = running_sum(heads_of(32), True)
    grad_step = heads_of(0) + grad_inc * rate
    grad_decay = jnp.sum(grad_inc * step, 0) * rate
    grad_step_pre = grad_step * jax.nn.sigmoid(step_pre)
    grad_step_bias = jnp.sum(grad_step_pre, 0)
    step_low = grad_step_pre.astype(jnp.bfloat16)
    grad_w_step = transposed_dot(normed, step_low)
    small_grads = (
        grad_w_step,
        grad_step_bias,
        grad_decay,
        grad_skip,
        grad_taps[:TAPS],
        grad_taps[TAPS],
        grad_gain_ssm,
        grad_gain_ffn,
    )
    grad_projected, step_low = flow.step((grad_projected, step_low))
    flat = jnp.concatenate([g.reshape(-1) for g in small_grads])
    flat = jnp.pad(flat, (0, -flat.shape[0] % 1024)).reshape(-1, SIDE)
    slot_flat = flow.add(butterfly_stream(flat))
    grad_normed = back(grad_projected, w_input_all) + back(step_low, w_step_all)
    grad_tokens_norm, grad_gain_attn = jax.vjp(rms_norm, own, gain_attn_f)[1](grad_normed)
    grad_low = (grad_middle + grad_tokens_norm).astype(jnp.bfloat16)
    places = piece_places()
    held = {}

    def finish_ready():
        for name in slots:
            if name not in held and all(slot["done"] for slot in slots[name]):
                held[name] = widen_rows([slot["result"] for slot in slots[name]], places)

    grad_low, gain_late = flow.step((grad_low, grad_gain_attn.reshape(-1, SIDE)))
    slot_grad = flow.add(rows_stream(grad_low))
    slot_late = flow.add(butterfly_stream(gain_late))
    finish_ready()
    held["block"] = pick_rows([block_all], jnp.zeros((1,), jnp.int32), target)
    held = flow.step(held, [slot for slot in flow.live if slot is not slot_grad])
    while flow.live:
        finish_ready()
        if slot_grad["done"] and "tokens" not in held:
            pieces, owners = slot_grad["result"]
            held["tokens"] = pick_rows(pieces, owners * input_rows, target)
        held = flow.step(held)
    finish_ready()
    block_out, grad_tokens, widened = held["block"], held["tokens"], held
    outs = [None] * 13
    outs[0] = own_block(slot_late["result"].reshape(-1), 0)
    summed = slot_flat["result"].reshape(-1)
    offset = 0
    for i, grad in zip((2, 3, 4, 5, 6, 7, 8, 10), small_grads):
        block = summed[offset : offset + grad.size].reshape(grad.shape)
        offset += grad.size
        outs[i] = own_block(block, 1 if i == 6 else 0)
    for i, name in ((1, "input"), (9, "output"), (11, "gate_up"), (12, "down")):
        outs[i] = widened[name]
    return (block_out, grad_tokens, *outs)


def solution(mesh):
    placed = (
        P(("rep", "shard"), None),
        P("rep", None),
        P("rep", None),
        P("shard"),
        P("shard", None),
        P("shard", None),
        P("shard"),
        P("shard"),
        P("shard"),
        P(None, "shard"),
        P("shard"),
        P("shard"),
        P("shard", None),
        P("shard"),
        P("shard", None),
        P("shard", None),
        P(("rep", "shard"), None),
    )
    return jax.shard_map(
        on_device,
        mesh=mesh,
        in_specs=placed,
        out_specs=(
            P(("rep", "shard"), None),
            P(("rep", "shard"), None),
            P("shard"),
            P("shard", None),
            P("shard", None),
            P("shard"),
            P("shard"),
            P("shard"),
            P(None, "shard"),
            P("shard"),
            P("shard"),
            P("shard", None),
            P("shard"),
            P("shard", None),
            P("shard", None),
        ),
        check_vma=False,
    )
```

```python
from functools import partial
import math

import jax
import jax.numpy as jnp
from jax import lax
from jax.experimental import pallas as pl
from jax.experimental.pallas import tpu as pltpu
from jax.sharding import PartitionSpec as P

QUERY_HEADS = 8
KEY_VALUE_HEADS = 2
HEAD_SIZE = 64
SSM_HEADS = 24
SSM_HD = 64
STATE = 128
INNER = 1536
QUERY_KEY_VALUE = 768
TAPS = 4

EPS = 1e-05
ROPE_BASE = 100000000000.0
SIDE = 128
QUAD = 4
LOW = -1e30
SCALE = HEAD_SIZE ** (-0.5)


def causal_bias(limit, rows, row0, cols):
    i = lax.broadcasted_iota(jnp.int32, (rows, cols), 0) + row0
    j = lax.broadcasted_iota(jnp.int32, (rows, cols), 1)
    seen = (j <= i) & ((j >= limit) | (i < limit))
    return jnp.where(seen, 0.0, LOW)


def contract_last(left, right):
    return lax.dot_general(left, right, (((1,), (1,)), ((), ())), preferred_element_type=jnp.float32)


def contract_first(left, right):
    return lax.dot_general(left, right, (((0,), (0,)), ((), ())), preferred_element_type=jnp.float32)


def halves(pair):
    lane = lax.broadcasted_iota(jnp.int32, pair.shape, 1)
    zero = jnp.zeros_like(pair)
    return (jnp.where(lane < HEAD_SIZE, pair, zero), jnp.where(lane >= HEAD_SIZE, pair, zero))


def four_lanes(values, step):
    return pltpu.roll(values, lax.rem(SIDE - QUAD * step, SIDE), 1)


def ssd_forward_kernel(limit_ref, c_ref, b_ref, x_ref, cum_col_ref, cum_row_ref, out_ref, inter, bias):
    count = c_ref.shape[0]

    @pl.when(pl.program_id(0) == 0)
    def _():
        inter[...] = contract_last(c_ref[...], b_ref[...])
        bias[...] = causal_bias(limit_ref[0], count, 0, count)

    step = pl.program_id(0)
    cum_col = four_lanes(cum_col_ref[...], step)
    cum_row = cum_row_ref[pl.ds(pl.multiple_of(step // 2 * 8, 8), 8), :]
    cum_row = jnp.where(step % 2 == 0, cum_row[:QUAD], cum_row[QUAD:])
    for pair in range(QUAD // 2):
        lanes = slice(pair * SIDE, (pair + 1) * SIDE)
        sides = halves(x_ref[:, lanes])
        for top in range(0, count, SIDE):
            rows = slice(top, top + SIDE)
            seen = top + SIDE
            total = None
            for half in range(2):
                h = pair * 2 + half
                gap = cum_col[rows, h : h + 1] - cum_row[h : h + 1, :seen]
                mixer = (inter[rows, :seen] * jnp.exp(gap + bias[rows, :seen])).astype(jnp.bfloat16)
                part = jnp.dot(mixer, sides[half][:seen], preferred_element_type=jnp.float32)
                total = part if total is None else total + part
            out_ref[rows, lanes] = total


def ssd_forward(limit, low, tables):
    count = low.shape[0]
    steps = SSM_HEADS // QUAD
    b_spec = pl.BlockSpec((count, STATE), lambda i: (0, INNER // STATE))
    c_spec = pl.BlockSpec((count, STATE), lambda i: (0, INNER // STATE + 1))
    return pl.pallas_call(
        ssd_forward_kernel,
        grid=(steps,),
        out_shape=jax.ShapeDtypeStruct((count, INNER), jnp.float32),
        in_specs=[
            pl.BlockSpec(memory_space=pltpu.SMEM),
            c_spec,
            b_spec,
            pl.BlockSpec((count, QUAD * HEAD_SIZE), lambda i: (0, i)),
            pl.BlockSpec((count, SIDE), lambda i: (0, 0)),
            pl.BlockSpec((SIDE, count), lambda i: (0, 0)),
        ],
        out_specs=pl.BlockSpec((count, QUAD * HEAD_SIZE), lambda i: (0, i)),
        scratch_shapes=[pltpu.VMEM((count, count), jnp.float32)] * 2,
        name="ssd_forward",
    )(limit, low, low, low, *tables)


def ssd_backward_kernel(part, limit_ref, c_ref, b_ref, x_ref, dy_ref, cum_col_ref, cum_row_ref, *refs):
    if part == 0:
        z_ref, total, inter, bias = refs
    else:
        held_ref, z_ref, total, gbc_ref, inter, bias = refs
    count = c_ref.shape[0]

    @pl.when(pl.program_id(0) == 0)
    def _():
        inter[...] = contract_last(c_ref[...], b_ref[...])
        bias[...] = causal_bias(limit_ref[0], count, 0, count)
        total[...] = jnp.zeros_like(total) if part == 0 else held_ref[...]

    step = pl.program_id(0) + part * (SSM_HEADS // QUAD // 2)
    cum_col = four_lanes(cum_col_ref[...], step)
    cum_row = cum_row_ref[pl.ds(pl.multiple_of(step // 2 * 8, 8), 8), :]
    cum_row = jnp.where(step % 2 == 0, cum_row[:QUAD], cum_row[QUAD:])
    for pair in range(QUAD // 2):
        lanes = slice(pair * SIDE, (pair + 1) * SIDE)
        x_pair = x_ref[:, lanes]
        sides = halves(dy_ref[:, lanes])
        for top in reversed(range(0, count, SIDE)):
            rows = slice(top, top + SIDE)
            seen = top + SIDE
            grad = None
            back = None
            for half in range(2):
                h = pair * 2 + half
                gap = cum_col[rows, h : h + 1] - cum_row[h : h + 1, :seen]
                decay = jnp.exp(gap + bias[rows, :seen])
                mixer = (inter[rows, :seen] * decay).astype(jnp.bfloat16)
                grad_mixer = contract_last(sides[half][rows], x_pair[:seen])
                piece = grad_mixer * decay
                grad = piece if grad is None else grad + piece
                piece = contract_first(mixer, sides[half][rows])
                back = piece if back is None else back + piece
            total[rows, :seen] += grad
            if seen == count:
                z_ref[:, lanes] = back
            else:
                z_ref[:seen, lanes] += back

    if part == 1:

        @pl.when(pl.program_id(0) == pl.num_programs(0) - 1)
        def _():
            low = total[...].astype(jnp.bfloat16)
            gbc_ref[:, :STATE] = contract_first(low, c_ref[...])
            gbc_ref[:, STATE:] = jnp.dot(low, b_ref[...], preferred_element_type=jnp.float32)


def ssd_backward(part, limit, low, grad_y, tables, held=None):
    count = low.shape[0]
    steps = SSM_HEADS // QUAD // 2
    b_spec = pl.BlockSpec((count, STATE), lambda i: (0, INNER // STATE))
    c_spec = pl.BlockSpec((count, STATE), lambda i: (0, INNER // STATE + 1))
    quad = pl.BlockSpec((count, QUAD * HEAD_SIZE), lambda i: (0, i + part * steps))
    square = pl.BlockSpec((count, count), lambda i: (0, 0))
    out_shape = [
        jax.ShapeDtypeStruct((count, INNER // 2), jnp.float32),
        jax.ShapeDtypeStruct((count, count), jnp.float32),
    ]
    out_specs = [pl.BlockSpec((count, QUAD * HEAD_SIZE), lambda i: (0, i)), square]
    if part == 1:
        out_shape.append(jax.ShapeDtypeStruct((count, 2 * STATE), jnp.float32))
        out_specs.append(pl.BlockSpec((count, 2 * STATE), lambda i: (0, 0)))
    more = [] if held is None else [held]
    return pl.pallas_call(
        partial(ssd_backward_kernel, part),
        grid=(steps,),
        out_shape=tuple(out_shape),
        in_specs=[
            pl.BlockSpec(memory_space=pltpu.SMEM),
            c_spec,
            b_spec,
            quad,
            quad,
            pl.BlockSpec((count, SIDE), lambda i: (0, 0)),
            pl.BlockSpec((SIDE, count), lambda i: (0, 0)),
        ]
        + [square] * len(more),
        out_specs=tuple(out_specs),
        scratch_shapes=[pltpu.VMEM((count, count), jnp.float32)] * 2,
        name="ssd_backward",
    )(limit, low, low, low, grad_y, *tables, *more)


def turn(values, cosine, sine):
    lane = lax.broadcasted_iota(jnp.int32, values.shape, 1) % HEAD_SIZE
    width = values.shape[1]
    ahead = pltpu.roll(values, width - HEAD_SIZE // 2, 1)
    behind = pltpu.roll(values, HEAD_SIZE // 2, 1)
    other = jnp.where(lane < HEAD_SIZE // 2, ahead, behind)
    return values * cosine + other * sine


def both_sides(pair, step):
    lane = lax.broadcasted_iota(jnp.int32, pair.shape, 1)
    mine = jnp.where((lane >= HEAD_SIZE) == (step > 0), pair, jnp.zeros_like(pair))
    return (mine + pltpu.roll(mine, HEAD_SIZE, 1)).astype(jnp.bfloat16)


def attention_forward_kernel(limit_ref, q_ref, k_ref, v_ref, cos_ref, sin_ref, out_ref, log_ref, bias):
    count = k_ref.shape[0]
    step = pl.program_id(0)

    @pl.when(step == 0)
    def _():
        bias[...] = causal_bias(limit_ref[0], count, 0, count)

    cosine, sine = cos_ref[...], sin_ref[...]
    key = both_sides(turn(k_ref[...], cosine, sine), step)
    value_sides = halves(both_sides(v_ref[...], step))
    for pair in range(2):
        lanes = slice(pair * SIDE, (pair + 1) * SIDE)
        sides = halves(turn(q_ref[:, lanes], cosine, sine).astype(jnp.bfloat16) * SCALE)
        for top in range(0, count, SIDE):
            rows = slice(top, top + SIDE)
            seen = top + SIDE
            total = None
            for half in range(2):
                score = contract_last(sides[half][rows], key[:seen]) + bias[rows, :seen]
                largest = jnp.max(score, -1, keepdims=True)
                raised = jnp.exp(score - largest)
                mass = jnp.sum(raised, -1, keepdims=True)
                weights = (raised * (1.0 / mass)).astype(jnp.bfloat16)
                part = jnp.dot(weights, value_sides[half][:seen], preferred_element_type=jnp.float32)
                total = part if total is None else total + part
                h = pair * 2 + half
                log_ref[0, rows, h : h + 1] = largest + jnp.log(mass)
            out_ref[rows, lanes] = total.astype(jnp.bfloat16)


def attention_specs(count):
    wide = pl.BlockSpec((count, 2 * SIDE), lambda i: (0, i))
    whole = pl.BlockSpec((count, SIDE), lambda i: (0, 0))
    keys = pl.BlockSpec((count, SIDE), lambda i: (0, QUERY_HEADS * HEAD_SIZE // SIDE))
    values = pl.BlockSpec((count, SIDE), lambda i: (0, QUERY_HEADS * HEAD_SIZE // SIDE + 1))
    logs = pl.BlockSpec((1, count, QUAD), lambda i: (i, 0, 0))
    return wide, whole, keys, values, logs


def attention_forward(limit, projected, cosine, sine):
    count = projected.shape[0]
    wide, whole, keys, values, logs = attention_specs(count)
    return pl.pallas_call(
        attention_forward_kernel,
        grid=(KEY_VALUE_HEADS,),
        out_shape=(
            jax.ShapeDtypeStruct((count, QUERY_HEADS * HEAD_SIZE), jnp.bfloat16),
            jax.ShapeDtypeStruct((KEY_VALUE_HEADS, count, QUAD), jnp.float32),
        ),
        in_specs=[pl.BlockSpec(memory_space=pltpu.SMEM), wide, keys, values, whole, whole],
        out_specs=(wide, logs),
        scratch_shapes=[pltpu.VMEM((count, count), jnp.float32)],
        name="attention_forward",
    )(limit, projected, projected, projected, cosine, sine)


def attention_backward_kernel(step, limit_ref, q_ref, k_ref, v_ref, cos_ref, sin_ref, go_ref, log_ref, *refs):
    (gq_ref, gkv_ref), (bias, gk, gv) = refs[-5:-3], refs[-3:]
    count = k_ref.shape[0]
    bias[...] = causal_bias(limit_ref[0], count, 0, count)
    cosine, sine = cos_ref[...], sin_ref[...]
    key = both_sides(turn(k_ref[...], cosine, sine), step)
    value = both_sides(v_ref[...], step)
    key_sides = halves(key)
    gk[...] = jnp.zeros_like(gk)
    gv[...] = jnp.zeros_like(gv)
    for pair in range(2):
        lanes = slice(pair * SIDE, (pair + 1) * SIDE)
        q_sides = halves(turn(q_ref[:, lanes], cosine, sine).astype(jnp.bfloat16) * SCALE)
        go_sides = halves(go_ref[:, lanes])
        for top in range(0, count, SIDE):
            rows = slice(top, top + SIDE)
            seen = top + SIDE
            total = None
            for half in range(2):
                h = pair * 2 + half
                score = contract_last(q_sides[half][rows], key[:seen])
                weights = jnp.exp(score + bias[rows, :seen] - log_ref[0, rows, h : h + 1])
                grad = contract_last(go_sides[half][rows], value[:seen])
                inner = jnp.sum(grad * weights, -1, keepdims=True)
                low = (weights * (grad - inner)).astype(jnp.bfloat16)
                part = jnp.dot(low, key_sides[half][:seen], preferred_element_type=jnp.float32)
                total = part if total is None else total + part
                gk[:seen, :] += contract_first(low, q_sides[half][rows])
                gv[:seen, :] += contract_first(weights.astype(jnp.bfloat16), go_sides[half][rows])
            gq_ref[rows, lanes] = turn(total * SCALE, cosine[rows], -sine[rows]).astype(jnp.bfloat16)
    lane = lax.broadcasted_iota(jnp.int32, (count, SIDE), 1)
    mine = (lane >= HEAD_SIZE) == (step > 0)
    for place, part in enumerate((gk, gv)):
        summed = part[...] + pltpu.roll(part[...], HEAD_SIZE, 1)
        if place == 0:
            summed = turn(summed, cosine, -sine)
        lanes = slice(place * SIDE, (place + 1) * SIDE)
        if step > 0:
            summed = jnp.where(mine, summed, refs[0][:, lanes].astype(jnp.float32))
        gkv_ref[:, lanes] = summed.astype(jnp.bfloat16)


def attention_backward(step, limit, projected, cosine, sine, grad_out, logs_in, other=None):
    count = projected.shape[0]
    _, whole, keys, values, _ = attention_specs(count)
    at = lambda spec: pl.BlockSpec(spec.block_shape, lambda i: spec.index_map(step))
    wide, _, _, _, logs = attention_specs(count)
    both = pl.BlockSpec((count, 2 * SIDE), lambda i: (0, 0))
    more = [] if other is None else [other]
    return pl.pallas_call(
        partial(attention_backward_kernel, step),
        grid=(1,),
        out_shape=(
            jax.ShapeDtypeStruct((count, 2 * SIDE), jnp.bfloat16),
            jax.ShapeDtypeStruct((count, 2 * SIDE), jnp.bfloat16),
        ),
        in_specs=[pl.BlockSpec(memory_space=pltpu.SMEM), at(wide), keys, values, whole, whole, at(wide), at(logs)]
        + [both] * len(more),
        out_specs=(both, both),
        scratch_shapes=[
            pltpu.VMEM((count, count), jnp.float32),
            pltpu.VMEM((count, SIDE), jnp.float32),
            pltpu.VMEM((count, SIDE), jnp.float32),
        ],
        name="attention_backward",
    )(limit, projected, projected, projected, cosine, sine, grad_out, logs_in, *more)


BLOCK = QUAD * HEAD_SIZE


TILE = 128
HALO = 8


def conv_taps(u_ref, top, place, weight_ref, bias_ref, lanes):
    mixed = bias_ref[:, lanes] + u_ref[HALO + top : HALO + top + TILE, lanes] * weight_ref[TAPS - 1 : TAPS, lanes]
    for back in range(1, TAPS):
        shifted = u_ref[HALO + top - back : HALO + top - back + TILE, lanes]
        mixed = mixed + jnp.where(place >= back, shifted, 0.0) * weight_ref[TAPS - 1 - back : TAPS - back, lanes]
    return mixed


def conv_forward_kernel(u_ref, place_ref, weight_ref, bias_ref, step_ref, out_ref, low_ref, held):
    count = u_ref.shape[0]
    held[:HALO, :] = jnp.zeros((HALO, BLOCK), jnp.float32)
    held[HALO:, :] = u_ref[...]
    lane = lax.broadcasted_iota(jnp.int32, (TILE, SIDE), 1)
    scale = four_lanes(step_ref[...], pl.program_id(0))
    for side in range(BLOCK // SIDE):
        lanes = slice(side * SIDE, (side + 1) * SIDE)
        for top in range(0, count, TILE):
            rows = slice(top, top + TILE)
            mixed = conv_taps(held, top, place_ref[rows], weight_ref, bias_ref, lanes)
            out = mixed / (1.0 + jnp.exp(-mixed))
            out_ref[rows, lanes] = out
            first, second = scale[rows, 2 * side : 2 * side + 1], scale[rows, 2 * side + 1 : 2 * side + 2]
            low_ref[rows, lanes] = (out * jnp.where(lane < HEAD_SIZE, first, second)).astype(jnp.bfloat16)


def conv_specs(count, begin=0):
    column = lambda i: (0, i + begin)
    first = (QUERY_KEY_VALUE + INNER) // BLOCK + begin
    return (
        pl.BlockSpec((count, BLOCK), lambda i: (0, first + i)),
        pl.BlockSpec((count, 1), lambda i: (0, 0)),
        pl.BlockSpec((TAPS, BLOCK), column),
        pl.BlockSpec((1, BLOCK), column),
        pl.BlockSpec((count, SIDE), lambda i: (0, 0)),
        pl.BlockSpec((count, BLOCK), column),
    )


def conv_forward(projected, position, weight, bias, step_quads):
    count, width = projected.shape[0], weight.shape[1]
    u, place, taps, row, quads, block = conv_specs(count)
    return pl.pallas_call(
        conv_forward_kernel,
        grid=(width // BLOCK,),
        out_shape=(
            jax.ShapeDtypeStruct((count, width), jnp.float32),
            jax.ShapeDtypeStruct((count, width), jnp.bfloat16),
        ),
        in_specs=[u, place, taps, row, quads],
        out_specs=(block, block),
        scratch_shapes=[pltpu.VMEM((HALO + count, BLOCK), jnp.float32)],
        name="conv_forward",
    )(projected, position[:, None], weight, bias[None], step_quads)


def head_sums(values, chosen):
    high = values.astype(jnp.bfloat16)
    rest = values - high.astype(jnp.float32)
    middle = rest.astype(jnp.bfloat16)
    low = (rest - middle.astype(jnp.float32)).astype(jnp.bfloat16)
    total = jnp.dot(high, chosen, preferred_element_type=jnp.float32)
    total = total + jnp.dot(middle, chosen, preferred_element_type=jnp.float32)
    return total + jnp.dot(low, chosen, preferred_element_type=jnp.float32)


def conv_backward_kernel(
    first, u_ref, place_ref, weight_ref, bias_ref, step_ref, skip_ref, z_ref, gy_ref, y_ref, low_ref, gbc_ref,
    gu_ref, gw_ref, heads_ref, held, grads,
):
    count = u_ref.shape[0]
    step = pl.program_id(0) + first
    inner = step < INNER // BLOCK
    scale = four_lanes(step_ref[...], step)
    held[:HALO, :] = jnp.zeros((HALO, BLOCK), jnp.float32)
    held[HALO:, :] = u_ref[...]
    lane = lax.broadcasted_iota(jnp.int32, (TILE, SIDE), 1)

    @pl.when(pl.program_id(0) == 0)
    def _():
        heads_ref[...] = jnp.zeros_like(heads_ref)

    for side in range(BLOCK // SIDE):
        lanes = slice(side * SIDE, (side + 1) * SIDE)
        sums = [None] * (TAPS + 1)
        head = lax.broadcasted_iota(jnp.int32, (SIDE, SIDE), 0) // HEAD_SIZE + 2 * side + QUAD * step
        column = lax.broadcasted_iota(jnp.int32, (SIDE, SIDE), 1)
        chosen = [(head + offset == column).astype(jnp.bfloat16) for offset in (0, 32, 64)]
        for back in range(1, TAPS):
            grads[back - 1, count:, lanes] = jnp.zeros((HALO, SIDE), jnp.float32)
        for top in range(0, count, TILE):
            rows = slice(top, top + TILE)
            place = place_ref[rows]
            mixed = conv_taps(held, top, place, weight_ref, bias_ref, lanes)
            gate = 1.0 / (1.0 + jnp.exp(-mixed))
            out = mixed * gate
            z, gy = z_ref[rows, lanes], gy_ref[rows, lanes]
            first, second = scale[rows, 2 * side : 2 * side + 1], scale[rows, 2 * side + 1 : 2 * side + 2]
            grad = z * jnp.where(lane < HEAD_SIZE, first, second) + skip_ref[:, lanes] * gy
            grad = jnp.where(inner, grad, gbc_ref[rows, lanes])
            gy_low = gy.astype(jnp.bfloat16).astype(jnp.float32)
            cum = gy_low * y_ref[rows, lanes] - low_ref[rows, lanes].astype(jnp.float32) * z
            part = head_sums(z * out, chosen[0]) + head_sums(cum, chosen[1]) + head_sums(gy * out, chosen[2])
            heads_ref[rows, :] += jnp.where(inner, part, 0.0)
            grad = grad * (gate + out * (1.0 - gate))
            parts = [jnp.sum(grad, 0, keepdims=True)]
            parts.append(jnp.sum(grad * held[HALO + top : HALO + top + TILE, lanes], 0, keepdims=True))
            grads[TAPS - 1, rows, lanes] = grad * weight_ref[TAPS - 1 : TAPS, lanes]
            for back in range(1, TAPS):
                seen = jnp.where(place >= back, grad, 0.0)
                shifted = held[HALO + top - back : HALO + top - back + TILE, lanes]
                parts.append(jnp.sum(seen * shifted, 0, keepdims=True))
                grads[back - 1, rows, lanes] = seen * weight_ref[TAPS - 1 - back : TAPS - back, lanes]
            sums = [p if s is None else s + p for s, p in zip(sums, parts)]
        gw_ref[:, lanes] = jnp.zeros((8, SIDE), jnp.float32)
        gw_ref[TAPS : TAPS + 1, lanes] = sums[0]
        for back in range(TAPS):
            gw_ref[TAPS - 1 - back : TAPS - back, lanes] = sums[1 + back]
        for top in range(0, count, TILE):
            total = grads[TAPS - 1, top : top + TILE, lanes]
            for back in range(1, TAPS):
                total = total + grads[back - 1, top + back : top + back + TILE, lanes]
            gu_ref[top : top + TILE, lanes] = total.astype(jnp.bfloat16)


def conv_backward(part, projected, position, weight, bias, step_lanes, skip, z, grad_y, y, low, grad_bc):
    count = projected.shape[0]
    cut = INNER // BLOCK // 2
    begin, blocks = (0, cut) if part == 0 else (cut, weight.shape[1] // BLOCK - cut)
    u, place, taps, row, lanes, block = conv_specs(count, begin)
    last = INNER // BLOCK - 1
    inner = pl.BlockSpec((count, BLOCK), lambda i: (0, jnp.minimum(i + begin, last)))
    half = pl.BlockSpec((count, BLOCK), lambda i: (0, jnp.minimum(i, cut - 1)))
    skip_row = pl.BlockSpec((1, BLOCK), lambda i: (0, jnp.minimum(i + begin, last)))
    return pl.pallas_call(
        partial(conv_backward_kernel, begin),
        grid=(blocks,),
        out_shape=(
            jax.ShapeDtypeStruct((count, blocks * BLOCK), jnp.bfloat16),
            jax.ShapeDtypeStruct((8, blocks * BLOCK), jnp.float32),
            jax.ShapeDtypeStruct((count, SIDE), jnp.float32),
        ),
        in_specs=[u, place, taps, row, lanes, skip_row, half, inner, inner, block, pl.BlockSpec((count, BLOCK), lambda i: (0, 0))],
        out_specs=(
            pl.BlockSpec((count, BLOCK), lambda i: (0, i)),
            pl.BlockSpec((8, BLOCK), lambda i: (0, i)),
            pl.BlockSpec((count, SIDE), lambda i: (0, 0)),
        ),
        scratch_shapes=[
            pltpu.VMEM((HALO + count, BLOCK), jnp.float32),
            pltpu.VMEM((TAPS, count + HALO, BLOCK), jnp.float32),
        ],
        name="conv_backward",
    )(projected, position[:, None], weight, bias[None], step_lanes, skip, z, grad_y, y, low, grad_bc)


def pick_kernel(shift_ref, wanted_ref, *refs):
    out_ref = refs[-1]
    pieces = refs[:-1]
    count = pieces[0].shape[0]
    place = lax.broadcasted_iota(jnp.int32, (out_ref.shape[0], count), 1)
    total = None
    for n, piece in enumerate(pieces):
        choice = (wanted_ref[...] - shift_ref[n] == place).astype(jnp.bfloat16)
        part = jnp.dot(choice, piece[...], preferred_element_type=jnp.float32)
        total = part if total is None else total + part
    out_ref[...] = total.astype(out_ref.dtype)


def pick_rows(pieces, shifts, wanted):
    vmem = pl.BlockSpec(memory_space=pltpu.VMEM)
    return pl.pallas_call(
        pick_kernel,
        out_shape=jax.ShapeDtypeStruct((wanted.shape[0], pieces[0].shape[1]), pieces[0].dtype),
        in_specs=[pl.BlockSpec(memory_space=pltpu.SMEM), vmem] + [vmem] * len(pieces),
        out_specs=vmem,
        name="pick_rows",
    )(shifts, wanted[:, None], *pieces)


def lay_rows_kernel(place_ref, *refs):
    sems = refs[-1]
    out_ref = refs[-2]
    pieces = refs[:-2]
    copies = []
    for n, piece in enumerate(pieces):
        rows = piece.shape[0]
        start = pl.multiple_of(place_ref[n] * 16, 16)
        copies.append(pltpu.make_async_copy(piece, out_ref.at[pl.ds(start, rows)], sems.at[n]))
    for copy in copies:
        copy.start()
    for copy in copies:
        copy.wait()


def lay_rows(pieces, places):
    rows = sum(piece.shape[0] for piece in pieces)
    hbm = pl.BlockSpec(memory_space=pl.ANY)
    return pl.pallas_call(
        lay_rows_kernel,
        out_shape=jax.ShapeDtypeStruct((rows, pieces[0].shape[1]), pieces[0].dtype),
        in_specs=[pl.BlockSpec(memory_space=pltpu.SMEM)] + [hbm] * len(pieces),
        out_specs=pl.BlockSpec(memory_space=pltpu.VMEM),
        scratch_shapes=[pltpu.SemaphoreType.DMA((len(pieces),))],
        name="lay_rows",
    )(places // 16, *pieces)


def widen_kernel(columns, near_ref, *refs):
    out_ref = refs[-1]
    for n, block in enumerate(refs[:-1]):
        rows, left = block.shape[0], columns[n // 2]
        start = pl.multiple_of((near_ref[0] ^ (n % 2)) * rows, rows)
        out_ref[pl.ds(start, rows), left : left + block.shape[1]] = block[...].astype(jnp.float32)


def widen_rows(chunks, near):
    flat = [block for chunk in chunks for block in chunk]
    columns, left = [], 0
    for chunk in chunks:
        columns.append(left)
        left += chunk[0].shape[1]
    rows = 2 * chunks[0][0].shape[0]
    vmem = pl.BlockSpec(memory_space=pltpu.VMEM)
    return pl.pallas_call(
        partial(widen_kernel, tuple(columns)),
        out_shape=jax.ShapeDtypeStruct((rows, left), jnp.float32),
        in_specs=[pl.BlockSpec(memory_space=pltpu.SMEM)] + [vmem] * len(flat),
        out_specs=vmem,
        name="widen_rows",
    )(near, *flat)


def swap(values, axis, mask):
    count = lax.axis_size(axis)
    return lax.ppermute(values, axis, [(i, i ^ mask) for i in range(count)])


def take(values, index, dim):
    return lax.dynamic_index_in_dim(values, index, dim, keepdims=False)


def add(first, *others):
    total = first.astype(jnp.float32)
    for other in others:
        total = total + other.astype(jnp.float32)
    return total.astype(jnp.bfloat16)


class Flow:
    def __init__(self):
        self.live = []

    def add(self, stream):
        slot = {"stream": stream, "sent": None, "left": 0, "result": None, "done": False}
        self.live.append(slot)
        self._advance(slot, None)
        return slot

    def _advance(self, slot, value):
        try:
            sent = slot["stream"].send(value)
            slot["sent"], slot["left"] = sent if isinstance(sent, tuple) else (sent, 1)
        except StopIteration as stop:
            slot["result"] = stop.value
            slot["sent"] = None
            slot["done"] = True
            self.live.remove(slot)

    def step(self, values=None, slots=None, force=False):
        slots = [slot for slot in (self.live if slots is None else slots) if not slot["done"]]
        for slot in slots:
            slot["left"] -= 1
        slots = [slot for slot in slots if slot["left"] <= 0 or force]
        values, sent = lax.optimization_barrier((values, [slot["sent"] for slot in slots]))
        for slot, came in zip(slots, sent):
            self._advance(slot, came)
        return values

    def until(self, slots, values=None, alone=False):
        while any(not slot["done"] for slot in slots):
            values = self.step(values, slots if alone else None)
        return values


def rows_stream(piece, wait=1):
    shard = lax.axis_index("shard")
    held = [(0, piece)]
    mask = lax.axis_size("shard") // 2
    first = True
    near = None
    while mask > 1:
        send = [swap(p, "shard", mask) for _, p in held]
        if first:
            send.append(swap(piece, "shard", 1))
        came = yield send, wait
        if first:
            near = came[-1]
            first = False
        held = held + [(k ^ mask, p) for (k, _), p in zip(held, came)]
        mask //= 2
    came = yield [swap(p, "shard", 1) for k, p in held[1:]]
    held = held + [(1, near)] + [(k ^ 1, p) for (k, _), p in zip(held[1:], came)]
    keys = [k for k, _ in held]
    return [p for _, p in held], jnp.stack([shard ^ k for k in keys]).astype(jnp.int32)


def weight_stream(piece):
    rows, width = piece.shape
    shard, near = lax.axis_index("shard"), lax.axis_index("rep") & 1
    part = lax.dynamic_slice_in_dim(piece, near * (rows // 2), rows // 2, 0)
    held = [(0, part)]
    both = []
    mask = lax.axis_size("shard") // 2
    beside = None
    while mask > 1:
        send = [swap(p, "shard", mask) for _, p in held]
        if beside is None:
            send.append(swap(piece, "shard", 1))
        came = yield send
        if beside is None:
            beside = came[-1]
        fresh = [(k ^ mask, p) for (k, _), p in zip(held, came)]
        passed = yield [swap(p, "rep", 1) for _, p in fresh] + [swap(p, "shard", 1) for _, p in fresh]
        count = len(fresh)
        for n, (k, p) in enumerate(fresh):
            both.append((k, 0, p))
            both.append((k ^ 1, 0, passed[count + n]))
            both.append((k, 1, passed[n]))
        held = held + fresh
        mask //= 2
    late = [(k, p) for k, side, p in both if side == 1]
    came = yield [swap(p, "shard", 1) for _, p in late]
    both = both + [(k ^ 1, 1, p) for (k, _), p in zip(late, came)]
    pieces = [piece, beside] + [p for _, _, p in both]
    places = [shard * rows, (shard ^ 1) * rows]
    places += [(shard ^ k) * rows + (near ^ side) * (rows // 2) for k, side, _ in both]
    return lay_rows(pieces, jnp.stack(places).astype(jnp.int32))


def transposed_dot(left, right):
    return lax.dot_general(left, right, (((0,), (0,)), ((), ())), preferred_element_type=jnp.float32)


def reduce_stream(left, right, waits=(1, 1, 1, 1)):
    shards, replicas = lax.axis_size("shard"), lax.axis_size("rep")
    block = left.shape[1] // shards
    shard, near = lax.axis_index("shard"), lax.axis_index("rep") & 1
    core, far = shard & 1, shard >> 1

    def product(r, c, extras=(), half=None):
        start, size = ((far ^ r) * 2 + c) * block, block
        if half is not None:
            size = block // 2
            start = start + half * size
            extras = [x if x.shape[0] == size else lax.dynamic_slice_in_dim(x, half * size, size, 0) for x in extras]
        total = transposed_dot(lax.dynamic_slice_in_dim(left, start, size, 1), right)
        for extra in extras:
            total = total + extra.astype(jnp.float32)
        return total.astype(jnp.bfloat16)

    count = shards // 2
    came = yield [swap(product(r, 1 - core), "shard", 1) for r in range(count)], waits[0]
    extras = [[c] for c in came]
    while count > 1:
        count //= 2
        came = yield [swap(product(r, core, extras[r]), "shard", 2 * count) for r in range(count, 2 * count)], waits[1]
        for n, c in enumerate(came):
            extras[n].append(c)
    came = yield [swap(product(0, core, extras[0], 1 - near), "rep", 1)], waits[2]
    total = product(0, core, [*extras[0], came[0]], near)
    mask = 2
    while mask < replicas:
        came = yield [swap(total, "rep", mask)], waits[3]
        total = add(total, came[0])
        mask *= 2
    came = yield [swap(total, "rep", 1)]
    return total, came[0]


def butterfly_stream(total):
    for axis in ("shard", "rep"):
        mask = 1
        while mask < lax.axis_size(axis):
            came = yield [swap(total, axis, mask)]
            total = total + came[0]
            mask *= 2
    return total


def small_stream(flat):
    held = flat[None]
    mask = 1
    shard = lax.axis_index("shard")
    while mask < lax.axis_size("shard"):
        came = yield [swap(held, "shard", mask)]
        flag = (shard & mask) == 0
        held = jnp.concatenate([jnp.where(flag, held, came[0]), jnp.where(flag, came[0], held)], 0)
        mask *= 2
    return held


def unpack_small(every, shapes, dims):
    parts = every.shape[0]
    outputs = []
    offset = 0
    for shape, dim in zip(shapes, dims):
        length = math.prod(shape)
        block = every[:, offset : offset + length].reshape((parts,) + shape)
        offset += length
        if dim == 0:
            outputs.append(block.reshape((-1,) + shape[1:]))
        else:
            outputs.append(jnp.swapaxes(block, 0, 1).reshape(shape[0], -1))
    return outputs


def own_block(values, dim):
    size = values.shape[dim] // lax.axis_size("shard")
    return lax.dynamic_slice_in_dim(values, lax.axis_index("shard") * size, size, dim)


def group_tables(lengths, order, input_rows, device):
    count = lengths.shape[0]
    slots = jnp.arange(count, dtype=jnp.int32)
    starts = jnp.cumsum(lengths) - lengths
    pick = (order[:, None] == slots[None, :]).astype(jnp.int32)
    owner_len = jnp.sum(pick * lengths[None, :], 1)
    owner_start = jnp.cumsum(owner_len) - owner_len
    owner_src = jnp.sum(pick * starts[None, :], 1)
    first_len = jnp.sum(jnp.where(slots == 2 * device, owner_len, 0))
    first_src = jnp.sum(jnp.where(slots == 2 * device, owner_src, 0))
    second_src = jnp.sum(jnp.where(slots == 2 * device + 1, owner_src, 0))
    local = jnp.arange(input_rows, dtype=jnp.int32)
    segment = (local >= first_len).astype(jnp.int32)
    position = local - segment * first_len
    source = jnp.where(segment > 0, second_src, first_src) + position
    given = device * input_rows + local
    seq_id = jnp.sum((starts[None, :] <= given[:, None]).astype(jnp.int32), 1) - 1
    member = (seq_id[:, None] == slots[None, :]).astype(jnp.int32)
    seq_start = jnp.sum(member * starts[None, :], 1)
    seq_owner_start = jnp.sum(pick * owner_start[:, None], 0)
    target = jnp.sum(member * seq_owner_start[None, :], 1) + given - seq_start
    return (source, position, first_len.reshape(1), target)


def rms_scale(values):
    return lax.rsqrt(jnp.mean(values * values, axis=-1, keepdims=True) + EPS)


def rms_norm(values, gain):
    return values * rms_scale(values) * gain


def rope_tables(position):
    half = HEAD_SIZE // 2
    lane = jnp.arange(SIDE, dtype=jnp.int32)
    ladder = (lane % half).astype(jnp.float32) * (2.0 / HEAD_SIZE)
    angles = position.astype(jnp.float32)[:, None] * jnp.exp(-math.log(ROPE_BASE) * ladder)
    sign = jnp.where(lane % HEAD_SIZE < half, -1.0, 1.0)
    return jnp.cos(angles), jnp.sin(angles) * sign


def gated_norm(ssm_y, gate_z, gain):
    gated = ssm_y * jax.nn.silu(gate_z)
    return gated * rms_scale(gated) * gain


def swiglu(gate_up):
    half = gate_up.shape[1] // 2
    return jax.nn.silu(gate_up[:, :half]) * gate_up[:, half:]


def dot(left, right):
    return jnp.dot(left, right, preferred_element_type=jnp.float32)


def running_sum(values, reverse):
    count = values.shape[0]
    i = lax.broadcasted_iota(jnp.int32, (count, count), 0)
    j = lax.broadcasted_iota(jnp.int32, (count, count), 1)
    chosen = ((i <= j) if reverse else (j <= i)).astype(jnp.float32)
    return jnp.dot(chosen, values, precision=lax.Precision.HIGHEST)


def to_lanes(values, fill):
    count, width = values.shape
    return jnp.concatenate([values, jnp.full((count, SIDE - width), fill, values.dtype)], 1)


WAITS = {
    "down": (1, 2, 1, 1),
    "gate": (1, 2, 1, 1),
    "up": (1, 2, 1, 1),
    "output": (1, 3, 1, 1),
    "qkvz": (1, 3, 1, 1),
}


def on_device(
    tokens,
    seq_lengths,
    owner_order,
    gain_attn,
    w_input,
    w_step,
    step_bias,
    decay_log,
    skip_scale,
    conv_weight,
    conv_bias,
    gain_ssm,
    w_output,
    gain_ffn,
    w_gate_up,
    w_down,
    cotangent,
):
    input_rows = tokens.shape[0]
    shard = lax.axis_index("shard")
    flow = Flow()
    f32 = lambda v: v.astype(jnp.float32)

    slot_input = flow.add(weight_stream(w_input))
    small_args = (gain_attn, w_step, step_bias, decay_log, skip_scale, conv_weight, conv_bias, gain_ssm, gain_ffn)
    small_dims = (0, 0, 0, 0, 0, 1, 0, 0, 0)
    slot_small = flow.add(small_stream(jnp.concatenate([a.reshape(-1) for a in small_args])))
    source, position, limit, target = group_tables(seq_lengths[0], owner_order[0], input_rows, shard)
    cosine, sine = rope_tables(position)
    source, position, tokens, cosine, sine, w_output = flow.step((source, position, tokens, cosine, sine, w_output))
    slot_tokens = flow.add(rows_stream(tokens))
    source, position, w_output, w_gate_up, w_down, cotangent = flow.step(
        (source, position, w_output, w_gate_up, w_down, cotangent)
    )
    w_output_all = lax.all_gather(w_output, "shard", axis=0, tiled=True)
    w_gate_up_all = lax.all_gather(w_gate_up, "shard", axis=0, tiled=True)
    w_down_all = lax.all_gather(w_down, "shard", axis=0, tiled=True)
    source, position, cotangent = flow.until([slot_tokens, slot_input, slot_small], (source, position, cotangent))

    gain_attn_all, w_step_all, step_bias_all, decay_all, skip_all, conv_w_all, conv_b_all, gain_ssm_all, gain_ffn_all = (
        unpack_small(slot_small["result"], [a.shape for a in small_args], small_dims)
    )
    gain_attn_f, gain_ssm_f, gain_ffn_f = f32(gain_attn_all), f32(gain_ssm_all), f32(gain_ffn_all)
    conv_w_f, conv_b_f = f32(conv_w_all), f32(conv_b_all)
    skip_lanes = jnp.repeat(f32(skip_all), SSM_HD)[None]
    pieces, owners = slot_tokens["result"]
    own = f32(pick_rows(pieces, owners * input_rows, source))
    w_input_all = slot_input["result"]

    normed = rms_norm(own, gain_attn_f).astype(jnp.bfloat16)
    projected = dot(normed, w_input_all)
    projected, normed, cotangent = lax.optimization_barrier((projected, normed, cotangent))
    slot_cot = flow.add(rows_stream(cotangent))
    step_pre = dot(normed, w_step_all) + f32(step_bias_all)
    step = jax.nn.softplus(step_pre)
    rate = -jnp.exp(f32(decay_all))
    cum = to_lanes(running_sum(step * rate, False), 0.0)
    tables = (cum, cum.T)
    step_lanes = to_lanes(step, 1.0)
    conv_out, low = conv_forward(projected, position, conv_w_f, conv_b_f, step_lanes)
    inner_x = conv_out[:, :INNER]
    ssd_out = ssd_forward(limit, low, tables)
    attn_out, logs = attention_forward(limit, projected, cosine, sine)
    gate_z = projected[:, QUERY_KEY_VALUE : QUERY_KEY_VALUE + INNER]
    ssm_y = ssd_out + skip_lanes * inner_x
    ssm_out = gated_norm(ssm_y, gate_z, gain_ssm_f).astype(jnp.bfloat16)
    joined = jnp.concatenate([attn_out, ssm_out], 1)
    middle = own + dot(joined, w_output_all)
    normed_ffn = rms_norm(middle, gain_ffn_f).astype(jnp.bfloat16)
    gate_up = dot(normed_ffn, w_gate_up_all)
    hidden = swiglu(gate_up).astype(jnp.bfloat16)
    gate_up, hidden = flow.until([slot_cot], (gate_up, hidden))
    pieces, owners = slot_cot["result"]
    cot = pick_rows(pieces, owners * input_rows, source)

    def back(left, weight):
        return lax.dot_general(left, weight, (((1,), (1,)), ((), ())), preferred_element_type=jnp.float32)

    slots = {}
    block_low = (middle + dot(hidden, w_down_all)).astype(jnp.bfloat16)
    slots["down"] = [flow.add(reduce_stream(hidden, cot, WAITS["down"]))]
    grad_hidden = back(cot, w_down_all)
    grad_gate_up = jax.vjp(swiglu, gate_up)[1](grad_hidden)[0].astype(jnp.bfloat16)
    grad_gate_up = flow.step(grad_gate_up)
    half = grad_gate_up.shape[1] // 2
    slots["gate_up"] = [flow.add(reduce_stream(normed_ffn, grad_gate_up[:, :half], WAITS["gate"]))]
    grad_normed_ffn = back(grad_gate_up, w_gate_up_all)
    grad_middle_norm, grad_gain_ffn = jax.vjp(rms_norm, middle, gain_ffn_f)[1](grad_normed_ffn)
    grad_middle = f32(cot) + grad_middle_norm
    grad_middle, grad_gate_up = flow.step((grad_middle, grad_gate_up))
    slots["gate_up"].append(flow.add(reduce_stream(normed_ffn, grad_gate_up[:, half:], WAITS["up"])))
    middle_low = grad_middle.astype(jnp.bfloat16)
    grad_joined = back(middle_low, w_output_all)
    grad_attn = grad_joined[:, : QUERY_HEADS * HEAD_SIZE].astype(jnp.bfloat16)
    grad_ssm_out = grad_joined[:, QUERY_HEADS * HEAD_SIZE :]
    grad_ssm_y, grad_z, grad_gain_ssm = jax.vjp(gated_norm, ssm_y, gate_z, gain_ssm_f)[1](grad_ssm_out)
    grad_z_low = grad_z.astype(jnp.bfloat16)
    grad_y_low = grad_ssm_y.astype(jnp.bfloat16)
    grad_ssm_y, grad_z_low, grad_attn, middle_low, grad_y_low, block_low = flow.step(
        (grad_ssm_y, grad_z_low, grad_attn, middle_low, grad_y_low, block_low)
    )
    slots["output"] = [flow.add(reduce_stream(joined, middle_low, WAITS["output"]))]
    block_all = lax.all_gather(block_low, "shard", axis=0, tiled=True)
    first = attention_backward(0, limit, projected, cosine, sine, grad_attn, logs)
    first, grad_attn = flow.step((first, grad_attn))
    second = attention_backward(1, limit, projected, cosine, sine, grad_attn, logs, first[1])
    second, grad_y_low, grad_z_low = flow.step((second, grad_y_low, grad_z_low))
    qkvz = jnp.concatenate([first[0], second[0], second[1], grad_z_low], 1)
    slots["input"] = [flow.add(reduce_stream(normed, qkvz, WAITS["qkvz"]))]
    upper = ssd_backward(0, limit, low, grad_y_low, tables)
    upper, grad_y_low = flow.step((upper, grad_y_low))
    lower = ssd_backward(1, limit, low, grad_y_low, tables, upper[1])
    lower, upper = flow.step((lower, upper))
    conv_args = (projected, position, conv_w_f, conv_b_f, step_lanes, skip_lanes)
    conv_upper = conv_backward(0, *conv_args, upper[0], grad_ssm_y, ssd_out, low, lower[2])
    conv_upper, lower = flow.step((conv_upper, lower))
    conv_lower = conv_backward(1, *conv_args, lower[0], grad_ssm_y, ssd_out, low, lower[2])
    conv_upper, conv_lower = flow.step((conv_upper, conv_lower))
    grad_u_low = jnp.concatenate([conv_upper[0], conv_lower[0]], 1)
    grad_taps = jnp.concatenate([conv_upper[1], conv_lower[1]], 1)
    head_parts = conv_upper[2] + conv_lower[2]
    slots["input"].append(flow.add(reduce_stream(normed, grad_u_low)))
    grad_projected = jnp.concatenate([qkvz, grad_u_low], 1)
    heads_of = lambda offset: head_parts[:, offset : offset + SSM_HEADS]
    grad_skip = jnp.sum(heads_of(64), 0)
    grad_inc = running_sum(heads_of(32), True)
    grad_step = heads_of(0) + grad_inc * rate
    grad_decay = jnp.sum(grad_inc * step, 0) * rate
    grad_step_pre = grad_step * jax.nn.sigmoid(step_pre)
    grad_step_bias = jnp.sum(grad_step_pre, 0)
    step_low = grad_step_pre.astype(jnp.bfloat16)
    grad_w_step = transposed_dot(normed, step_low)
    small_grads = (
        grad_w_step,
        grad_step_bias,
        grad_decay,
        grad_skip,
        grad_taps[:TAPS],
        grad_taps[TAPS],
        grad_gain_ssm,
        grad_gain_ffn,
    )
    grad_projected, step_low = flow.step((grad_projected, step_low))
    flat = jnp.concatenate([g.reshape(-1) for g in small_grads])
    flat = jnp.pad(flat, (0, -flat.shape[0] % 1024)).reshape(-1, SIDE)
    slot_flat = flow.add(butterfly_stream(flat))
    grad_normed = back(grad_projected, w_input_all) + back(step_low, w_step_all)
    grad_tokens_norm, grad_gain_attn = jax.vjp(rms_norm, own, gain_attn_f)[1](grad_normed)
    grad_low = (grad_middle + grad_tokens_norm).astype(jnp.bfloat16)
    near_flag = (lax.axis_index("rep") & 1).reshape(1).astype(jnp.int32)
    held = {}

    def finish_ready():
        for name in slots:
            if name not in held and all(slot["done"] for slot in slots[name]):
                held[name] = widen_rows([slot["result"] for slot in slots[name]], near_flag)

    grad_low, gain_late = flow.step((grad_low, grad_gain_attn.reshape(-1, SIDE)))
    slot_grad = flow.add(rows_stream(grad_low))
    slot_late = flow.add(butterfly_stream(gain_late))
    finish_ready()
    held["block"] = pick_rows([block_all], jnp.zeros((1,), jnp.int32), target)
    held = flow.step(held, [slot for slot in flow.live if slot is not slot_grad])
    while flow.live:
        finish_ready()
        if slot_grad["done"] and "tokens" not in held:
            pieces, owners = slot_grad["result"]
            held["tokens"] = pick_rows(pieces, owners * input_rows, target)
        held = flow.step(held)
    finish_ready()
    block_out, grad_tokens, widened = held["block"], held["tokens"], held
    outs = [None] * 13
    outs[0] = own_block(slot_late["result"].reshape(-1), 0)
    summed = slot_flat["result"].reshape(-1)
    offset = 0
    for i, grad in zip((2, 3, 4, 5, 6, 7, 8, 10), small_grads):
        block = summed[offset : offset + grad.size].reshape(grad.shape)
        offset += grad.size
        outs[i] = own_block(block, 1 if i == 6 else 0)
    for i, name in ((1, "input"), (9, "output"), (11, "gate_up"), (12, "down")):
        outs[i] = widened[name]
    return (block_out, grad_tokens, *outs)


def solution(mesh):
    placed = (
        P(("rep", "shard"), None),
        P("rep", None),
        P("rep", None),
        P("shard"),
        P("shard", None),
        P("shard", None),
        P("shard"),
        P("shard"),
        P("shard"),
        P(None, "shard"),
        P("shard"),
        P("shard"),
        P("shard", None),
        P("shard"),
        P("shard", None),
        P("shard", None),
        P(("rep", "shard"), None),
    )
    return jax.shard_map(
        on_device,
        mesh=mesh,
        in_specs=placed,
        out_specs=(
            P(("rep", "shard"), None),
            P(("rep", "shard"), None),
            P("shard"),
            P("shard", None),
            P("shard", None),
            P("shard"),
            P("shard"),
            P("shard"),
            P(None, "shard"),
            P("shard"),
            P("shard"),
            P("shard", None),
            P("shard"),
            P("shard", None),
            P("shard", None),
        ),
        check_vma=False,
    )
```

```python
from functools import partial
import math

import jax
import jax.numpy as jnp
from jax import lax
from jax.experimental import pallas as pl
from jax.experimental.pallas import tpu as pltpu
from jax.sharding import PartitionSpec as P

QUERY_HEADS = 8
KEY_VALUE_HEADS = 2
HEAD_SIZE = 64
SSM_HEADS = 24
SSM_HD = 64
STATE = 128
INNER = 1536
QUERY_KEY_VALUE = 768
TAPS = 4

EPS = 1e-05
ROPE_BASE = 100000000000.0
SIDE = 128
QUAD = 4
LOW = -1e30
SCALE = HEAD_SIZE ** (-0.5)


def causal_bias(limit, rows, row0, cols):
    i = lax.broadcasted_iota(jnp.int32, (rows, cols), 0) + row0
    j = lax.broadcasted_iota(jnp.int32, (rows, cols), 1)
    seen = (j <= i) & ((j >= limit) | (i < limit))
    return jnp.where(seen, 0.0, LOW)


def contract_last(left, right):
    return lax.dot_general(left, right, (((1,), (1,)), ((), ())), preferred_element_type=jnp.float32)


def contract_first(left, right):
    return lax.dot_general(left, right, (((0,), (0,)), ((), ())), preferred_element_type=jnp.float32)


def halves(pair):
    lane = lax.broadcasted_iota(jnp.int32, pair.shape, 1)
    zero = jnp.zeros_like(pair)
    return (jnp.where(lane < HEAD_SIZE, pair, zero), jnp.where(lane >= HEAD_SIZE, pair, zero))


def four_lanes(values, step):
    return pltpu.roll(values, lax.rem(SIDE - QUAD * step, SIDE), 1)


def ssd_forward_kernel(limit_ref, c_ref, b_ref, x_ref, cum_col_ref, cum_row_ref, out_ref, inter, bias):
    count = c_ref.shape[0]

    @pl.when(pl.program_id(0) == 0)
    def _():
        inter[...] = contract_last(c_ref[...], b_ref[...])
        bias[...] = causal_bias(limit_ref[0], count, 0, count)

    step = pl.program_id(0)
    cum_col = four_lanes(cum_col_ref[...], step)
    cum_row = cum_row_ref[pl.ds(pl.multiple_of(step // 2 * 8, 8), 8), :]
    cum_row = jnp.where(step % 2 == 0, cum_row[:QUAD], cum_row[QUAD:])
    for pair in range(QUAD // 2):
        lanes = slice(pair * SIDE, (pair + 1) * SIDE)
        sides = halves(x_ref[:, lanes])
        for top in range(0, count, SIDE):
            rows = slice(top, top + SIDE)
            seen = top + SIDE
            total = None
            for half in range(2):
                h = pair * 2 + half
                gap = cum_col[rows, h : h + 1] - cum_row[h : h + 1, :seen]
                mixer = (inter[rows, :seen] * jnp.exp(gap + bias[rows, :seen])).astype(jnp.bfloat16)
                part = jnp.dot(mixer, sides[half][:seen], preferred_element_type=jnp.float32)
                total = part if total is None else total + part
            out_ref[rows, lanes] = total


def ssd_forward(limit, low, tables):
    count = low.shape[0]
    steps = SSM_HEADS // QUAD
    b_spec = pl.BlockSpec((count, STATE), lambda i: (0, INNER // STATE))
    c_spec = pl.BlockSpec((count, STATE), lambda i: (0, INNER // STATE + 1))
    return pl.pallas_call(
        ssd_forward_kernel,
        grid=(steps,),
        out_shape=jax.ShapeDtypeStruct((count, INNER), jnp.float32),
        in_specs=[
            pl.BlockSpec(memory_space=pltpu.SMEM),
            c_spec,
            b_spec,
            pl.BlockSpec((count, QUAD * HEAD_SIZE), lambda i: (0, i)),
            pl.BlockSpec((count, SIDE), lambda i: (0, 0)),
            pl.BlockSpec((SIDE, count), lambda i: (0, 0)),
        ],
        out_specs=pl.BlockSpec((count, QUAD * HEAD_SIZE), lambda i: (0, i)),
        scratch_shapes=[pltpu.VMEM((count, count), jnp.float32)] * 2,
        name="ssd_forward",
    )(limit, low, low, low, *tables)


def ssd_backward_kernel(part, limit_ref, c_ref, b_ref, x_ref, dy_ref, cum_col_ref, cum_row_ref, *refs):
    if part == 0:
        z_ref, total, inter, bias = refs
    else:
        held_ref, z_ref, total, gbc_ref, inter, bias = refs
    count = c_ref.shape[0]

    @pl.when(pl.program_id(0) == 0)
    def _():
        inter[...] = contract_last(c_ref[...], b_ref[...])
        bias[...] = causal_bias(limit_ref[0], count, 0, count)
        total[...] = jnp.zeros_like(total) if part == 0 else held_ref[...]

    step = pl.program_id(0) + part * (SSM_HEADS // QUAD // 2)
    cum_col = four_lanes(cum_col_ref[...], step)
    cum_row = cum_row_ref[pl.ds(pl.multiple_of(step // 2 * 8, 8), 8), :]
    cum_row = jnp.where(step % 2 == 0, cum_row[:QUAD], cum_row[QUAD:])
    for pair in range(QUAD // 2):
        lanes = slice(pair * SIDE, (pair + 1) * SIDE)
        x_pair = x_ref[:, lanes]
        sides = halves(dy_ref[:, lanes])
        for top in reversed(range(0, count, SIDE)):
            rows = slice(top, top + SIDE)
            seen = top + SIDE
            grad = None
            back = None
            for half in range(2):
                h = pair * 2 + half
                gap = cum_col[rows, h : h + 1] - cum_row[h : h + 1, :seen]
                decay = jnp.exp(gap + bias[rows, :seen])
                mixer = (inter[rows, :seen] * decay).astype(jnp.bfloat16)
                grad_mixer = contract_last(sides[half][rows], x_pair[:seen])
                piece = grad_mixer * decay
                grad = piece if grad is None else grad + piece
                piece = contract_first(mixer, sides[half][rows])
                back = piece if back is None else back + piece
            total[rows, :seen] += grad
            if seen == count:
                z_ref[:, lanes] = back
            else:
                z_ref[:seen, lanes] += back

    if part == 1:

        @pl.when(pl.program_id(0) == pl.num_programs(0) - 1)
        def _():
            low = total[...].astype(jnp.bfloat16)
            gbc_ref[:, :STATE] = contract_first(low, c_ref[...])
            gbc_ref[:, STATE:] = jnp.dot(low, b_ref[...], preferred_element_type=jnp.float32)


def ssd_backward(part, limit, low, grad_y, tables, held=None):
    count = low.shape[0]
    steps = SSM_HEADS // QUAD // 2
    b_spec = pl.BlockSpec((count, STATE), lambda i: (0, INNER // STATE))
    c_spec = pl.BlockSpec((count, STATE), lambda i: (0, INNER // STATE + 1))
    quad = pl.BlockSpec((count, QUAD * HEAD_SIZE), lambda i: (0, i + part * steps))
    square = pl.BlockSpec((count, count), lambda i: (0, 0))
    out_shape = [
        jax.ShapeDtypeStruct((count, INNER // 2), jnp.float32),
        jax.ShapeDtypeStruct((count, count), jnp.float32),
    ]
    out_specs = [pl.BlockSpec((count, QUAD * HEAD_SIZE), lambda i: (0, i)), square]
    if part == 1:
        out_shape.append(jax.ShapeDtypeStruct((count, 2 * STATE), jnp.float32))
        out_specs.append(pl.BlockSpec((count, 2 * STATE), lambda i: (0, 0)))
    more = [] if held is None else [held]
    return pl.pallas_call(
        partial(ssd_backward_kernel, part),
        grid=(steps,),
        out_shape=tuple(out_shape),
        in_specs=[
            pl.BlockSpec(memory_space=pltpu.SMEM),
            c_spec,
            b_spec,
            quad,
            quad,
            pl.BlockSpec((count, SIDE), lambda i: (0, 0)),
            pl.BlockSpec((SIDE, count), lambda i: (0, 0)),
        ]
        + [square] * len(more),
        out_specs=tuple(out_specs),
        scratch_shapes=[pltpu.VMEM((count, count), jnp.float32)] * 2,
        name="ssd_backward",
    )(limit, low, low, low, grad_y, *tables, *more)


def turn(values, cosine, sine):
    lane = lax.broadcasted_iota(jnp.int32, values.shape, 1) % HEAD_SIZE
    width = values.shape[1]
    ahead = pltpu.roll(values, width - HEAD_SIZE // 2, 1)
    behind = pltpu.roll(values, HEAD_SIZE // 2, 1)
    other = jnp.where(lane < HEAD_SIZE // 2, ahead, behind)
    return values * cosine + other * sine


def both_sides(pair, step):
    lane = lax.broadcasted_iota(jnp.int32, pair.shape, 1)
    mine = jnp.where((lane >= HEAD_SIZE) == (step > 0), pair, jnp.zeros_like(pair))
    return (mine + pltpu.roll(mine, HEAD_SIZE, 1)).astype(jnp.bfloat16)


def attention_forward_kernel(limit_ref, q_ref, k_ref, v_ref, cos_ref, sin_ref, out_ref, log_ref, bias):
    count = k_ref.shape[0]
    step = pl.program_id(0)

    @pl.when(step == 0)
    def _():
        bias[...] = causal_bias(limit_ref[0], count, 0, count)

    cosine, sine = cos_ref[...], sin_ref[...]
    key = both_sides(turn(k_ref[...], cosine, sine), step)
    value_sides = halves(both_sides(v_ref[...], step))
    for pair in range(2):
        lanes = slice(pair * SIDE, (pair + 1) * SIDE)
        sides = halves(turn(q_ref[:, lanes], cosine, sine).astype(jnp.bfloat16) * SCALE)
        for top in range(0, count, SIDE):
            rows = slice(top, top + SIDE)
            seen = top + SIDE
            total = None
            for half in range(2):
                score = contract_last(sides[half][rows], key[:seen]) + bias[rows, :seen]
                largest = jnp.max(score, -1, keepdims=True)
                raised = jnp.exp(score - largest)
                mass = jnp.sum(raised, -1, keepdims=True)
                weights = (raised * (1.0 / mass)).astype(jnp.bfloat16)
                part = jnp.dot(weights, value_sides[half][:seen], preferred_element_type=jnp.float32)
                total = part if total is None else total + part
                h = pair * 2 + half
                log_ref[0, rows, h : h + 1] = largest + jnp.log(mass)
            out_ref[rows, lanes] = total.astype(jnp.bfloat16)


def attention_specs(count):
    wide = pl.BlockSpec((count, 2 * SIDE), lambda i: (0, i))
    whole = pl.BlockSpec((count, SIDE), lambda i: (0, 0))
    keys = pl.BlockSpec((count, SIDE), lambda i: (0, QUERY_HEADS * HEAD_SIZE // SIDE))
    values = pl.BlockSpec((count, SIDE), lambda i: (0, QUERY_HEADS * HEAD_SIZE // SIDE + 1))
    logs = pl.BlockSpec((1, count, QUAD), lambda i: (i, 0, 0))
    return wide, whole, keys, values, logs


def attention_forward(limit, projected, cosine, sine):
    count = projected.shape[0]
    wide, whole, keys, values, logs = attention_specs(count)
    return pl.pallas_call(
        attention_forward_kernel,
        grid=(KEY_VALUE_HEADS,),
        out_shape=(
            jax.ShapeDtypeStruct((count, QUERY_HEADS * HEAD_SIZE), jnp.bfloat16),
            jax.ShapeDtypeStruct((KEY_VALUE_HEADS, count, QUAD), jnp.float32),
        ),
        in_specs=[pl.BlockSpec(memory_space=pltpu.SMEM), wide, keys, values, whole, whole],
        out_specs=(wide, logs),
        scratch_shapes=[pltpu.VMEM((count, count), jnp.float32)],
        name="attention_forward",
    )(limit, projected, projected, projected, cosine, sine)


def attention_backward_kernel(step, limit_ref, q_ref, k_ref, v_ref, cos_ref, sin_ref, go_ref, log_ref, *refs):
    (gq_ref, gkv_ref), (bias, gk, gv) = refs[-5:-3], refs[-3:]
    count = k_ref.shape[0]
    bias[...] = causal_bias(limit_ref[0], count, 0, count)
    cosine, sine = cos_ref[...], sin_ref[...]
    key = both_sides(turn(k_ref[...], cosine, sine), step)
    value = both_sides(v_ref[...], step)
    key_sides = halves(key)
    gk[...] = jnp.zeros_like(gk)
    gv[...] = jnp.zeros_like(gv)
    for pair in range(2):
        lanes = slice(pair * SIDE, (pair + 1) * SIDE)
        q_sides = halves(turn(q_ref[:, lanes], cosine, sine).astype(jnp.bfloat16) * SCALE)
        go_sides = halves(go_ref[:, lanes])
        for top in range(0, count, SIDE):
            rows = slice(top, top + SIDE)
            seen = top + SIDE
            total = None
            for half in range(2):
                h = pair * 2 + half
                score = contract_last(q_sides[half][rows], key[:seen])
                weights = jnp.exp(score + bias[rows, :seen] - log_ref[0, rows, h : h + 1])
                grad = contract_last(go_sides[half][rows], value[:seen])
                inner = jnp.sum(grad * weights, -1, keepdims=True)
                low = (weights * (grad - inner)).astype(jnp.bfloat16)
                part = jnp.dot(low, key_sides[half][:seen], preferred_element_type=jnp.float32)
                total = part if total is None else total + part
                gk[:seen, :] += contract_first(low, q_sides[half][rows])
                gv[:seen, :] += contract_first(weights.astype(jnp.bfloat16), go_sides[half][rows])
            gq_ref[rows, lanes] = turn(total * SCALE, cosine[rows], -sine[rows]).astype(jnp.bfloat16)
    lane = lax.broadcasted_iota(jnp.int32, (count, SIDE), 1)
    mine = (lane >= HEAD_SIZE) == (step > 0)
    for place, part in enumerate((gk, gv)):
        summed = part[...] + pltpu.roll(part[...], HEAD_SIZE, 1)
        if place == 0:
            summed = turn(summed, cosine, -sine)
        lanes = slice(place * SIDE, (place + 1) * SIDE)
        if step > 0:
            summed = jnp.where(mine, summed, refs[0][:, lanes].astype(jnp.float32))
        gkv_ref[:, lanes] = summed.astype(jnp.bfloat16)


def attention_backward(step, limit, projected, cosine, sine, grad_out, logs_in, other=None):
    count = projected.shape[0]
    _, whole, keys, values, _ = attention_specs(count)
    at = lambda spec: pl.BlockSpec(spec.block_shape, lambda i: spec.index_map(step))
    wide, _, _, _, logs = attention_specs(count)
    both = pl.BlockSpec((count, 2 * SIDE), lambda i: (0, 0))
    more = [] if other is None else [other]
    return pl.pallas_call(
        partial(attention_backward_kernel, step),
        grid=(1,),
        out_shape=(
            jax.ShapeDtypeStruct((count, 2 * SIDE), jnp.bfloat16),
            jax.ShapeDtypeStruct((count, 2 * SIDE), jnp.bfloat16),
        ),
        in_specs=[pl.BlockSpec(memory_space=pltpu.SMEM), at(wide), keys, values, whole, whole, at(wide), at(logs)]
        + [both] * len(more),
        out_specs=(both, both),
        scratch_shapes=[
            pltpu.VMEM((count, count), jnp.float32),
            pltpu.VMEM((count, SIDE), jnp.float32),
            pltpu.VMEM((count, SIDE), jnp.float32),
        ],
        name="attention_backward",
    )(limit, projected, projected, projected, cosine, sine, grad_out, logs_in, *more)


BLOCK = QUAD * HEAD_SIZE


TILE = 128
HALO = 8


def conv_taps(u_ref, top, place, weight_ref, bias_ref, lanes):
    mixed = bias_ref[:, lanes] + u_ref[HALO + top : HALO + top + TILE, lanes] * weight_ref[TAPS - 1 : TAPS, lanes]
    for back in range(1, TAPS):
        shifted = u_ref[HALO + top - back : HALO + top - back + TILE, lanes]
        mixed = mixed + jnp.where(place >= back, shifted, 0.0) * weight_ref[TAPS - 1 - back : TAPS - back, lanes]
    return mixed


def conv_forward_kernel(u_ref, place_ref, weight_ref, bias_ref, step_ref, out_ref, low_ref, held):
    count = u_ref.shape[0]
    held[:HALO, :] = jnp.zeros((HALO, BLOCK), jnp.float32)
    held[HALO:, :] = u_ref[...]
    lane = lax.broadcasted_iota(jnp.int32, (TILE, SIDE), 1)
    scale = four_lanes(step_ref[...], pl.program_id(0))
    for side in range(BLOCK // SIDE):
        lanes = slice(side * SIDE, (side + 1) * SIDE)
        for top in range(0, count, TILE):
            rows = slice(top, top + TILE)
            mixed = conv_taps(held, top, place_ref[rows], weight_ref, bias_ref, lanes)
            out = mixed / (1.0 + jnp.exp(-mixed))
            out_ref[rows, lanes] = out
            first, second = scale[rows, 2 * side : 2 * side + 1], scale[rows, 2 * side + 1 : 2 * side + 2]
            low_ref[rows, lanes] = (out * jnp.where(lane < HEAD_SIZE, first, second)).astype(jnp.bfloat16)


def conv_specs(count, begin=0):
    column = lambda i: (0, i + begin)
    first = (QUERY_KEY_VALUE + INNER) // BLOCK + begin
    return (
        pl.BlockSpec((count, BLOCK), lambda i: (0, first + i)),
        pl.BlockSpec((count, 1), lambda i: (0, 0)),
        pl.BlockSpec((TAPS, BLOCK), column),
        pl.BlockSpec((1, BLOCK), column),
        pl.BlockSpec((count, SIDE), lambda i: (0, 0)),
        pl.BlockSpec((count, BLOCK), column),
    )


def conv_forward(projected, position, weight, bias, step_quads):
    count, width = projected.shape[0], weight.shape[1]
    u, place, taps, row, quads, block = conv_specs(count)
    return pl.pallas_call(
        conv_forward_kernel,
        grid=(width // BLOCK,),
        out_shape=(
            jax.ShapeDtypeStruct((count, width), jnp.float32),
            jax.ShapeDtypeStruct((count, width), jnp.bfloat16),
        ),
        in_specs=[u, place, taps, row, quads],
        out_specs=(block, block),
        scratch_shapes=[pltpu.VMEM((HALO + count, BLOCK), jnp.float32)],
        name="conv_forward",
    )(projected, position[:, None], weight, bias[None], step_quads)


def head_sums(values, chosen):
    high = values.astype(jnp.bfloat16)
    low = (values - high.astype(jnp.float32)).astype(jnp.bfloat16)
    return jnp.dot(high, chosen, preferred_element_type=jnp.float32) + jnp.dot(
        low, chosen, preferred_element_type=jnp.float32
    )


def conv_backward_kernel(
    first, u_ref, place_ref, weight_ref, bias_ref, step_ref, skip_ref, z_ref, gy_ref, y_ref, low_ref, gbc_ref,
    gu_ref, gw_ref, heads_ref, held, grads,
):
    count = u_ref.shape[0]
    step = pl.program_id(0) + first
    inner = step < INNER // BLOCK
    scale = four_lanes(step_ref[...], step)
    held[:HALO, :] = jnp.zeros((HALO, BLOCK), jnp.float32)
    held[HALO:, :] = u_ref[...]
    lane = lax.broadcasted_iota(jnp.int32, (TILE, SIDE), 1)

    @pl.when(pl.program_id(0) == 0)
    def _():
        heads_ref[...] = jnp.zeros_like(heads_ref)

    for side in range(BLOCK // SIDE):
        lanes = slice(side * SIDE, (side + 1) * SIDE)
        sums = [None] * (TAPS + 1)
        head = lax.broadcasted_iota(jnp.int32, (SIDE, SIDE), 0) // HEAD_SIZE + 2 * side + QUAD * step
        column = lax.broadcasted_iota(jnp.int32, (SIDE, SIDE), 1)
        chosen = [(head + offset == column).astype(jnp.bfloat16) for offset in (0, 32, 64)]
        for back in range(1, TAPS):
            grads[back - 1, count:, lanes] = jnp.zeros((HALO, SIDE), jnp.float32)
        for top in range(0, count, TILE):
            rows = slice(top, top + TILE)
            place = place_ref[rows]
            mixed = conv_taps(held, top, place, weight_ref, bias_ref, lanes)
            gate = 1.0 / (1.0 + jnp.exp(-mixed))
            out = mixed * gate
            z, gy = z_ref[rows, lanes], gy_ref[rows, lanes]
            first, second = scale[rows, 2 * side : 2 * side + 1], scale[rows, 2 * side + 1 : 2 * side + 2]
            grad = z * jnp.where(lane < HEAD_SIZE, first, second) + skip_ref[:, lanes] * gy
            grad = jnp.where(inner, grad, gbc_ref[rows, lanes])
            gy_low = gy.astype(jnp.bfloat16).astype(jnp.float32)
            cum = gy_low * y_ref[rows, lanes] - low_ref[rows, lanes].astype(jnp.float32) * z
            part = head_sums(z * out, chosen[0]) + head_sums(cum, chosen[1]) + head_sums(gy * out, chosen[2])
            heads_ref[rows, :] += jnp.where(inner, part, 0.0)
            grad = grad * (gate + out * (1.0 - gate))
            parts = [jnp.sum(grad, 0, keepdims=True)]
            parts.append(jnp.sum(grad * held[HALO + top : HALO + top + TILE, lanes], 0, keepdims=True))
            grads[TAPS - 1, rows, lanes] = grad * weight_ref[TAPS - 1 : TAPS, lanes]
            for back in range(1, TAPS):
                seen = jnp.where(place >= back, grad, 0.0)
                shifted = held[HALO + top - back : HALO + top - back + TILE, lanes]
                parts.append(jnp.sum(seen * shifted, 0, keepdims=True))
                grads[back - 1, rows, lanes] = seen * weight_ref[TAPS - 1 - back : TAPS - back, lanes]
            sums = [p if s is None else s + p for s, p in zip(sums, parts)]
        gw_ref[:, lanes] = jnp.zeros((8, SIDE), jnp.float32)
        gw_ref[TAPS : TAPS + 1, lanes] = sums[0]
        for back in range(TAPS):
            gw_ref[TAPS - 1 - back : TAPS - back, lanes] = sums[1 + back]
        for top in range(0, count, TILE):
            total = grads[TAPS - 1, top : top + TILE, lanes]
            for back in range(1, TAPS):
                total = total + grads[back - 1, top + back : top + back + TILE, lanes]
            gu_ref[top : top + TILE, lanes] = total.astype(jnp.bfloat16)


def conv_backward(part, projected, position, weight, bias, step_lanes, skip, z, grad_y, y, low, grad_bc):
    count = projected.shape[0]
    cut = INNER // BLOCK // 2
    begin, blocks = (0, cut) if part == 0 else (cut, weight.shape[1] // BLOCK - cut)
    u, place, taps, row, lanes, block = conv_specs(count, begin)
    last = INNER // BLOCK - 1
    inner = pl.BlockSpec((count, BLOCK), lambda i: (0, jnp.minimum(i + begin, last)))
    half = pl.BlockSpec((count, BLOCK), lambda i: (0, jnp.minimum(i, cut - 1)))
    skip_row = pl.BlockSpec((1, BLOCK), lambda i: (0, jnp.minimum(i + begin, last)))
    return pl.pallas_call(
        partial(conv_backward_kernel, begin),
        grid=(blocks,),
        out_shape=(
            jax.ShapeDtypeStruct((count, blocks * BLOCK), jnp.bfloat16),
            jax.ShapeDtypeStruct((8, blocks * BLOCK), jnp.float32),
            jax.ShapeDtypeStruct((count, SIDE), jnp.float32),
        ),
        in_specs=[u, place, taps, row, lanes, skip_row, half, inner, inner, block, pl.BlockSpec((count, BLOCK), lambda i: (0, 0))],
        out_specs=(
            pl.BlockSpec((count, BLOCK), lambda i: (0, i)),
            pl.BlockSpec((8, BLOCK), lambda i: (0, i)),
            pl.BlockSpec((count, SIDE), lambda i: (0, 0)),
        ),
        scratch_shapes=[
            pltpu.VMEM((HALO + count, BLOCK), jnp.float32),
            pltpu.VMEM((TAPS, count + HALO, BLOCK), jnp.float32),
        ],
        name="conv_backward",
    )(projected, position[:, None], weight, bias[None], step_lanes, skip, z, grad_y, y, low, grad_bc)


def pick_kernel(shift_ref, wanted_ref, *refs):
    out_ref = refs[-1]
    pieces = refs[:-1]
    count = pieces[0].shape[0]
    place = lax.broadcasted_iota(jnp.int32, (out_ref.shape[0], count), 1)
    total = None
    for n, piece in enumerate(pieces):
        choice = (wanted_ref[...] - shift_ref[n] == place).astype(jnp.bfloat16)
        part = jnp.dot(choice, piece[...], preferred_element_type=jnp.float32)
        total = part if total is None else total + part
    out_ref[...] = total.astype(out_ref.dtype)


def pick_rows(pieces, shifts, wanted):
    vmem = pl.BlockSpec(memory_space=pltpu.VMEM)
    return pl.pallas_call(
        pick_kernel,
        out_shape=jax.ShapeDtypeStruct((wanted.shape[0], pieces[0].shape[1]), pieces[0].dtype),
        in_specs=[pl.BlockSpec(memory_space=pltpu.SMEM), vmem] + [vmem] * len(pieces),
        out_specs=vmem,
        name="pick_rows",
    )(shifts, wanted[:, None], *pieces)


def lay_rows_kernel(place_ref, *refs):
    sems = refs[-1]
    out_ref = refs[-2]
    pieces = refs[:-2]
    copies = []
    for n, piece in enumerate(pieces):
        rows = piece.shape[0]
        start = pl.multiple_of(place_ref[n] * 16, 16)
        copies.append(pltpu.make_async_copy(piece, out_ref.at[pl.ds(start, rows)], sems.at[n]))
    for copy in copies:
        copy.start()
    for copy in copies:
        copy.wait()


def lay_rows(pieces, places):
    rows = sum(piece.shape[0] for piece in pieces)
    hbm = pl.BlockSpec(memory_space=pl.ANY)
    return pl.pallas_call(
        lay_rows_kernel,
        out_shape=jax.ShapeDtypeStruct((rows, pieces[0].shape[1]), pieces[0].dtype),
        in_specs=[pl.BlockSpec(memory_space=pltpu.SMEM)] + [hbm] * len(pieces),
        out_specs=pl.BlockSpec(memory_space=pltpu.VMEM),
        scratch_shapes=[pltpu.SemaphoreType.DMA((len(pieces),))],
        name="lay_rows",
    )(places // 16, *pieces)


def widen_kernel(columns, parts, replica_ref, *refs):
    out_ref = refs[-1]
    near, rest = replica_ref[0] & 1, replica_ref[0] >> 1
    for n, block in enumerate(refs[:-1]):
        left, count = columns[n // 2], parts[n // 2]
        rows = block.shape[0] // count
        for k in range(count):
            place = near ^ (n % 2)
            if count > 1:
                place = place * count + (rest ^ k)
            start = pl.multiple_of(place * rows, rows)
            piece = block[k * rows : (k + 1) * rows, :]
            out_ref[pl.ds(start, rows), left : left + block.shape[1]] = piece.astype(jnp.float32)


def widen_rows(chunks, parts, replica):
    flat = [block for chunk in chunks for block in chunk]
    columns, left = [], 0
    for chunk in chunks:
        columns.append(left)
        left += chunk[0].shape[1]
    rows = 2 * chunks[0][0].shape[0]
    vmem = pl.BlockSpec(memory_space=pltpu.VMEM)
    return pl.pallas_call(
        partial(widen_kernel, tuple(columns), tuple(parts)),
        out_shape=jax.ShapeDtypeStruct((rows, left), jnp.float32),
        in_specs=[pl.BlockSpec(memory_space=pltpu.SMEM)] + [vmem] * len(flat),
        out_specs=vmem,
        name="widen_rows",
    )(replica, *flat)


def swap(values, axis, mask):
    count = lax.axis_size(axis)
    return lax.ppermute(values, axis, [(i, i ^ mask) for i in range(count)])


def take(values, index, dim):
    return lax.dynamic_index_in_dim(values, index, dim, keepdims=False)


def add(first, *others):
    total = first.astype(jnp.float32)
    for other in others:
        total = total + other.astype(jnp.float32)
    return total.astype(jnp.bfloat16)


class Flow:
    def __init__(self):
        self.live = []

    def add(self, stream):
        slot = {"stream": stream, "sent": None, "left": 0, "result": None, "done": False}
        self.live.append(slot)
        self._advance(slot, None)
        return slot

    def _advance(self, slot, value):
        try:
            sent = slot["stream"].send(value)
            slot["sent"], slot["left"] = sent if isinstance(sent, tuple) else (sent, 1)
        except StopIteration as stop:
            slot["result"] = stop.value
            slot["sent"] = None
            slot["done"] = True
            self.live.remove(slot)

    def step(self, values=None, slots=None, force=False):
        slots = [slot for slot in (self.live if slots is None else slots) if not slot["done"]]
        for slot in slots:
            slot["left"] -= 1
        slots = [slot for slot in slots if slot["left"] <= 0 or force]
        values, sent = lax.optimization_barrier((values, [slot["sent"] for slot in slots]))
        for slot, came in zip(slots, sent):
            self._advance(slot, came)
        return values

    def until(self, slots, values=None, alone=False):
        while any(not slot["done"] for slot in slots):
            values = self.step(values, slots if alone else None)
        return values


def rows_stream(piece, wait=1):
    shard = lax.axis_index("shard")
    held = [(0, piece)]
    mask = lax.axis_size("shard") // 2
    first = True
    near = None
    while mask > 1:
        send = [swap(p, "shard", mask) for _, p in held]
        if first:
            send.append(swap(piece, "shard", 1))
        came = yield send, wait
        if first:
            near = came[-1]
            first = False
        held = held + [(k ^ mask, p) for (k, _), p in zip(held, came)]
        mask //= 2
    came = yield [swap(p, "shard", 1) for k, p in held[1:]]
    held = held + [(1, near)] + [(k ^ 1, p) for (k, _), p in zip(held[1:], came)]
    keys = [k for k, _ in held]
    return [p for _, p in held], jnp.stack([shard ^ k for k in keys]).astype(jnp.int32)


def weight_stream(piece, wait=1):
    rows, width = piece.shape
    shard, near = lax.axis_index("shard"), lax.axis_index("rep") & 1
    part = lax.dynamic_slice_in_dim(piece, near * (rows // 2), rows // 2, 0)
    held = [(0, part)]
    both = []
    mask = lax.axis_size("shard") // 2
    beside = None
    while mask > 1:
        send = [swap(p, "shard", mask) for _, p in held]
        if beside is None:
            send.append(swap(piece, "shard", 1))
        came = yield send, wait
        if beside is None:
            beside = came[-1]
        fresh = [(k ^ mask, p) for (k, _), p in zip(held, came)]
        passed = yield [swap(p, "rep", 1) for _, p in fresh] + [swap(p, "shard", 1) for _, p in fresh]
        count = len(fresh)
        for n, (k, p) in enumerate(fresh):
            both.append((k, 0, p))
            both.append((k ^ 1, 0, passed[count + n]))
            both.append((k, 1, passed[n]))
        held = held + fresh
        mask //= 2
    late = [(k, p) for k, side, p in both if side == 1]
    came = yield [swap(p, "shard", 1) for _, p in late]
    both = both + [(k ^ 1, 1, p) for (k, _), p in zip(late, came)]
    pieces = [piece, beside] + [p for _, _, p in both]
    places = [shard * rows, (shard ^ 1) * rows]
    places += [(shard ^ k) * rows + (near ^ side) * (rows // 2) for k, side, _ in both]
    return lay_rows(pieces, jnp.stack(places).astype(jnp.int32))


def transposed_dot(left, right):
    return lax.dot_general(left, right, (((0,), (0,)), ((), ())), preferred_element_type=jnp.float32)


def reduce_stream(left, right, waits=(1, 1, 1, 1, 1), direct=False):
    shards, replicas = lax.axis_size("shard"), lax.axis_size("rep")
    block = left.shape[1] // shards
    shard, near = lax.axis_index("shard"), lax.axis_index("rep") & 1
    core, far = shard & 1, shard >> 1

    def product(r, c, extras=(), half=None):
        start, size = ((far ^ r) * 2 + c) * block, block
        if half is not None:
            size = block // 2
            start = start + half * size
            extras = [x if x.shape[0] == size else lax.dynamic_slice_in_dim(x, half * size, size, 0) for x in extras]
        total = transposed_dot(lax.dynamic_slice_in_dim(left, start, size, 1), right)
        for extra in extras:
            total = total + extra.astype(jnp.float32)
        return total.astype(jnp.bfloat16)

    count = shards // 2
    came = yield [swap(product(r, 1 - core), "shard", 1) for r in range(count)], waits[0]
    extras = [[c] for c in came]
    while count > 1:
        count //= 2
        came = yield [swap(product(r, core, extras[r]), "shard", 2 * count) for r in range(count, 2 * count)], waits[1]
        for n, c in enumerate(came):
            extras[n].append(c)
    came = yield [swap(product(0, core, extras[0], 1 - near), "rep", 1)], waits[2]
    total = product(0, core, [*extras[0], came[0]], near)
    if direct:
        parts = lax.axis_size("rep") // 2
        rest = lax.axis_index("rep") >> 1
        split = total.reshape(parts, -1, right.shape[1])
        others = range(1, parts)
        came = yield [swap(take(split, rest ^ k, 0), "rep", 2 * k) for k in others]
        mine = add(take(split, rest, 0), *came)
        came = yield [swap(mine, "rep", 2 * k) for k in others]
        total = jnp.concatenate([mine, *came], 0)
        came = yield [swap(total, "rep", 1)]
        return total, came[0]
    mask = 2
    while mask < replicas:
        came = yield [swap(total, "rep", mask)], waits[3 if mask == 2 else 4]
        total = add(total, came[0])
        mask *= 2
    came = yield [swap(total, "rep", 1)]
    return total, came[0]


def butterfly_stream(total):
    for axis in ("shard", "rep"):
        mask = 1
        while mask < lax.axis_size(axis):
            came = yield [swap(total, axis, mask)]
            total = total + came[0]
            mask *= 2
    return total


def small_stream(flat):
    held = flat[None]
    mask = 1
    shard = lax.axis_index("shard")
    while mask < lax.axis_size("shard"):
        came = yield [swap(held, "shard", mask)]
        flag = (shard & mask) == 0
        held = jnp.concatenate([jnp.where(flag, held, came[0]), jnp.where(flag, came[0], held)], 0)
        mask *= 2
    return held


def unpack_small(every, shapes, dims):
    parts = every.shape[0]
    outputs = []
    offset = 0
    for shape, dim in zip(shapes, dims):
        length = math.prod(shape)
        block = every[:, offset : offset + length].reshape((parts,) + shape)
        offset += length
        if dim == 0:
            outputs.append(block.reshape((-1,) + shape[1:]))
        else:
            outputs.append(jnp.swapaxes(block, 0, 1).reshape(shape[0], -1))
    return outputs


def own_block(values, dim):
    size = values.shape[dim] // lax.axis_size("shard")
    return lax.dynamic_slice_in_dim(values, lax.axis_index("shard") * size, size, dim)


def group_tables(lengths, order, input_rows, device):
    count = lengths.shape[0]
    slots = jnp.arange(count, dtype=jnp.int32)
    starts = jnp.cumsum(lengths) - lengths
    pick = (order[:, None] == slots[None, :]).astype(jnp.int32)
    owner_len = jnp.sum(pick * lengths[None, :], 1)
    owner_start = jnp.cumsum(owner_len) - owner_len
    owner_src = jnp.sum(pick * starts[None, :], 1)
    first_len = jnp.sum(jnp.where(slots == 2 * device, owner_len, 0))
    first_src = jnp.sum(jnp.where(slots == 2 * device, owner_src, 0))
    second_src = jnp.sum(jnp.where(slots == 2 * device + 1, owner_src, 0))
    local = jnp.arange(input_rows, dtype=jnp.int32)
    segment = (local >= first_len).astype(jnp.int32)
    position = local - segment * first_len
    source = jnp.where(segment > 0, second_src, first_src) + position
    given = device * input_rows + local
    seq_id = jnp.sum((starts[None, :] <= given[:, None]).astype(jnp.int32), 1) - 1
    member = (seq_id[:, None] == slots[None, :]).astype(jnp.int32)
    seq_start = jnp.sum(member * starts[None, :], 1)
    seq_owner_start = jnp.sum(pick * owner_start[:, None], 0)
    target = jnp.sum(member * seq_owner_start[None, :], 1) + given - seq_start
    return (source, position, first_len.reshape(1), target)


def rms_scale(values):
    return lax.rsqrt(jnp.mean(values * values, axis=-1, keepdims=True) + EPS)


def rms_norm(values, gain):
    return values * rms_scale(values) * gain


def rope_tables(position):
    half = HEAD_SIZE // 2
    lane = jnp.arange(SIDE, dtype=jnp.int32)
    ladder = (lane % half).astype(jnp.float32) * (2.0 / HEAD_SIZE)
    angles = position.astype(jnp.float32)[:, None] * jnp.exp(-math.log(ROPE_BASE) * ladder)
    sign = jnp.where(lane % HEAD_SIZE < half, -1.0, 1.0)
    return jnp.cos(angles), jnp.sin(angles) * sign


def gated_norm(ssm_y, gate_z, gain):
    gated = ssm_y * jax.nn.silu(gate_z)
    return gated * rms_scale(gated) * gain


def swiglu(gate_up):
    half = gate_up.shape[1] // 2
    return jax.nn.silu(gate_up[:, :half]) * gate_up[:, half:]


def dot(left, right):
    return jnp.dot(left, right, preferred_element_type=jnp.float32)


def running_sum(values, reverse):
    count = values.shape[0]
    i = lax.broadcasted_iota(jnp.int32, (count, count), 0)
    j = lax.broadcasted_iota(jnp.int32, (count, count), 1)
    chosen = ((i <= j) if reverse else (j <= i)).astype(jnp.float32)
    return jnp.dot(chosen, values, precision=lax.Precision.HIGHEST)


def to_lanes(values, fill):
    count, width = values.shape
    return jnp.concatenate([values, jnp.full((count, SIDE - width), fill, values.dtype)], 1)


SMALL = (2, 3, 4, 5, 6, 7, 8, 10)
PLAN = (0, 2, 2)
WAITS = {
    "down": (1, 2, 1, 1, 1),
    "gate": (1, 2, 1, 1, 1),
    "up": (1, 2, 1, 1, 1),
    "output": (1, 3, 1, 1, 1),
    "qkvz": (1, 3, 1, 1, 1),
    "u": (1, 1, 1, 1, 1),
}


def on_device(
    tokens,
    seq_lengths,
    owner_order,
    gain_attn,
    w_input,
    w_step,
    step_bias,
    decay_log,
    skip_scale,
    conv_weight,
    conv_bias,
    gain_ssm,
    w_output,
    gain_ffn,
    w_gate_up,
    w_down,
    cotangent,
):
    input_rows = tokens.shape[0]
    shard = lax.axis_index("shard")
    flow = Flow()
    f32 = lambda v: v.astype(jnp.float32)

    slot_input = flow.add(weight_stream(w_input))
    small_args = (gain_attn, w_step, step_bias, decay_log, skip_scale, conv_weight, conv_bias, gain_ssm, gain_ffn)
    small_dims = (0, 0, 0, 0, 0, 1, 0, 0, 0)
    slot_small = flow.add(small_stream(jnp.concatenate([a.reshape(-1) for a in small_args])))
    source, position, limit, target = group_tables(seq_lengths[0], owner_order[0], input_rows, shard)
    cosine, sine = rope_tables(position)
    source, position, tokens, cosine, sine, w_output = flow.step((source, position, tokens, cosine, sine, w_output))
    slot_tokens = flow.add(rows_stream(tokens))
    source, position, w_output, w_gate_up, w_down, cotangent = flow.step(
        (source, position, w_output, w_gate_up, w_down, cotangent)
    )
    slot_output = flow.add(weight_stream(w_output, 2))
    w_gate_up_all = lax.all_gather(w_gate_up, "shard", axis=0, tiled=True)
    w_down_all = lax.all_gather(w_down, "shard", axis=0, tiled=True)
    source, position, cotangent = flow.until([slot_tokens, slot_input, slot_small], (source, position, cotangent), True)

    gain_attn_all, w_step_all, step_bias_all, decay_all, skip_all, conv_w_all, conv_b_all, gain_ssm_all, gain_ffn_all = (
        unpack_small(slot_small["result"], [a.shape for a in small_args], small_dims)
    )
    gain_attn_f, gain_ssm_f, gain_ffn_f = f32(gain_attn_all), f32(gain_ssm_all), f32(gain_ffn_all)
    conv_w_f, conv_b_f = f32(conv_w_all), f32(conv_b_all)
    skip_lanes = jnp.repeat(f32(skip_all), SSM_HD)[None]
    pieces, owners = slot_tokens["result"]
    own = f32(pick_rows(pieces, owners * input_rows, source))
    w_input_all = slot_input["result"]

    normed = rms_norm(own, gain_attn_f).astype(jnp.bfloat16)
    projected = dot(normed, w_input_all)
    step_pre = dot(normed, w_step_all) + f32(step_bias_all)
    step = jax.nn.softplus(step_pre)
    rate = -jnp.exp(f32(decay_all))
    cum = to_lanes(running_sum(step * rate, False), 0.0)
    tables = (cum, cum.T)
    step_lanes = to_lanes(step, 1.0)
    projected, normed = flow.step((projected, normed))
    conv_out, low = conv_forward(projected, position, conv_w_f, conv_b_f, step_lanes)
    inner_x = conv_out[:, :INNER]
    low, cotangent, projected = flow.step((low, cotangent, projected))
    slot_cot = flow.add(rows_stream(cotangent, 2))
    attn_out, logs = attention_forward(limit, projected, cosine, sine)
    attn_out, low = flow.step((attn_out, low))
    ssd_out = ssd_forward(limit, low, tables)
    ssd_out, projected = flow.until([slot_output], (ssd_out, projected), True)
    w_output_all = slot_output["result"]
    gate_z = projected[:, QUERY_KEY_VALUE : QUERY_KEY_VALUE + INNER]
    ssm_y = ssd_out + skip_lanes * inner_x
    ssm_out = gated_norm(ssm_y, gate_z, gain_ssm_f).astype(jnp.bfloat16)
    joined = jnp.concatenate([attn_out, ssm_out], 1)
    middle = own + dot(joined, w_output_all)
    normed_ffn = rms_norm(middle, gain_ffn_f).astype(jnp.bfloat16)
    gate_up = dot(normed_ffn, w_gate_up_all)
    hidden = swiglu(gate_up).astype(jnp.bfloat16)
    gate_up, hidden = flow.until([slot_cot], (gate_up, hidden))
    pieces, owners = slot_cot["result"]
    cot = pick_rows(pieces, owners * input_rows, source)

    def back(left, weight):
        return lax.dot_general(left, weight, (((1,), (1,)), ((), ())), preferred_element_type=jnp.float32)

    slots = {}
    slots["down"] = [flow.add(reduce_stream(hidden, cot, WAITS["down"]))]
    grad_hidden = back(cot, w_down_all)
    grad_gate_up = jax.vjp(swiglu, gate_up)[1](grad_hidden)[0].astype(jnp.bfloat16)
    grad_gate_up = flow.step(grad_gate_up)
    half = grad_gate_up.shape[1] // 2
    slots["gate_up"] = [flow.add(reduce_stream(normed_ffn, grad_gate_up[:, :half], WAITS["gate"]))]
    grad_normed_ffn = back(grad_gate_up, w_gate_up_all)
    grad_middle_norm, grad_gain_ffn = jax.vjp(rms_norm, middle, gain_ffn_f)[1](grad_normed_ffn)
    grad_middle = f32(cot) + grad_middle_norm
    grad_middle, grad_gate_up = flow.step((grad_middle, grad_gate_up))
    slots["gate_up"].append(flow.add(reduce_stream(normed_ffn, grad_gate_up[:, half:], WAITS["up"])))
    middle_low = grad_middle.astype(jnp.bfloat16)
    grad_joined = back(middle_low, w_output_all)
    grad_attn = grad_joined[:, : QUERY_HEADS * HEAD_SIZE].astype(jnp.bfloat16)
    grad_ssm_out = grad_joined[:, QUERY_HEADS * HEAD_SIZE :]
    grad_ssm_y, grad_z, grad_gain_ssm = jax.vjp(gated_norm, ssm_y, gate_z, gain_ssm_f)[1](grad_ssm_out)
    grad_z_low = grad_z.astype(jnp.bfloat16)
    grad_y_low = grad_ssm_y.astype(jnp.bfloat16)
    grad_ssm_y, grad_z_low, grad_attn, middle_low, grad_y_low = flow.step(
        (grad_ssm_y, grad_z_low, grad_attn, middle_low, grad_y_low)
    )
    slots["output"] = [flow.add(reduce_stream(joined, middle_low, WAITS["output"]))]
    first = attention_backward(0, limit, projected, cosine, sine, grad_attn, logs)
    first, grad_attn = flow.step((first, grad_attn))
    second = attention_backward(1, limit, projected, cosine, sine, grad_attn, logs, first[1])
    second, grad_y_low, grad_z_low = flow.step((second, grad_y_low, grad_z_low))
    qkvz = jnp.concatenate([first[0], second[0], second[1], grad_z_low], 1)
    slots["input"] = [flow.add(reduce_stream(normed, qkvz, WAITS["qkvz"]))]
    upper = ssd_backward(0, limit, low, grad_y_low, tables)
    upper, grad_y_low, hidden = flow.step((upper, grad_y_low, hidden))
    block_low = (middle + dot(hidden, w_down_all)).astype(jnp.bfloat16)
    lower = ssd_backward(1, limit, low, grad_y_low, tables, upper[1])
    lower, upper, block_low = flow.step((lower, upper, block_low))
    block_all = lax.all_gather(block_low, "shard", axis=0, tiled=True)
    conv_args = (projected, position, conv_w_f, conv_b_f, step_lanes, skip_lanes)
    conv_upper = conv_backward(0, *conv_args, upper[0], grad_ssm_y, ssd_out, low, lower[2])
    conv_upper, lower = flow.step((conv_upper, lower))
    conv_lower = conv_backward(1, *conv_args, lower[0], grad_ssm_y, ssd_out, low, lower[2])
    conv_upper, conv_lower = flow.step((conv_upper, conv_lower))
    grad_u_low = jnp.concatenate([conv_upper[0], conv_lower[0]], 1)
    grad_taps = jnp.concatenate([conv_upper[1], conv_lower[1]], 1)
    head_parts = conv_upper[2] + conv_lower[2]
    slots["input"].append(flow.add(reduce_stream(normed, grad_u_low, WAITS["u"], True)))
    last = slots["input"][-1:]
    grad_projected = jnp.concatenate([qkvz, grad_u_low], 1)
    heads_of = lambda offset: head_parts[:, offset : offset + SSM_HEADS]
    grad_skip = jnp.sum(heads_of(64), 0)
    grad_inc = running_sum(heads_of(32), True)
    grad_step = heads_of(0) + grad_inc * rate
    grad_decay = jnp.sum(grad_inc * step, 0) * rate
    grad_step_pre = grad_step * jax.nn.sigmoid(step_pre)
    grad_step_bias = jnp.sum(grad_step_pre, 0)
    step_low = grad_step_pre.astype(jnp.bfloat16)
    grad_w_step = transposed_dot(normed, step_low)
    small_grads = (
        grad_w_step,
        grad_step_bias,
        grad_decay,
        grad_skip,
        grad_taps[:TAPS],
        grad_taps[TAPS],
        grad_gain_ssm,
        grad_gain_ffn,
    )
    grad_projected, step_low = flow.step((grad_projected, step_low))
    flat = jnp.concatenate([g.reshape(-1) for g in small_grads])
    flat = jnp.pad(flat, (0, -flat.shape[0] % 1024)).reshape(-1, SIDE)
    slot_flat = flow.add(butterfly_stream(flat))
    grad_normed = back(grad_projected, w_input_all) + back(step_low, w_step_all)
    grad_tokens_norm, grad_gain_attn = jax.vjp(rms_norm, own, gain_attn_f)[1](grad_normed)
    grad_low = (grad_middle + grad_tokens_norm).astype(jnp.bfloat16)
    replica = lax.axis_index("rep").reshape(1).astype(jnp.int32)
    line = lax.axis_size("rep") // 2
    held = {}

    def widen(name):
        parts = [line if slot in last else 1 for slot in slots[name]]
        held[name] = widen_rows([slot["result"] for slot in slots[name]], parts, replica)

    grad_low, gain_late, block_all = flow.step((grad_low, grad_gain_attn.reshape(-1, SIDE), block_all))
    slot_grad = flow.add(rows_stream(grad_low))
    slot_late = flow.add(butterfly_stream(gain_late))
    queue = ["late", "small", "down", "gate_up", "block", "output", "tokens", "input"]

    def small_outputs():
        summed = slot_flat["result"].reshape(-1)
        offset = 0
        blocks = []
        for i, grad in zip(SMALL, small_grads):
            block = summed[offset : offset + grad.size].reshape(grad.shape)
            offset += grad.size
            blocks.append(own_block(block, 1 if i == 6 else 0))
        return blocks

    def work(limit):
        for name in list(queue):
            if limit == 0:
                return
            if name in ("late", "small"):
                if not (slot_late if name == "late" else slot_flat)["done"]:
                    continue
                held[name] = small_outputs() if name == "small" else own_block(slot_late["result"].reshape(-1), 0)
                limit += 1
            elif name == "block":
                held["block"] = pick_rows([block_all], jnp.zeros((1,), jnp.int32), target)
            elif name == "tokens":
                if not slot_grad["done"]:
                    continue
                pieces, owners = slot_grad["result"]
                held["tokens"] = pick_rows(pieces, owners * input_rows, target)
            else:
                if not all(slot["done"] for slot in slots[name]):
                    continue
                widen(name)
            queue.remove(name)
            limit -= 1

    boundary = 0
    while flow.live:
        work(PLAN[boundary] if boundary < len(PLAN) else 2)
        held = flow.step(held, [slot for slot in flow.live if slot is not slot_grad] if boundary == 0 else None)
        boundary += 1
    work(len(queue))
    block_out, grad_tokens, widened = held["block"], held["tokens"], held
    outs = [None] * 13
    outs[0] = held["late"]
    for i, name in enumerate(SMALL):
        outs[name] = held["small"][i]
    for i, name in ((1, "input"), (9, "output"), (11, "gate_up"), (12, "down")):
        outs[i] = widened[name]
    return (block_out, grad_tokens, *outs)


def solution(mesh):
    placed = (
        P(("rep", "shard"), None),
        P("rep", None),
        P("rep", None),
        P("shard"),
        P("shard", None),
        P("shard", None),
        P("shard"),
        P("shard"),
        P("shard"),
        P(None, "shard"),
        P("shard"),
        P("shard"),
        P("shard", None),
        P("shard"),
        P("shard", None),
        P("shard", None),
        P(("rep", "shard"), None),
    )
    return jax.shard_map(
        on_device,
        mesh=mesh,
        in_specs=placed,
        out_specs=(
            P(("rep", "shard"), None),
            P(("rep", "shard"), None),
            P("shard"),
            P("shard", None),
            P("shard", None),
            P("shard"),
            P("shard"),
            P("shard"),
            P(None, "shard"),
            P("shard"),
            P("shard"),
            P("shard", None),
            P("shard"),
            P("shard", None),
            P("shard", None),
        ),
        check_vma=False,
    )
```

```python
from functools import partial
import math

import jax
import jax.numpy as jnp
from jax import lax
from jax.experimental import pallas as pl
from jax.experimental.pallas import tpu as pltpu
from jax.sharding import PartitionSpec as P

QUERY_HEADS = 8
KEY_VALUE_HEADS = 2
HEAD_SIZE = 64
SSM_HEADS = 24
SSM_HD = 64
STATE = 128
INNER = 1536
QUERY_KEY_VALUE = 768
TAPS = 4

EPS = 1e-05
ROPE_BASE = 100000000000.0
SIDE = 128
QUAD = 4
LOW = -1e30
SCALE = HEAD_SIZE ** (-0.5)


def causal_bias(limit, rows, row0, cols):
    i = lax.broadcasted_iota(jnp.int32, (rows, cols), 0) + row0
    j = lax.broadcasted_iota(jnp.int32, (rows, cols), 1)
    seen = (j <= i) & ((j >= limit) | (i < limit))
    return jnp.where(seen, 0.0, LOW)


def contract_last(left, right):
    return lax.dot_general(left, right, (((1,), (1,)), ((), ())), preferred_element_type=jnp.float32)


def contract_first(left, right):
    return lax.dot_general(left, right, (((0,), (0,)), ((), ())), preferred_element_type=jnp.float32)


def halves(pair):
    lane = lax.broadcasted_iota(jnp.int32, pair.shape, 1)
    zero = jnp.zeros_like(pair)
    return (jnp.where(lane < HEAD_SIZE, pair, zero), jnp.where(lane >= HEAD_SIZE, pair, zero))


def four_lanes(values, step):
    return pltpu.roll(values, lax.rem(SIDE - QUAD * step, SIDE), 1)


def ssd_forward_kernel(limit_ref, c_ref, b_ref, x_ref, cum_col_ref, cum_row_ref, out_ref, inter, bias):
    count = c_ref.shape[0]

    @pl.when(pl.program_id(0) == 0)
    def _():
        inter[...] = contract_last(c_ref[...], b_ref[...])
        bias[...] = causal_bias(limit_ref[0], count, 0, count)

    step = pl.program_id(0)
    cum_col = four_lanes(cum_col_ref[...], step)
    cum_row = cum_row_ref[pl.ds(pl.multiple_of(step // 2 * 8, 8), 8), :]
    cum_row = jnp.where(step % 2 == 0, cum_row[:QUAD], cum_row[QUAD:])
    for pair in range(QUAD // 2):
        lanes = slice(pair * SIDE, (pair + 1) * SIDE)
        sides = halves(x_ref[:, lanes])
        for top in range(0, count, SIDE):
            rows = slice(top, top + SIDE)
            seen = top + SIDE
            total = None
            for half in range(2):
                h = pair * 2 + half
                gap = cum_col[rows, h : h + 1] - cum_row[h : h + 1, :seen]
                mixer = (inter[rows, :seen] * jnp.exp(gap + bias[rows, :seen])).astype(jnp.bfloat16)
                part = jnp.dot(mixer, sides[half][:seen], preferred_element_type=jnp.float32)
                total = part if total is None else total + part
            out_ref[rows, lanes] = total


def ssd_forward(limit, low, tables):
    count = low.shape[0]
    steps = SSM_HEADS // QUAD
    b_spec = pl.BlockSpec((count, STATE), lambda i: (0, INNER // STATE))
    c_spec = pl.BlockSpec((count, STATE), lambda i: (0, INNER // STATE + 1))
    return pl.pallas_call(
        ssd_forward_kernel,
        grid=(steps,),
        out_shape=jax.ShapeDtypeStruct((count, INNER), jnp.float32),
        in_specs=[
            pl.BlockSpec(memory_space=pltpu.SMEM),
            c_spec,
            b_spec,
            pl.BlockSpec((count, QUAD * HEAD_SIZE), lambda i: (0, i)),
            pl.BlockSpec((count, SIDE), lambda i: (0, 0)),
            pl.BlockSpec((SIDE, count), lambda i: (0, 0)),
        ],
        out_specs=pl.BlockSpec((count, QUAD * HEAD_SIZE), lambda i: (0, i)),
        scratch_shapes=[pltpu.VMEM((count, count), jnp.float32)] * 2,
        name="ssd_forward",
    )(limit, low, low, low, *tables)


def ssd_backward_kernel(part, limit_ref, c_ref, b_ref, x_ref, dy_ref, cum_col_ref, cum_row_ref, *refs):
    if part == 0:
        z_ref, total, inter, bias = refs
    else:
        held_ref, z_ref, total, gbc_ref, inter, bias = refs
    count = c_ref.shape[0]

    @pl.when(pl.program_id(0) == 0)
    def _():
        inter[...] = contract_last(c_ref[...], b_ref[...])
        bias[...] = causal_bias(limit_ref[0], count, 0, count)
        total[...] = jnp.zeros_like(total) if part == 0 else held_ref[...]

    step = pl.program_id(0) + part * (SSM_HEADS // QUAD // 2)
    cum_col = four_lanes(cum_col_ref[...], step)
    cum_row = cum_row_ref[pl.ds(pl.multiple_of(step // 2 * 8, 8), 8), :]
    cum_row = jnp.where(step % 2 == 0, cum_row[:QUAD], cum_row[QUAD:])
    for pair in range(QUAD // 2):
        lanes = slice(pair * SIDE, (pair + 1) * SIDE)
        x_pair = x_ref[:, lanes]
        sides = halves(dy_ref[:, lanes])
        for top in reversed(range(0, count, SIDE)):
            rows = slice(top, top + SIDE)
            seen = top + SIDE
            grad = None
            back = None
            for half in range(2):
                h = pair * 2 + half
                gap = cum_col[rows, h : h + 1] - cum_row[h : h + 1, :seen]
                decay = jnp.exp(gap + bias[rows, :seen])
                mixer = (inter[rows, :seen] * decay).astype(jnp.bfloat16)
                grad_mixer = contract_last(sides[half][rows], x_pair[:seen])
                piece = grad_mixer * decay
                grad = piece if grad is None else grad + piece
                piece = contract_first(mixer, sides[half][rows])
                back = piece if back is None else back + piece
            total[rows, :seen] += grad
            if seen == count:
                z_ref[:, lanes] = back
            else:
                z_ref[:seen, lanes] += back

    if part == 1:

        @pl.when(pl.program_id(0) == pl.num_programs(0) - 1)
        def _():
            low = total[...].astype(jnp.bfloat16)
            gbc_ref[:, :STATE] = contract_first(low, c_ref[...])
            gbc_ref[:, STATE:] = jnp.dot(low, b_ref[...], preferred_element_type=jnp.float32)


def ssd_backward(part, limit, low, grad_y, tables, held=None):
    count = low.shape[0]
    steps = SSM_HEADS // QUAD // 2
    b_spec = pl.BlockSpec((count, STATE), lambda i: (0, INNER // STATE))
    c_spec = pl.BlockSpec((count, STATE), lambda i: (0, INNER // STATE + 1))
    quad = pl.BlockSpec((count, QUAD * HEAD_SIZE), lambda i: (0, i + part * steps))
    square = pl.BlockSpec((count, count), lambda i: (0, 0))
    out_shape = [
        jax.ShapeDtypeStruct((count, INNER // 2), jnp.float32),
        jax.ShapeDtypeStruct((count, count), jnp.float32),
    ]
    out_specs = [pl.BlockSpec((count, QUAD * HEAD_SIZE), lambda i: (0, i)), square]
    if part == 1:
        out_shape.append(jax.ShapeDtypeStruct((count, 2 * STATE), jnp.float32))
        out_specs.append(pl.BlockSpec((count, 2 * STATE), lambda i: (0, 0)))
    more = [] if held is None else [held]
    return pl.pallas_call(
        partial(ssd_backward_kernel, part),
        grid=(steps,),
        out_shape=tuple(out_shape),
        in_specs=[
            pl.BlockSpec(memory_space=pltpu.SMEM),
            c_spec,
            b_spec,
            quad,
            quad,
            pl.BlockSpec((count, SIDE), lambda i: (0, 0)),
            pl.BlockSpec((SIDE, count), lambda i: (0, 0)),
        ]
        + [square] * len(more),
        out_specs=tuple(out_specs),
        scratch_shapes=[pltpu.VMEM((count, count), jnp.float32)] * 2,
        name="ssd_backward",
    )(limit, low, low, low, grad_y, *tables, *more)


def turn(values, cosine, sine):
    lane = lax.broadcasted_iota(jnp.int32, values.shape, 1) % HEAD_SIZE
    width = values.shape[1]
    ahead = pltpu.roll(values, width - HEAD_SIZE // 2, 1)
    behind = pltpu.roll(values, HEAD_SIZE // 2, 1)
    other = jnp.where(lane < HEAD_SIZE // 2, ahead, behind)
    return values * cosine + other * sine


def both_sides(pair, step):
    lane = lax.broadcasted_iota(jnp.int32, pair.shape, 1)
    mine = jnp.where((lane >= HEAD_SIZE) == (step > 0), pair, jnp.zeros_like(pair))
    return (mine + pltpu.roll(mine, HEAD_SIZE, 1)).astype(jnp.bfloat16)


def attention_forward_kernel(limit_ref, q_ref, k_ref, v_ref, cos_ref, sin_ref, out_ref, log_ref, bias):
    count = k_ref.shape[0]
    step = pl.program_id(0)

    @pl.when(step == 0)
    def _():
        bias[...] = causal_bias(limit_ref[0], count, 0, count)

    cosine, sine = cos_ref[...], sin_ref[...]
    key = both_sides(turn(k_ref[...], cosine, sine), step)
    value_sides = halves(both_sides(v_ref[...], step))
    for pair in range(2):
        lanes = slice(pair * SIDE, (pair + 1) * SIDE)
        sides = halves(turn(q_ref[:, lanes], cosine, sine).astype(jnp.bfloat16) * SCALE)
        for top in range(0, count, SIDE):
            rows = slice(top, top + SIDE)
            seen = top + SIDE
            total = None
            for half in range(2):
                score = contract_last(sides[half][rows], key[:seen]) + bias[rows, :seen]
                largest = jnp.max(score, -1, keepdims=True)
                raised = jnp.exp(score - largest)
                mass = jnp.sum(raised, -1, keepdims=True)
                weights = (raised * (1.0 / mass)).astype(jnp.bfloat16)
                part = jnp.dot(weights, value_sides[half][:seen], preferred_element_type=jnp.float32)
                total = part if total is None else total + part
                h = pair * 2 + half
                log_ref[0, rows, h : h + 1] = largest + jnp.log(mass)
            out_ref[rows, lanes] = total.astype(jnp.bfloat16)


def attention_specs(count):
    wide = pl.BlockSpec((count, 2 * SIDE), lambda i: (0, i))
    whole = pl.BlockSpec((count, SIDE), lambda i: (0, 0))
    keys = pl.BlockSpec((count, SIDE), lambda i: (0, QUERY_HEADS * HEAD_SIZE // SIDE))
    values = pl.BlockSpec((count, SIDE), lambda i: (0, QUERY_HEADS * HEAD_SIZE // SIDE + 1))
    logs = pl.BlockSpec((1, count, QUAD), lambda i: (i, 0, 0))
    return wide, whole, keys, values, logs


def attention_forward(limit, projected, cosine, sine):
    count = projected.shape[0]
    wide, whole, keys, values, logs = attention_specs(count)
    return pl.pallas_call(
        attention_forward_kernel,
        grid=(KEY_VALUE_HEADS,),
        out_shape=(
            jax.ShapeDtypeStruct((count, QUERY_HEADS * HEAD_SIZE), jnp.bfloat16),
            jax.ShapeDtypeStruct((KEY_VALUE_HEADS, count, QUAD), jnp.float32),
        ),
        in_specs=[pl.BlockSpec(memory_space=pltpu.SMEM), wide, keys, values, whole, whole],
        out_specs=(wide, logs),
        scratch_shapes=[pltpu.VMEM((count, count), jnp.float32)],
        name="attention_forward",
    )(limit, projected, projected, projected, cosine, sine)


def attention_backward_kernel(step, limit_ref, q_ref, k_ref, v_ref, cos_ref, sin_ref, go_ref, log_ref, *refs):
    (gq_ref, gkv_ref), (bias, gk, gv) = refs[-5:-3], refs[-3:]
    count = k_ref.shape[0]
    bias[...] = causal_bias(limit_ref[0], count, 0, count)
    cosine, sine = cos_ref[...], sin_ref[...]
    key = both_sides(turn(k_ref[...], cosine, sine), step)
    value = both_sides(v_ref[...], step)
    key_sides = halves(key)
    gk[...] = jnp.zeros_like(gk)
    gv[...] = jnp.zeros_like(gv)
    for pair in range(2):
        lanes = slice(pair * SIDE, (pair + 1) * SIDE)
        q_sides = halves(turn(q_ref[:, lanes], cosine, sine).astype(jnp.bfloat16) * SCALE)
        go_sides = halves(go_ref[:, lanes])
        for top in range(0, count, SIDE):
            rows = slice(top, top + SIDE)
            seen = top + SIDE
            total = None
            for half in range(2):
                h = pair * 2 + half
                score = contract_last(q_sides[half][rows], key[:seen])
                weights = jnp.exp(score + bias[rows, :seen] - log_ref[0, rows, h : h + 1])
                grad = contract_last(go_sides[half][rows], value[:seen])
                inner = jnp.sum(grad * weights, -1, keepdims=True)
                low = (weights * (grad - inner)).astype(jnp.bfloat16)
                part = jnp.dot(low, key_sides[half][:seen], preferred_element_type=jnp.float32)
                total = part if total is None else total + part
                gk[:seen, :] += contract_first(low, q_sides[half][rows])
                gv[:seen, :] += contract_first(weights.astype(jnp.bfloat16), go_sides[half][rows])
            gq_ref[rows, lanes] = turn(total * SCALE, cosine[rows], -sine[rows]).astype(jnp.bfloat16)
    lane = lax.broadcasted_iota(jnp.int32, (count, SIDE), 1)
    mine = (lane >= HEAD_SIZE) == (step > 0)
    for place, part in enumerate((gk, gv)):
        summed = part[...] + pltpu.roll(part[...], HEAD_SIZE, 1)
        if place == 0:
            summed = turn(summed, cosine, -sine)
        lanes = slice(place * SIDE, (place + 1) * SIDE)
        if step > 0:
            summed = jnp.where(mine, summed, refs[0][:, lanes].astype(jnp.float32))
        gkv_ref[:, lanes] = summed.astype(jnp.bfloat16)


def attention_backward(step, limit, projected, cosine, sine, grad_out, logs_in, other=None):
    count = projected.shape[0]
    _, whole, keys, values, _ = attention_specs(count)
    at = lambda spec: pl.BlockSpec(spec.block_shape, lambda i: spec.index_map(step))
    wide, _, _, _, logs = attention_specs(count)
    both = pl.BlockSpec((count, 2 * SIDE), lambda i: (0, 0))
    more = [] if other is None else [other]
    return pl.pallas_call(
        partial(attention_backward_kernel, step),
        grid=(1,),
        out_shape=(
            jax.ShapeDtypeStruct((count, 2 * SIDE), jnp.bfloat16),
            jax.ShapeDtypeStruct((count, 2 * SIDE), jnp.bfloat16),
        ),
        in_specs=[pl.BlockSpec(memory_space=pltpu.SMEM), at(wide), keys, values, whole, whole, at(wide), at(logs)]
        + [both] * len(more),
        out_specs=(both, both),
        scratch_shapes=[
            pltpu.VMEM((count, count), jnp.float32),
            pltpu.VMEM((count, SIDE), jnp.float32),
            pltpu.VMEM((count, SIDE), jnp.float32),
        ],
        name="attention_backward",
    )(limit, projected, projected, projected, cosine, sine, grad_out, logs_in, *more)


BLOCK = QUAD * HEAD_SIZE


TILE = 128
HALO = 8


def conv_taps(u_ref, top, place, weight_ref, bias_ref, lanes):
    mixed = bias_ref[:, lanes] + u_ref[HALO + top : HALO + top + TILE, lanes] * weight_ref[TAPS - 1 : TAPS, lanes]
    for back in range(1, TAPS):
        shifted = u_ref[HALO + top - back : HALO + top - back + TILE, lanes]
        mixed = mixed + jnp.where(place >= back, shifted, 0.0) * weight_ref[TAPS - 1 - back : TAPS - back, lanes]
    return mixed


def conv_forward_kernel(u_ref, place_ref, weight_ref, bias_ref, step_ref, out_ref, low_ref, held):
    count = u_ref.shape[0]
    held[:HALO, :] = jnp.zeros((HALO, BLOCK), jnp.float32)
    held[HALO:, :] = u_ref[...]
    lane = lax.broadcasted_iota(jnp.int32, (TILE, SIDE), 1)
    scale = four_lanes(step_ref[...], pl.program_id(0))
    for side in range(BLOCK // SIDE):
        lanes = slice(side * SIDE, (side + 1) * SIDE)
        for top in range(0, count, TILE):
            rows = slice(top, top + TILE)
            mixed = conv_taps(held, top, place_ref[rows], weight_ref, bias_ref, lanes)
            out = mixed / (1.0 + jnp.exp(-mixed))
            out_ref[rows, lanes] = out
            first, second = scale[rows, 2 * side : 2 * side + 1], scale[rows, 2 * side + 1 : 2 * side + 2]
            low_ref[rows, lanes] = (out * jnp.where(lane < HEAD_SIZE, first, second)).astype(jnp.bfloat16)


def conv_specs(count, begin=0):
    column = lambda i: (0, i + begin)
    first = (QUERY_KEY_VALUE + INNER) // BLOCK + begin
    return (
        pl.BlockSpec((count, BLOCK), lambda i: (0, first + i)),
        pl.BlockSpec((count, 1), lambda i: (0, 0)),
        pl.BlockSpec((TAPS, BLOCK), column),
        pl.BlockSpec((1, BLOCK), column),
        pl.BlockSpec((count, SIDE), lambda i: (0, 0)),
        pl.BlockSpec((count, BLOCK), column),
    )


def conv_forward(projected, position, weight, bias, step_quads):
    count, width = projected.shape[0], weight.shape[1]
    u, place, taps, row, quads, block = conv_specs(count)
    return pl.pallas_call(
        conv_forward_kernel,
        grid=(width // BLOCK,),
        out_shape=(
            jax.ShapeDtypeStruct((count, width), jnp.float32),
            jax.ShapeDtypeStruct((count, width), jnp.bfloat16),
        ),
        in_specs=[u, place, taps, row, quads],
        out_specs=(block, block),
        scratch_shapes=[pltpu.VMEM((HALO + count, BLOCK), jnp.float32)],
        name="conv_forward",
    )(projected, position[:, None], weight, bias[None], step_quads)


def head_sums(values, chosen):
    high = values.astype(jnp.bfloat16)
    low = (values - high.astype(jnp.float32)).astype(jnp.bfloat16)
    return jnp.dot(high, chosen, preferred_element_type=jnp.float32) + jnp.dot(
        low, chosen, preferred_element_type=jnp.float32
    )


def conv_backward_kernel(
    first, u_ref, place_ref, weight_ref, bias_ref, step_ref, skip_ref, z_ref, gy_ref, y_ref, low_ref, gbc_ref,
    gu_ref, gw_ref, heads_ref, held, grads,
):
    count = u_ref.shape[0]
    step = pl.program_id(0) + first
    inner = step < INNER // BLOCK
    scale = four_lanes(step_ref[...], step)
    held[:HALO, :] = jnp.zeros((HALO, BLOCK), jnp.float32)
    held[HALO:, :] = u_ref[...]
    lane = lax.broadcasted_iota(jnp.int32, (TILE, SIDE), 1)

    @pl.when(pl.program_id(0) == 0)
    def _():
        heads_ref[...] = jnp.zeros_like(heads_ref)

    for side in range(BLOCK // SIDE):
        lanes = slice(side * SIDE, (side + 1) * SIDE)
        sums = [None] * (TAPS + 1)
        head = lax.broadcasted_iota(jnp.int32, (SIDE, SIDE), 0) // HEAD_SIZE + 2 * side + QUAD * step
        column = lax.broadcasted_iota(jnp.int32, (SIDE, SIDE), 1)
        chosen = [(head + offset == column).astype(jnp.bfloat16) for offset in (0, 32, 64)]
        for back in range(1, TAPS):
            grads[back - 1, count:, lanes] = jnp.zeros((HALO, SIDE), jnp.float32)
        for top in range(0, count, TILE):
            rows = slice(top, top + TILE)
            place = place_ref[rows]
            mixed = conv_taps(held, top, place, weight_ref, bias_ref, lanes)
            gate = 1.0 / (1.0 + jnp.exp(-mixed))
            out = mixed * gate
            z, gy = z_ref[rows, lanes], gy_ref[rows, lanes]
            first, second = scale[rows, 2 * side : 2 * side + 1], scale[rows, 2 * side + 1 : 2 * side + 2]
            grad = z * jnp.where(lane < HEAD_SIZE, first, second) + skip_ref[:, lanes] * gy
            grad = jnp.where(inner, grad, gbc_ref[rows, lanes])
            gy_low = gy.astype(jnp.bfloat16).astype(jnp.float32)
            cum = gy_low * y_ref[rows, lanes] - low_ref[rows, lanes].astype(jnp.float32) * z
            part = head_sums(z * out, chosen[0]) + head_sums(cum, chosen[1]) + head_sums(gy * out, chosen[2])
            heads_ref[rows, :] += jnp.where(inner, part, 0.0)
            grad = grad * (gate + out * (1.0 - gate))
            parts = [jnp.sum(grad, 0, keepdims=True)]
            parts.append(jnp.sum(grad * held[HALO + top : HALO + top + TILE, lanes], 0, keepdims=True))
            grads[TAPS - 1, rows, lanes] = grad * weight_ref[TAPS - 1 : TAPS, lanes]
            for back in range(1, TAPS):
                seen = jnp.where(place >= back, grad, 0.0)
                shifted = held[HALO + top - back : HALO + top - back + TILE, lanes]
                parts.append(jnp.sum(seen * shifted, 0, keepdims=True))
                grads[back - 1, rows, lanes] = seen * weight_ref[TAPS - 1 - back : TAPS - back, lanes]
            sums = [p if s is None else s + p for s, p in zip(sums, parts)]
        gw_ref[:, lanes] = jnp.zeros((8, SIDE), jnp.float32)
        gw_ref[TAPS : TAPS + 1, lanes] = sums[0]
        for back in range(TAPS):
            gw_ref[TAPS - 1 - back : TAPS - back, lanes] = sums[1 + back]
        for top in range(0, count, TILE):
            total = grads[TAPS - 1, top : top + TILE, lanes]
            for back in range(1, TAPS):
                total = total + grads[back - 1, top + back : top + back + TILE, lanes]
            gu_ref[top : top + TILE, lanes] = total.astype(jnp.bfloat16)


def conv_backward(part, projected, position, weight, bias, step_lanes, skip, z, grad_y, y, low, grad_bc):
    count = projected.shape[0]
    cut = INNER // BLOCK // 2
    begin, blocks = (0, cut) if part == 0 else (cut, weight.shape[1] // BLOCK - cut)
    u, place, taps, row, lanes, block = conv_specs(count, begin)
    last = INNER // BLOCK - 1
    inner = pl.BlockSpec((count, BLOCK), lambda i: (0, jnp.minimum(i + begin, last)))
    half = pl.BlockSpec((count, BLOCK), lambda i: (0, jnp.minimum(i, cut - 1)))
    skip_row = pl.BlockSpec((1, BLOCK), lambda i: (0, jnp.minimum(i + begin, last)))
    return pl.pallas_call(
        partial(conv_backward_kernel, begin),
        grid=(blocks,),
        out_shape=(
            jax.ShapeDtypeStruct((count, blocks * BLOCK), jnp.bfloat16),
            jax.ShapeDtypeStruct((8, blocks * BLOCK), jnp.float32),
            jax.ShapeDtypeStruct((count, SIDE), jnp.float32),
        ),
        in_specs=[u, place, taps, row, lanes, skip_row, half, inner, inner, block, pl.BlockSpec((count, BLOCK), lambda i: (0, 0))],
        out_specs=(
            pl.BlockSpec((count, BLOCK), lambda i: (0, i)),
            pl.BlockSpec((8, BLOCK), lambda i: (0, i)),
            pl.BlockSpec((count, SIDE), lambda i: (0, 0)),
        ),
        scratch_shapes=[
            pltpu.VMEM((HALO + count, BLOCK), jnp.float32),
            pltpu.VMEM((TAPS, count + HALO, BLOCK), jnp.float32),
        ],
        name="conv_backward",
    )(projected, position[:, None], weight, bias[None], step_lanes, skip, z, grad_y, y, low, grad_bc)


def pick_kernel(shift_ref, wanted_ref, *refs):
    out_ref = refs[-1]
    pieces = refs[:-1]
    count = pieces[0].shape[0]
    place = lax.broadcasted_iota(jnp.int32, (out_ref.shape[0], count), 1)
    total = None
    for n, piece in enumerate(pieces):
        choice = (wanted_ref[...] - shift_ref[n] == place).astype(jnp.bfloat16)
        part = jnp.dot(choice, piece[...], preferred_element_type=jnp.float32)
        total = part if total is None else total + part
    out_ref[...] = total.astype(out_ref.dtype)


def pick_rows(pieces, shifts, wanted):
    vmem = pl.BlockSpec(memory_space=pltpu.VMEM)
    return pl.pallas_call(
        pick_kernel,
        out_shape=jax.ShapeDtypeStruct((wanted.shape[0], pieces[0].shape[1]), pieces[0].dtype),
        in_specs=[pl.BlockSpec(memory_space=pltpu.SMEM), vmem] + [vmem] * len(pieces),
        out_specs=vmem,
        name="pick_rows",
    )(shifts, wanted[:, None], *pieces)


def lay_rows_kernel(place_ref, *refs):
    sems = refs[-1]
    out_ref = refs[-2]
    pieces = refs[:-2]
    copies = []
    for n, piece in enumerate(pieces):
        rows = piece.shape[0]
        start = pl.multiple_of(place_ref[n] * 16, 16)
        copies.append(pltpu.make_async_copy(piece, out_ref.at[pl.ds(start, rows)], sems.at[n]))
    for copy in copies:
        copy.start()
    for copy in copies:
        copy.wait()


def lay_rows(pieces, places):
    rows = sum(piece.shape[0] for piece in pieces)
    hbm = pl.BlockSpec(memory_space=pl.ANY)
    return pl.pallas_call(
        lay_rows_kernel,
        out_shape=jax.ShapeDtypeStruct((rows, pieces[0].shape[1]), pieces[0].dtype),
        in_specs=[pl.BlockSpec(memory_space=pltpu.SMEM)] + [hbm] * len(pieces),
        out_specs=pl.BlockSpec(memory_space=pltpu.VMEM),
        scratch_shapes=[pltpu.SemaphoreType.DMA((len(pieces),))],
        name="lay_rows",
    )(places // 16, *pieces)


def widen_kernel(columns, parts, replica_ref, *refs):
    out_ref = refs[-1]
    near, rest = replica_ref[0] & 1, replica_ref[0] >> 1
    for n, block in enumerate(refs[:-1]):
        left, count = columns[n // 2], parts[n // 2]
        rows = block.shape[0] // count
        for k in range(count):
            place = near ^ (n % 2)
            if count > 1:
                place = place * count + (rest ^ k)
            start = pl.multiple_of(place * rows, rows)
            piece = block[k * rows : (k + 1) * rows, :]
            out_ref[pl.ds(start, rows), left : left + block.shape[1]] = piece.astype(jnp.float32)


def widen_rows(chunks, parts, replica):
    flat = [block for chunk in chunks for block in chunk]
    columns, left = [], 0
    for chunk in chunks:
        columns.append(left)
        left += chunk[0].shape[1]
    rows = 2 * chunks[0][0].shape[0]
    vmem = pl.BlockSpec(memory_space=pltpu.VMEM)
    return pl.pallas_call(
        partial(widen_kernel, tuple(columns), tuple(parts)),
        out_shape=jax.ShapeDtypeStruct((rows, left), jnp.float32),
        in_specs=[pl.BlockSpec(memory_space=pltpu.SMEM)] + [vmem] * len(flat),
        out_specs=vmem,
        name="widen_rows",
    )(replica, *flat)


def swap(values, axis, mask):
    count = lax.axis_size(axis)
    return lax.ppermute(values, axis, [(i, i ^ mask) for i in range(count)])


def take(values, index, dim):
    return lax.dynamic_index_in_dim(values, index, dim, keepdims=False)


def add(first, *others):
    total = first.astype(jnp.float32)
    for other in others:
        total = total + other.astype(jnp.float32)
    return total.astype(jnp.bfloat16)


class Flow:
    def __init__(self):
        self.live = []

    def add(self, stream):
        slot = {"stream": stream, "sent": None, "left": 0, "result": None, "done": False}
        self.live.append(slot)
        self._advance(slot, None)
        return slot

    def _advance(self, slot, value):
        try:
            sent = slot["stream"].send(value)
            slot["sent"], slot["left"] = sent if isinstance(sent, tuple) else (sent, 1)
        except StopIteration as stop:
            slot["result"] = stop.value
            slot["sent"] = None
            slot["done"] = True
            self.live.remove(slot)

    def step(self, values=None, slots=None, force=False):
        slots = [slot for slot in (self.live if slots is None else slots) if not slot["done"]]
        for slot in slots:
            slot["left"] -= 1
        slots = [slot for slot in slots if slot["left"] <= 0 or force]
        values, sent = lax.optimization_barrier((values, [slot["sent"] for slot in slots]))
        for slot, came in zip(slots, sent):
            self._advance(slot, came)
        return values

    def until(self, slots, values=None, alone=False):
        while any(not slot["done"] for slot in slots):
            values = self.step(values, slots if alone else None)
        return values


def rows_stream(piece, wait=1):
    shard = lax.axis_index("shard")
    held = [(0, piece)]
    mask = lax.axis_size("shard") // 2
    first = True
    near = None
    while mask > 1:
        send = [swap(p, "shard", mask) for _, p in held]
        if first:
            send.append(swap(piece, "shard", 1))
        came = yield send, wait
        if first:
            near = came[-1]
            first = False
        held = held + [(k ^ mask, p) for (k, _), p in zip(held, came)]
        mask //= 2
    came = yield [swap(p, "shard", 1) for k, p in held[1:]]
    held = held + [(1, near)] + [(k ^ 1, p) for (k, _), p in zip(held[1:], came)]
    keys = [k for k, _ in held]
    return [p for _, p in held], jnp.stack([shard ^ k for k in keys]).astype(jnp.int32)


def weight_stream(piece, wait=1):
    rows, width = piece.shape
    shard, near = lax.axis_index("shard"), lax.axis_index("rep") & 1
    part = lax.dynamic_slice_in_dim(piece, near * (rows // 2), rows // 2, 0)
    held = [(0, part)]
    both = []
    mask = lax.axis_size("shard") // 2
    beside = None
    while mask > 1:
        send = [swap(p, "shard", mask) for _, p in held]
        if beside is None:
            send.append(swap(piece, "shard", 1))
        came = yield send, wait
        if beside is None:
            beside = came[-1]
        fresh = [(k ^ mask, p) for (k, _), p in zip(held, came)]
        passed = yield [swap(p, "rep", 1) for _, p in fresh] + [swap(p, "shard", 1) for _, p in fresh]
        count = len(fresh)
        for n, (k, p) in enumerate(fresh):
            both.append((k, 0, p))
            both.append((k ^ 1, 0, passed[count + n]))
            both.append((k, 1, passed[n]))
        held = held + fresh
        mask //= 2
    late = [(k, p) for k, side, p in both if side == 1]
    came = yield [swap(p, "shard", 1) for _, p in late]
    both = both + [(k ^ 1, 1, p) for (k, _), p in zip(late, came)]
    pieces = [piece, beside] + [p for _, _, p in both]
    places = [shard * rows, (shard ^ 1) * rows]
    places += [(shard ^ k) * rows + (near ^ side) * (rows // 2) for k, side, _ in both]
    return lay_rows(pieces, jnp.stack(places).astype(jnp.int32))


def transposed_dot(left, right):
    return lax.dot_general(left, right, (((0,), (0,)), ((), ())), preferred_element_type=jnp.float32)


def reduce_stream(left, right, waits=(1, 1, 1, 1, 1), direct=False):
    shards, replicas = lax.axis_size("shard"), lax.axis_size("rep")
    block = left.shape[1] // shards
    shard, near = lax.axis_index("shard"), lax.axis_index("rep") & 1
    core, far = shard & 1, shard >> 1

    def product(r, c, extras=(), half=None):
        start, size = ((far ^ r) * 2 + c) * block, block
        if half is not None:
            size = block // 2
            start = start + half * size
            extras = [x if x.shape[0] == size else lax.dynamic_slice_in_dim(x, half * size, size, 0) for x in extras]
        total = transposed_dot(lax.dynamic_slice_in_dim(left, start, size, 1), right)
        for extra in extras:
            total = total + extra.astype(jnp.float32)
        return total.astype(jnp.bfloat16)

    count = shards // 2
    came = yield [swap(product(r, 1 - core), "shard", 1) for r in range(count)], waits[0]
    extras = [[c] for c in came]
    while count > 1:
        count //= 2
        came = yield [swap(product(r, core, extras[r]), "shard", 2 * count) for r in range(count, 2 * count)], waits[1]
        for n, c in enumerate(came):
            extras[n].append(c)
    came = yield [swap(product(0, core, extras[0], 1 - near), "rep", 1)], waits[2]
    total = product(0, core, [*extras[0], came[0]], near)
    if direct:
        parts = lax.axis_size("rep") // 2
        rest = lax.axis_index("rep") >> 1
        split = total.reshape(parts, -1, right.shape[1])
        others = range(1, parts)
        came = yield [swap(take(split, rest ^ k, 0), "rep", 2 * k) for k in others]
        mine = add(take(split, rest, 0), *came)
        came = yield [swap(mine, "rep", 2 * k) for k in others]
        total = jnp.concatenate([mine, *came], 0)
        came = yield [swap(total, "rep", 1)]
        return total, came[0]
    mask = 2
    while mask < replicas:
        came = yield [swap(total, "rep", mask)], waits[3 if mask == 2 else 4]
        total = add(total, came[0])
        mask *= 2
    came = yield [swap(total, "rep", 1)]
    return total, came[0]


def butterfly_stream(total):
    for axis in ("shard", "rep"):
        mask = 1
        while mask < lax.axis_size(axis):
            came = yield [swap(total, axis, mask)]
            total = total + came[0]
            mask *= 2
    return total


def small_stream(flat):
    held = flat[None]
    mask = 1
    shard = lax.axis_index("shard")
    while mask < lax.axis_size("shard"):
        came = yield [swap(held, "shard", mask)]
        flag = (shard & mask) == 0
        held = jnp.concatenate([jnp.where(flag, held, came[0]), jnp.where(flag, came[0], held)], 0)
        mask *= 2
    return held


def unpack_small(every, shapes, dims):
    parts = every.shape[0]
    outputs = []
    offset = 0
    for shape, dim in zip(shapes, dims):
        length = math.prod(shape)
        block = every[:, offset : offset + length].reshape((parts,) + shape)
        offset += length
        if dim == 0:
            outputs.append(block.reshape((-1,) + shape[1:]))
        else:
            outputs.append(jnp.swapaxes(block, 0, 1).reshape(shape[0], -1))
    return outputs


def own_block(values, dim):
    size = values.shape[dim] // lax.axis_size("shard")
    return lax.dynamic_slice_in_dim(values, lax.axis_index("shard") * size, size, dim)


def group_tables(lengths, order, input_rows, device):
    count = lengths.shape[0]
    slots = jnp.arange(count, dtype=jnp.int32)
    starts = jnp.cumsum(lengths) - lengths
    pick = (order[:, None] == slots[None, :]).astype(jnp.int32)
    owner_len = jnp.sum(pick * lengths[None, :], 1)
    owner_start = jnp.cumsum(owner_len) - owner_len
    owner_src = jnp.sum(pick * starts[None, :], 1)
    first_len = jnp.sum(jnp.where(slots == 2 * device, owner_len, 0))
    first_src = jnp.sum(jnp.where(slots == 2 * device, owner_src, 0))
    second_src = jnp.sum(jnp.where(slots == 2 * device + 1, owner_src, 0))
    local = jnp.arange(input_rows, dtype=jnp.int32)
    segment = (local >= first_len).astype(jnp.int32)
    position = local - segment * first_len
    source = jnp.where(segment > 0, second_src, first_src) + position
    given = device * input_rows + local
    seq_id = jnp.sum((starts[None, :] <= given[:, None]).astype(jnp.int32), 1) - 1
    member = (seq_id[:, None] == slots[None, :]).astype(jnp.int32)
    seq_start = jnp.sum(member * starts[None, :], 1)
    seq_owner_start = jnp.sum(pick * owner_start[:, None], 0)
    target = jnp.sum(member * seq_owner_start[None, :], 1) + given - seq_start
    return (source, position, first_len.reshape(1), target)


def rms_scale(values):
    return lax.rsqrt(jnp.mean(values * values, axis=-1, keepdims=True) + EPS)


def rms_norm(values, gain):
    return values * rms_scale(values) * gain


def rope_tables(position):
    half = HEAD_SIZE // 2
    lane = jnp.arange(SIDE, dtype=jnp.int32)
    ladder = (lane % half).astype(jnp.float32) * (2.0 / HEAD_SIZE)
    angles = position.astype(jnp.float32)[:, None] * jnp.exp(-math.log(ROPE_BASE) * ladder)
    sign = jnp.where(lane % HEAD_SIZE < half, -1.0, 1.0)
    return jnp.cos(angles), jnp.sin(angles) * sign


def gated_norm(ssm_y, gate_z, gain):
    gated = ssm_y * jax.nn.silu(gate_z)
    return gated * rms_scale(gated) * gain


def swiglu(gate_up):
    half = gate_up.shape[1] // 2
    return jax.nn.silu(gate_up[:, :half]) * gate_up[:, half:]


def dot(left, right):
    return jnp.dot(left, right, preferred_element_type=jnp.float32)


def running_sum(values, reverse):
    count = values.shape[0]
    i = lax.broadcasted_iota(jnp.int32, (count, count), 0)
    j = lax.broadcasted_iota(jnp.int32, (count, count), 1)
    chosen = ((i <= j) if reverse else (j <= i)).astype(jnp.float32)
    return jnp.dot(chosen, values, precision=lax.Precision.HIGHEST)


def to_lanes(values, fill):
    count, width = values.shape
    return jnp.concatenate([values, jnp.full((count, SIDE - width), fill, values.dtype)], 1)


SMALL = (2, 3, 4, 5, 6, 7, 8, 10)
PLAN = (0, 2, 2)
WAITS = {
    "down": (1, 2, 1, 1, 1),
    "gate": (1, 2, 1, 1, 2),
    "up": (1, 2, 1, 1, 3),
    "output": (1, 3, 1, 1, 2),
    "qkvz": (1, 3, 1, 1, 1),
    "u": (1, 1, 1, 1, 1),
}


def on_device(
    tokens,
    seq_lengths,
    owner_order,
    gain_attn,
    w_input,
    w_step,
    step_bias,
    decay_log,
    skip_scale,
    conv_weight,
    conv_bias,
    gain_ssm,
    w_output,
    gain_ffn,
    w_gate_up,
    w_down,
    cotangent,
):
    input_rows = tokens.shape[0]
    shard = lax.axis_index("shard")
    flow = Flow()
    f32 = lambda v: v.astype(jnp.float32)

    slot_input = flow.add(weight_stream(w_input))
    small_args = (gain_attn, w_step, step_bias, decay_log, skip_scale, conv_weight, conv_bias, gain_ssm, gain_ffn)
    small_dims = (0, 0, 0, 0, 0, 1, 0, 0, 0)
    slot_small = flow.add(small_stream(jnp.concatenate([a.reshape(-1) for a in small_args])))
    source, position, limit, target = group_tables(seq_lengths[0], owner_order[0], input_rows, shard)
    cosine, sine = rope_tables(position)
    source, position, tokens, cosine, sine, w_output = flow.step((source, position, tokens, cosine, sine, w_output))
    slot_tokens = flow.add(rows_stream(tokens))
    source, position, w_output, w_gate_up, w_down, cotangent = flow.step(
        (source, position, w_output, w_gate_up, w_down, cotangent)
    )
    slot_output = flow.add(weight_stream(w_output, 2))
    w_gate_up_all = lax.all_gather(w_gate_up, "shard", axis=0, tiled=True)
    w_down_all = lax.all_gather(w_down, "shard", axis=0, tiled=True)
    source, position, cotangent = flow.until([slot_tokens, slot_input, slot_small], (source, position, cotangent), True)

    gain_attn_all, w_step_all, step_bias_all, decay_all, skip_all, conv_w_all, conv_b_all, gain_ssm_all, gain_ffn_all = (
        unpack_small(slot_small["result"], [a.shape for a in small_args], small_dims)
    )
    gain_attn_f, gain_ssm_f, gain_ffn_f = f32(gain_attn_all), f32(gain_ssm_all), f32(gain_ffn_all)
    conv_w_f, conv_b_f = f32(conv_w_all), f32(conv_b_all)
    skip_lanes = jnp.repeat(f32(skip_all), SSM_HD)[None]
    pieces, owners = slot_tokens["result"]
    own = f32(pick_rows(pieces, owners * input_rows, source))
    w_input_all = slot_input["result"]

    normed = rms_norm(own, gain_attn_f).astype(jnp.bfloat16)
    projected = dot(normed, w_input_all)
    step_pre = dot(normed, w_step_all) + f32(step_bias_all)
    step = jax.nn.softplus(step_pre)
    rate = -jnp.exp(f32(decay_all))
    cum = to_lanes(running_sum(step * rate, False), 0.0)
    tables = (cum, cum.T)
    step_lanes = to_lanes(step, 1.0)
    projected, normed = flow.step((projected, normed))
    conv_out, low = conv_forward(projected, position, conv_w_f, conv_b_f, step_lanes)
    inner_x = conv_out[:, :INNER]
    low, cotangent, projected = flow.step((low, cotangent, projected))
    slot_cot = flow.add(rows_stream(cotangent, 2))
    attn_out, logs = attention_forward(limit, projected, cosine, sine)
    attn_out, low = flow.step((attn_out, low))
    ssd_out = ssd_forward(limit, low, tables)
    ssd_out, projected = flow.until([slot_output], (ssd_out, projected), True)
    w_output_all = slot_output["result"]
    gate_z = projected[:, QUERY_KEY_VALUE : QUERY_KEY_VALUE + INNER]
    ssm_y = ssd_out + skip_lanes * inner_x
    ssm_out = gated_norm(ssm_y, gate_z, gain_ssm_f).astype(jnp.bfloat16)
    joined = jnp.concatenate([attn_out, ssm_out], 1)
    middle = own + dot(joined, w_output_all)
    normed_ffn = rms_norm(middle, gain_ffn_f).astype(jnp.bfloat16)
    gate_up = dot(normed_ffn, w_gate_up_all)
    hidden = swiglu(gate_up).astype(jnp.bfloat16)
    gate_up, hidden = flow.until([slot_cot], (gate_up, hidden))
    pieces, owners = slot_cot["result"]
    cot = pick_rows(pieces, owners * input_rows, source)

    def back(left, weight):
        return lax.dot_general(left, weight, (((1,), (1,)), ((), ())), preferred_element_type=jnp.float32)

    slots = {}
    slots["down"] = [flow.add(reduce_stream(hidden, cot, WAITS["down"]))]
    grad_hidden = back(cot, w_down_all)
    grad_gate_up = jax.vjp(swiglu, gate_up)[1](grad_hidden)[0].astype(jnp.bfloat16)
    grad_gate_up = flow.step(grad_gate_up)
    half = grad_gate_up.shape[1] // 2
    slots["gate_up"] = [flow.add(reduce_stream(normed_ffn, grad_gate_up[:, :half], WAITS["gate"]))]
    grad_normed_ffn = back(grad_gate_up, w_gate_up_all)
    grad_middle_norm, grad_gain_ffn = jax.vjp(rms_norm, middle, gain_ffn_f)[1](grad_normed_ffn)
    grad_middle = f32(cot) + grad_middle_norm
    grad_middle, grad_gate_up = flow.step((grad_middle, grad_gate_up))
    slots["gate_up"].append(flow.add(reduce_stream(normed_ffn, grad_gate_up[:, half:], WAITS["up"])))
    middle_low = grad_middle.astype(jnp.bfloat16)
    grad_joined = back(middle_low, w_output_all)
    grad_attn = grad_joined[:, : QUERY_HEADS * HEAD_SIZE].astype(jnp.bfloat16)
    grad_ssm_out = grad_joined[:, QUERY_HEADS * HEAD_SIZE :]
    grad_ssm_y, grad_z, grad_gain_ssm = jax.vjp(gated_norm, ssm_y, gate_z, gain_ssm_f)[1](grad_ssm_out)
    grad_z_low = grad_z.astype(jnp.bfloat16)
    grad_y_low = grad_ssm_y.astype(jnp.bfloat16)
    grad_ssm_y, grad_z_low, grad_attn, middle_low, grad_y_low = flow.step(
        (grad_ssm_y, grad_z_low, grad_attn, middle_low, grad_y_low)
    )
    slots["output"] = [flow.add(reduce_stream(joined, middle_low, WAITS["output"]))]
    first = attention_backward(0, limit, projected, cosine, sine, grad_attn, logs)
    first, grad_attn = flow.step((first, grad_attn))
    second = attention_backward(1, limit, projected, cosine, sine, grad_attn, logs, first[1])
    second, grad_y_low, grad_z_low = flow.step((second, grad_y_low, grad_z_low))
    qkvz = jnp.concatenate([first[0], second[0], second[1], grad_z_low], 1)
    slots["input"] = [flow.add(reduce_stream(normed, qkvz, WAITS["qkvz"]))]
    upper = ssd_backward(0, limit, low, grad_y_low, tables)
    upper, grad_y_low, hidden = flow.step((upper, grad_y_low, hidden))
    block_low = (middle + dot(hidden, w_down_all)).astype(jnp.bfloat16)
    lower = ssd_backward(1, limit, low, grad_y_low, tables, upper[1])
    lower, upper, block_low = flow.step((lower, upper, block_low))
    block_all = lax.all_gather(block_low, "shard", axis=0, tiled=True)
    conv_args = (projected, position, conv_w_f, conv_b_f, step_lanes, skip_lanes)
    conv_upper = conv_backward(0, *conv_args, upper[0], grad_ssm_y, ssd_out, low, lower[2])
    conv_upper, lower = flow.step((conv_upper, lower))
    conv_lower = conv_backward(1, *conv_args, lower[0], grad_ssm_y, ssd_out, low, lower[2])
    conv_upper, conv_lower = flow.step((conv_upper, conv_lower))
    grad_u_low = jnp.concatenate([conv_upper[0], conv_lower[0]], 1)
    grad_taps = jnp.concatenate([conv_upper[1], conv_lower[1]], 1)
    head_parts = conv_upper[2] + conv_lower[2]
    slots["input"].append(flow.add(reduce_stream(normed, grad_u_low, WAITS["u"], True)))
    last = slots["input"][-1:]
    grad_projected = jnp.concatenate([qkvz, grad_u_low], 1)
    heads_of = lambda offset: head_parts[:, offset : offset + SSM_HEADS]
    grad_skip = jnp.sum(heads_of(64), 0)
    grad_inc = running_sum(heads_of(32), True)
    grad_step = heads_of(0) + grad_inc * rate
    grad_decay = jnp.sum(grad_inc * step, 0) * rate
    grad_step_pre = grad_step * jax.nn.sigmoid(step_pre)
    grad_step_bias = jnp.sum(grad_step_pre, 0)
    step_low = grad_step_pre.astype(jnp.bfloat16)
    grad_w_step = transposed_dot(normed, step_low)
    small_grads = (
        grad_w_step,
        grad_step_bias,
        grad_decay,
        grad_skip,
        grad_taps[:TAPS],
        grad_taps[TAPS],
        grad_gain_ssm,
        grad_gain_ffn,
    )
    grad_projected, step_low = flow.step((grad_projected, step_low))
    flat = jnp.concatenate([g.reshape(-1) for g in small_grads])
    flat = jnp.pad(flat, (0, -flat.shape[0] % 1024)).reshape(-1, SIDE)
    slot_flat = flow.add(butterfly_stream(flat))
    grad_normed = back(grad_projected, w_input_all) + back(step_low, w_step_all)
    grad_tokens_norm, grad_gain_attn = jax.vjp(rms_norm, own, gain_attn_f)[1](grad_normed)
    grad_low = (grad_middle + grad_tokens_norm).astype(jnp.bfloat16)
    replica = lax.axis_index("rep").reshape(1).astype(jnp.int32)
    line = lax.axis_size("rep") // 2
    held = {}

    def widen(name):
        parts = [line if slot in last else 1 for slot in slots[name]]
        held[name] = widen_rows([slot["result"] for slot in slots[name]], parts, replica)

    grad_low, gain_late, block_all = flow.step((grad_low, grad_gain_attn.reshape(-1, SIDE), block_all))
    slot_grad = flow.add(rows_stream(grad_low))
    slot_late = flow.add(butterfly_stream(gain_late))
    queue = ["late", "small", "down", "gate_up", "block", "output", "tokens", "input"]

    def small_outputs():
        summed = slot_flat["result"].reshape(-1)
        offset = 0
        blocks = []
        for i, grad in zip(SMALL, small_grads):
            block = summed[offset : offset + grad.size].reshape(grad.shape)
            offset += grad.size
            blocks.append(own_block(block, 1 if i == 6 else 0))
        return blocks

    def work(limit):
        for name in list(queue):
            if limit == 0:
                return
            if name in ("late", "small"):
                if not (slot_late if name == "late" else slot_flat)["done"]:
                    continue
                held[name] = small_outputs() if name == "small" else own_block(slot_late["result"].reshape(-1), 0)
                limit += 1
            elif name == "block":
                held["block"] = pick_rows([block_all], jnp.zeros((1,), jnp.int32), target)
            elif name == "tokens":
                if not slot_grad["done"]:
                    continue
                pieces, owners = slot_grad["result"]
                held["tokens"] = pick_rows(pieces, owners * input_rows, target)
            else:
                if not all(slot["done"] for slot in slots[name]):
                    continue
                widen(name)
            queue.remove(name)
            limit -= 1

    boundary = 0
    while flow.live:
        work(PLAN[boundary] if boundary < len(PLAN) else 2)
        held = flow.step(held, [slot for slot in flow.live if slot is not slot_grad] if boundary == 0 else None)
        boundary += 1
    work(len(queue))
    block_out, grad_tokens, widened = held["block"], held["tokens"], held
    outs = [None] * 13
    outs[0] = held["late"]
    for i, name in enumerate(SMALL):
        outs[name] = held["small"][i]
    for i, name in ((1, "input"), (9, "output"), (11, "gate_up"), (12, "down")):
        outs[i] = widened[name]
    return (block_out, grad_tokens, *outs)


def solution(mesh):
    placed = (
        P(("rep", "shard"), None),
        P("rep", None),
        P("rep", None),
        P("shard"),
        P("shard", None),
        P("shard", None),
        P("shard"),
        P("shard"),
        P("shard"),
        P(None, "shard"),
        P("shard"),
        P("shard"),
        P("shard", None),
        P("shard"),
        P("shard", None),
        P("shard", None),
        P(("rep", "shard"), None),
    )
    return jax.shard_map(
        on_device,
        mesh=mesh,
        in_specs=placed,
        out_specs=(
            P(("rep", "shard"), None),
            P(("rep", "shard"), None),
            P("shard"),
            P("shard", None),
            P("shard", None),
            P("shard"),
            P("shard"),
            P("shard"),
            P(None, "shard"),
            P("shard"),
            P("shard"),
            P("shard", None),
            P("shard"),
            P("shard", None),
            P("shard", None),
        ),
        check_vma=False,
    )
```

```python
from functools import partial
import math

import jax
import jax.numpy as jnp
from jax import lax
from jax.experimental import pallas as pl
from jax.experimental.pallas import tpu as pltpu
from jax.sharding import PartitionSpec as P

QUERY_HEADS = 8
KEY_VALUE_HEADS = 2
HEAD_SIZE = 64
SSM_HEADS = 24
SSM_HD = 64
STATE = 128
INNER = 1536
QUERY_KEY_VALUE = 768
TAPS = 4

EPS = 1e-05
ROPE_BASE = 100000000000.0
SIDE = 128
QUAD = 4
LOW = -1e30
SCALE = HEAD_SIZE ** (-0.5)


def causal_bias(limit, rows, row0, cols):
    i = lax.broadcasted_iota(jnp.int32, (rows, cols), 0) + row0
    j = lax.broadcasted_iota(jnp.int32, (rows, cols), 1)
    seen = (j <= i) & ((j >= limit) | (i < limit))
    return jnp.where(seen, 0.0, LOW)


def contract_last(left, right):
    return lax.dot_general(left, right, (((1,), (1,)), ((), ())), preferred_element_type=jnp.float32)


def contract_first(left, right):
    return lax.dot_general(left, right, (((0,), (0,)), ((), ())), preferred_element_type=jnp.float32)


def halves(pair):
    lane = lax.broadcasted_iota(jnp.int32, pair.shape, 1)
    zero = jnp.zeros_like(pair)
    return (jnp.where(lane < HEAD_SIZE, pair, zero), jnp.where(lane >= HEAD_SIZE, pair, zero))


def four_lanes(values, step):
    return pltpu.roll(values, lax.rem(SIDE - QUAD * step, SIDE), 1)


def ssd_forward_kernel(limit_ref, c_ref, b_ref, x_ref, cum_col_ref, cum_row_ref, out_ref, inter, bias):
    count = c_ref.shape[0]

    @pl.when(pl.program_id(0) == 0)
    def _():
        inter[...] = contract_last(c_ref[...], b_ref[...])
        bias[...] = causal_bias(limit_ref[0], count, 0, count)

    step = pl.program_id(0)
    cum_col = four_lanes(cum_col_ref[...], step)
    cum_row = cum_row_ref[pl.ds(pl.multiple_of(step // 2 * 8, 8), 8), :]
    cum_row = jnp.where(step % 2 == 0, cum_row[:QUAD], cum_row[QUAD:])
    for pair in range(QUAD // 2):
        lanes = slice(pair * SIDE, (pair + 1) * SIDE)
        sides = halves(x_ref[:, lanes])
        for top in range(0, count, SIDE):
            rows = slice(top, top + SIDE)
            seen = top + SIDE
            total = None
            for half in range(2):
                h = pair * 2 + half
                gap = cum_col[rows, h : h + 1] - cum_row[h : h + 1, :seen]
                mixer = (inter[rows, :seen] * jnp.exp(gap + bias[rows, :seen])).astype(jnp.bfloat16)
                part = jnp.dot(mixer, sides[half][:seen], preferred_element_type=jnp.float32)
                total = part if total is None else total + part
            out_ref[rows, lanes] = total


def ssd_forward(limit, low, tables):
    count = low.shape[0]
    steps = SSM_HEADS // QUAD
    b_spec = pl.BlockSpec((count, STATE), lambda i: (0, INNER // STATE))
    c_spec = pl.BlockSpec((count, STATE), lambda i: (0, INNER // STATE + 1))
    return pl.pallas_call(
        ssd_forward_kernel,
        grid=(steps,),
        out_shape=jax.ShapeDtypeStruct((count, INNER), jnp.float32),
        in_specs=[
            pl.BlockSpec(memory_space=pltpu.SMEM),
            c_spec,
            b_spec,
            pl.BlockSpec((count, QUAD * HEAD_SIZE), lambda i: (0, i)),
            pl.BlockSpec((count, SIDE), lambda i: (0, 0)),
            pl.BlockSpec((SIDE, count), lambda i: (0, 0)),
        ],
        out_specs=pl.BlockSpec((count, QUAD * HEAD_SIZE), lambda i: (0, i)),
        scratch_shapes=[pltpu.VMEM((count, count), jnp.float32)] * 2,
        name="ssd_forward",
    )(limit, low, low, low, *tables)


def ssd_backward_kernel(part, limit_ref, c_ref, b_ref, x_ref, dy_ref, cum_col_ref, cum_row_ref, *refs):
    if part == 0:
        z_ref, total, inter, bias = refs
    else:
        held_ref, z_ref, total, gbc_ref, inter, bias = refs
    count = c_ref.shape[0]

    @pl.when(pl.program_id(0) == 0)
    def _():
        inter[...] = contract_last(c_ref[...], b_ref[...])
        bias[...] = causal_bias(limit_ref[0], count, 0, count)
        total[...] = jnp.zeros_like(total) if part == 0 else held_ref[...]

    step = pl.program_id(0) + part * (SSM_HEADS // QUAD // 2)
    cum_col = four_lanes(cum_col_ref[...], step)
    cum_row = cum_row_ref[pl.ds(pl.multiple_of(step // 2 * 8, 8), 8), :]
    cum_row = jnp.where(step % 2 == 0, cum_row[:QUAD], cum_row[QUAD:])
    for pair in range(QUAD // 2):
        lanes = slice(pair * SIDE, (pair + 1) * SIDE)
        x_pair = x_ref[:, lanes]
        sides = halves(dy_ref[:, lanes])
        for top in reversed(range(0, count, SIDE)):
            rows = slice(top, top + SIDE)
            seen = top + SIDE
            grad = None
            back = None
            for half in range(2):
                h = pair * 2 + half
                gap = cum_col[rows, h : h + 1] - cum_row[h : h + 1, :seen]
                decay = jnp.exp(gap + bias[rows, :seen])
                mixer = (inter[rows, :seen] * decay).astype(jnp.bfloat16)
                grad_mixer = contract_last(sides[half][rows], x_pair[:seen])
                piece = grad_mixer * decay
                grad = piece if grad is None else grad + piece
                piece = contract_first(mixer, sides[half][rows])
                back = piece if back is None else back + piece
            total[rows, :seen] += grad
            if seen == count:
                z_ref[:, lanes] = back
            else:
                z_ref[:seen, lanes] += back

    if part == 1:

        @pl.when(pl.program_id(0) == pl.num_programs(0) - 1)
        def _():
            low = total[...].astype(jnp.bfloat16)
            gbc_ref[:, :STATE] = contract_first(low, c_ref[...])
            gbc_ref[:, STATE:] = jnp.dot(low, b_ref[...], preferred_element_type=jnp.float32)


def ssd_backward(part, limit, low, grad_y, tables, held=None):
    count = low.shape[0]
    steps = SSM_HEADS // QUAD // 2
    b_spec = pl.BlockSpec((count, STATE), lambda i: (0, INNER // STATE))
    c_spec = pl.BlockSpec((count, STATE), lambda i: (0, INNER // STATE + 1))
    quad = pl.BlockSpec((count, QUAD * HEAD_SIZE), lambda i: (0, i + part * steps))
    square = pl.BlockSpec((count, count), lambda i: (0, 0))
    out_shape = [
        jax.ShapeDtypeStruct((count, INNER // 2), jnp.float32),
        jax.ShapeDtypeStruct((count, count), jnp.float32),
    ]
    out_specs = [pl.BlockSpec((count, QUAD * HEAD_SIZE), lambda i: (0, i)), square]
    if part == 1:
        out_shape.append(jax.ShapeDtypeStruct((count, 2 * STATE), jnp.float32))
        out_specs.append(pl.BlockSpec((count, 2 * STATE), lambda i: (0, 0)))
    more = [] if held is None else [held]
    return pl.pallas_call(
        partial(ssd_backward_kernel, part),
        grid=(steps,),
        out_shape=tuple(out_shape),
        in_specs=[
            pl.BlockSpec(memory_space=pltpu.SMEM),
            c_spec,
            b_spec,
            quad,
            quad,
            pl.BlockSpec((count, SIDE), lambda i: (0, 0)),
            pl.BlockSpec((SIDE, count), lambda i: (0, 0)),
        ]
        + [square] * len(more),
        out_specs=tuple(out_specs),
        scratch_shapes=[pltpu.VMEM((count, count), jnp.float32)] * 2,
        name="ssd_backward",
    )(limit, low, low, low, grad_y, *tables, *more)


def turn(values, cosine, sine):
    lane = lax.broadcasted_iota(jnp.int32, values.shape, 1) % HEAD_SIZE
    width = values.shape[1]
    ahead = pltpu.roll(values, width - HEAD_SIZE // 2, 1)
    behind = pltpu.roll(values, HEAD_SIZE // 2, 1)
    other = jnp.where(lane < HEAD_SIZE // 2, ahead, behind)
    return values * cosine + other * sine


def both_sides(pair, step):
    lane = lax.broadcasted_iota(jnp.int32, pair.shape, 1)
    mine = jnp.where((lane >= HEAD_SIZE) == (step > 0), pair, jnp.zeros_like(pair))
    return (mine + pltpu.roll(mine, HEAD_SIZE, 1)).astype(jnp.bfloat16)


def attention_forward_kernel(limit_ref, q_ref, k_ref, v_ref, cos_ref, sin_ref, out_ref, log_ref, bias):
    count = k_ref.shape[0]
    step = pl.program_id(0)

    @pl.when(step == 0)
    def _():
        bias[...] = causal_bias(limit_ref[0], count, 0, count)

    cosine, sine = cos_ref[...], sin_ref[...]
    key = both_sides(turn(k_ref[...], cosine, sine), step)
    value_sides = halves(both_sides(v_ref[...], step))
    for pair in range(2):
        lanes = slice(pair * SIDE, (pair + 1) * SIDE)
        sides = halves(turn(q_ref[:, lanes], cosine, sine).astype(jnp.bfloat16) * SCALE)
        for top in range(0, count, SIDE):
            rows = slice(top, top + SIDE)
            seen = top + SIDE
            total = None
            for half in range(2):
                score = contract_last(sides[half][rows], key[:seen]) + bias[rows, :seen]
                largest = jnp.max(score, -1, keepdims=True)
                raised = jnp.exp(score - largest)
                mass = jnp.sum(raised, -1, keepdims=True)
                weights = (raised * (1.0 / mass)).astype(jnp.bfloat16)
                part = jnp.dot(weights, value_sides[half][:seen], preferred_element_type=jnp.float32)
                total = part if total is None else total + part
                h = pair * 2 + half
                log_ref[0, rows, h : h + 1] = largest + jnp.log(mass)
            out_ref[rows, lanes] = total.astype(jnp.bfloat16)


def attention_specs(count):
    wide = pl.BlockSpec((count, 2 * SIDE), lambda i: (0, i))
    whole = pl.BlockSpec((count, SIDE), lambda i: (0, 0))
    keys = pl.BlockSpec((count, SIDE), lambda i: (0, QUERY_HEADS * HEAD_SIZE // SIDE))
    values = pl.BlockSpec((count, SIDE), lambda i: (0, QUERY_HEADS * HEAD_SIZE // SIDE + 1))
    logs = pl.BlockSpec((1, count, QUAD), lambda i: (i, 0, 0))
    return wide, whole, keys, values, logs


def attention_forward(limit, projected, cosine, sine):
    count = projected.shape[0]
    wide, whole, keys, values, logs = attention_specs(count)
    return pl.pallas_call(
        attention_forward_kernel,
        grid=(KEY_VALUE_HEADS,),
        out_shape=(
            jax.ShapeDtypeStruct((count, QUERY_HEADS * HEAD_SIZE), jnp.bfloat16),
            jax.ShapeDtypeStruct((KEY_VALUE_HEADS, count, QUAD), jnp.float32),
        ),
        in_specs=[pl.BlockSpec(memory_space=pltpu.SMEM), wide, keys, values, whole, whole],
        out_specs=(wide, logs),
        scratch_shapes=[pltpu.VMEM((count, count), jnp.float32)],
        name="attention_forward",
    )(limit, projected, projected, projected, cosine, sine)


def attention_backward_kernel(step, limit_ref, q_ref, k_ref, v_ref, cos_ref, sin_ref, go_ref, log_ref, *refs):
    (gq_ref, gkv_ref), (bias, gk, gv) = refs[-5:-3], refs[-3:]
    count = k_ref.shape[0]
    bias[...] = causal_bias(limit_ref[0], count, 0, count)
    cosine, sine = cos_ref[...], sin_ref[...]
    key = both_sides(turn(k_ref[...], cosine, sine), step)
    value = both_sides(v_ref[...], step)
    key_sides = halves(key)
    gk[...] = jnp.zeros_like(gk)
    gv[...] = jnp.zeros_like(gv)
    for pair in range(2):
        lanes = slice(pair * SIDE, (pair + 1) * SIDE)
        q_sides = halves(turn(q_ref[:, lanes], cosine, sine).astype(jnp.bfloat16) * SCALE)
        go_sides = halves(go_ref[:, lanes])
        for top in range(0, count, SIDE):
            rows = slice(top, top + SIDE)
            seen = top + SIDE
            total = None
            for half in range(2):
                h = pair * 2 + half
                score = contract_last(q_sides[half][rows], key[:seen])
                weights = jnp.exp(score + bias[rows, :seen] - log_ref[0, rows, h : h + 1])
                grad = contract_last(go_sides[half][rows], value[:seen])
                inner = jnp.sum(grad * weights, -1, keepdims=True)
                low = (weights * (grad - inner)).astype(jnp.bfloat16)
                part = jnp.dot(low, key_sides[half][:seen], preferred_element_type=jnp.float32)
                total = part if total is None else total + part
                gk[:seen, :] += contract_first(low, q_sides[half][rows])
                gv[:seen, :] += contract_first(weights.astype(jnp.bfloat16), go_sides[half][rows])
            gq_ref[rows, lanes] = turn(total * SCALE, cosine[rows], -sine[rows]).astype(jnp.bfloat16)
    lane = lax.broadcasted_iota(jnp.int32, (count, SIDE), 1)
    mine = (lane >= HEAD_SIZE) == (step > 0)
    for place, part in enumerate((gk, gv)):
        summed = part[...] + pltpu.roll(part[...], HEAD_SIZE, 1)
        if place == 0:
            summed = turn(summed, cosine, -sine)
        lanes = slice(place * SIDE, (place + 1) * SIDE)
        if step > 0:
            summed = jnp.where(mine, summed, refs[0][:, lanes].astype(jnp.float32))
        gkv_ref[:, lanes] = summed.astype(jnp.bfloat16)


def attention_backward(step, limit, projected, cosine, sine, grad_out, logs_in, other=None):
    count = projected.shape[0]
    _, whole, keys, values, _ = attention_specs(count)
    at = lambda spec: pl.BlockSpec(spec.block_shape, lambda i: spec.index_map(step))
    wide, _, _, _, logs = attention_specs(count)
    both = pl.BlockSpec((count, 2 * SIDE), lambda i: (0, 0))
    more = [] if other is None else [other]
    return pl.pallas_call(
        partial(attention_backward_kernel, step),
        grid=(1,),
        out_shape=(
            jax.ShapeDtypeStruct((count, 2 * SIDE), jnp.bfloat16),
            jax.ShapeDtypeStruct((count, 2 * SIDE), jnp.bfloat16),
        ),
        in_specs=[pl.BlockSpec(memory_space=pltpu.SMEM), at(wide), keys, values, whole, whole, at(wide), at(logs)]
        + [both] * len(more),
        out_specs=(both, both),
        scratch_shapes=[
            pltpu.VMEM((count, count), jnp.float32),
            pltpu.VMEM((count, SIDE), jnp.float32),
            pltpu.VMEM((count, SIDE), jnp.float32),
        ],
        name="attention_backward",
    )(limit, projected, projected, projected, cosine, sine, grad_out, logs_in, *more)


BLOCK = QUAD * HEAD_SIZE


TILE = 128
HALO = 8


def conv_taps(u_ref, top, place, weight_ref, bias_ref, lanes):
    mixed = bias_ref[:, lanes] + u_ref[HALO + top : HALO + top + TILE, lanes] * weight_ref[TAPS - 1 : TAPS, lanes]
    for back in range(1, TAPS):
        shifted = u_ref[HALO + top - back : HALO + top - back + TILE, lanes]
        mixed = mixed + jnp.where(place >= back, shifted, 0.0) * weight_ref[TAPS - 1 - back : TAPS - back, lanes]
    return mixed


def conv_forward_kernel(u_ref, place_ref, weight_ref, bias_ref, step_ref, out_ref, low_ref, held):
    count = u_ref.shape[0]
    held[:HALO, :] = jnp.zeros((HALO, BLOCK), jnp.float32)
    held[HALO:, :] = u_ref[...]
    lane = lax.broadcasted_iota(jnp.int32, (TILE, SIDE), 1)
    scale = four_lanes(step_ref[...], pl.program_id(0))
    for side in range(BLOCK // SIDE):
        lanes = slice(side * SIDE, (side + 1) * SIDE)
        for top in range(0, count, TILE):
            rows = slice(top, top + TILE)
            mixed = conv_taps(held, top, place_ref[rows], weight_ref, bias_ref, lanes)
            out = mixed / (1.0 + jnp.exp(-mixed))
            out_ref[rows, lanes] = out
            first, second = scale[rows, 2 * side : 2 * side + 1], scale[rows, 2 * side + 1 : 2 * side + 2]
            low_ref[rows, lanes] = (out * jnp.where(lane < HEAD_SIZE, first, second)).astype(jnp.bfloat16)


def conv_specs(count, begin=0):
    column = lambda i: (0, i + begin)
    first = (QUERY_KEY_VALUE + INNER) // BLOCK + begin
    return (
        pl.BlockSpec((count, BLOCK), lambda i: (0, first + i)),
        pl.BlockSpec((count, 1), lambda i: (0, 0)),
        pl.BlockSpec((TAPS, BLOCK), column),
        pl.BlockSpec((1, BLOCK), column),
        pl.BlockSpec((count, SIDE), lambda i: (0, 0)),
        pl.BlockSpec((count, BLOCK), column),
    )


def conv_forward(projected, position, weight, bias, step_quads):
    count, width = projected.shape[0], weight.shape[1]
    u, place, taps, row, quads, block = conv_specs(count)
    return pl.pallas_call(
        conv_forward_kernel,
        grid=(width // BLOCK,),
        out_shape=(
            jax.ShapeDtypeStruct((count, width), jnp.float32),
            jax.ShapeDtypeStruct((count, width), jnp.bfloat16),
        ),
        in_specs=[u, place, taps, row, quads],
        out_specs=(block, block),
        scratch_shapes=[pltpu.VMEM((HALO + count, BLOCK), jnp.float32)],
        name="conv_forward",
    )(projected, position[:, None], weight, bias[None], step_quads)


def head_sums(values, chosen):
    high = values.astype(jnp.bfloat16)
    low = (values - high.astype(jnp.float32)).astype(jnp.bfloat16)
    return jnp.dot(high, chosen, preferred_element_type=jnp.float32) + jnp.dot(
        low, chosen, preferred_element_type=jnp.float32
    )


def conv_backward_kernel(
    first, u_ref, place_ref, weight_ref, bias_ref, step_ref, skip_ref, z_ref, gy_ref, y_ref, low_ref, gbc_ref,
    gu_ref, gw_ref, heads_ref, held, grads,
):
    count = u_ref.shape[0]
    step = pl.program_id(0) + first
    inner = step < INNER // BLOCK
    scale = four_lanes(step_ref[...], step)
    held[:HALO, :] = jnp.zeros((HALO, BLOCK), jnp.float32)
    held[HALO:, :] = u_ref[...]
    lane = lax.broadcasted_iota(jnp.int32, (TILE, SIDE), 1)

    @pl.when(pl.program_id(0) == 0)
    def _():
        heads_ref[...] = jnp.zeros_like(heads_ref)

    for side in range(BLOCK // SIDE):
        lanes = slice(side * SIDE, (side + 1) * SIDE)
        sums = [None] * (TAPS + 1)
        head = lax.broadcasted_iota(jnp.int32, (SIDE, SIDE), 0) // HEAD_SIZE + 2 * side + QUAD * step
        column = lax.broadcasted_iota(jnp.int32, (SIDE, SIDE), 1)
        chosen = [(head + offset == column).astype(jnp.bfloat16) for offset in (0, 32, 64)]
        for back in range(1, TAPS):
            grads[back - 1, count:, lanes] = jnp.zeros((HALO, SIDE), jnp.float32)
        for top in range(0, count, TILE):
            rows = slice(top, top + TILE)
            place = place_ref[rows]
            mixed = conv_taps(held, top, place, weight_ref, bias_ref, lanes)
            gate = 1.0 / (1.0 + jnp.exp(-mixed))
            out = mixed * gate
            z, gy = z_ref[rows, lanes], gy_ref[rows, lanes]
            first, second = scale[rows, 2 * side : 2 * side + 1], scale[rows, 2 * side + 1 : 2 * side + 2]
            grad = z * jnp.where(lane < HEAD_SIZE, first, second) + skip_ref[:, lanes] * gy
            grad = jnp.where(inner, grad, gbc_ref[rows, lanes])
            gy_low = gy.astype(jnp.bfloat16).astype(jnp.float32)
            cum = gy_low * y_ref[rows, lanes] - low_ref[rows, lanes].astype(jnp.float32) * z
            part = head_sums(z * out, chosen[0]) + head_sums(cum, chosen[1]) + head_sums(gy * out, chosen[2])
            heads_ref[rows, :] += jnp.where(inner, part, 0.0)
            grad = grad * (gate + out * (1.0 - gate))
            parts = [jnp.sum(grad, 0, keepdims=True)]
            parts.append(jnp.sum(grad * held[HALO + top : HALO + top + TILE, lanes], 0, keepdims=True))
            grads[TAPS - 1, rows, lanes] = grad * weight_ref[TAPS - 1 : TAPS, lanes]
            for back in range(1, TAPS):
                seen = jnp.where(place >= back, grad, 0.0)
                shifted = held[HALO + top - back : HALO + top - back + TILE, lanes]
                parts.append(jnp.sum(seen * shifted, 0, keepdims=True))
                grads[back - 1, rows, lanes] = seen * weight_ref[TAPS - 1 - back : TAPS - back, lanes]
            sums = [p if s is None else s + p for s, p in zip(sums, parts)]
        gw_ref[:, lanes] = jnp.zeros((8, SIDE), jnp.float32)
        gw_ref[TAPS : TAPS + 1, lanes] = sums[0]
        for back in range(TAPS):
            gw_ref[TAPS - 1 - back : TAPS - back, lanes] = sums[1 + back]
        for top in range(0, count, TILE):
            total = grads[TAPS - 1, top : top + TILE, lanes]
            for back in range(1, TAPS):
                total = total + grads[back - 1, top + back : top + back + TILE, lanes]
            gu_ref[top : top + TILE, lanes] = total.astype(jnp.bfloat16)


def conv_backward(part, projected, position, weight, bias, step_lanes, skip, z, grad_y, y, low, grad_bc):
    count = projected.shape[0]
    cut = INNER // BLOCK // 2
    begin, blocks = (0, cut) if part == 0 else (cut, weight.shape[1] // BLOCK - cut)
    u, place, taps, row, lanes, block = conv_specs(count, begin)
    last = INNER // BLOCK - 1
    inner = pl.BlockSpec((count, BLOCK), lambda i: (0, jnp.minimum(i + begin, last)))
    half = pl.BlockSpec((count, BLOCK), lambda i: (0, jnp.minimum(i, cut - 1)))
    skip_row = pl.BlockSpec((1, BLOCK), lambda i: (0, jnp.minimum(i + begin, last)))
    return pl.pallas_call(
        partial(conv_backward_kernel, begin),
        grid=(blocks,),
        out_shape=(
            jax.ShapeDtypeStruct((count, blocks * BLOCK), jnp.bfloat16),
            jax.ShapeDtypeStruct((8, blocks * BLOCK), jnp.float32),
            jax.ShapeDtypeStruct((count, SIDE), jnp.float32),
        ),
        in_specs=[u, place, taps, row, lanes, skip_row, half, inner, inner, block, pl.BlockSpec((count, BLOCK), lambda i: (0, 0))],
        out_specs=(
            pl.BlockSpec((count, BLOCK), lambda i: (0, i)),
            pl.BlockSpec((8, BLOCK), lambda i: (0, i)),
            pl.BlockSpec((count, SIDE), lambda i: (0, 0)),
        ),
        scratch_shapes=[
            pltpu.VMEM((HALO + count, BLOCK), jnp.float32),
            pltpu.VMEM((TAPS, count + HALO, BLOCK), jnp.float32),
        ],
        name="conv_backward",
    )(projected, position[:, None], weight, bias[None], step_lanes, skip, z, grad_y, y, low, grad_bc)


def pick_kernel(shift_ref, wanted_ref, *refs):
    out_ref = refs[-1]
    pieces = refs[:-1]
    count = pieces[0].shape[0]
    place = lax.broadcasted_iota(jnp.int32, (out_ref.shape[0], count), 1)
    total = None
    for n, piece in enumerate(pieces):
        choice = (wanted_ref[...] - shift_ref[n] == place).astype(jnp.bfloat16)
        part = jnp.dot(choice, piece[...], preferred_element_type=jnp.float32)
        total = part if total is None else total + part
    out_ref[...] = total.astype(out_ref.dtype)


def pick_rows(pieces, shifts, wanted):
    vmem = pl.BlockSpec(memory_space=pltpu.VMEM)
    return pl.pallas_call(
        pick_kernel,
        out_shape=jax.ShapeDtypeStruct((wanted.shape[0], pieces[0].shape[1]), pieces[0].dtype),
        in_specs=[pl.BlockSpec(memory_space=pltpu.SMEM), vmem] + [vmem] * len(pieces),
        out_specs=vmem,
        name="pick_rows",
    )(shifts, wanted[:, None], *pieces)


def lay_rows_kernel(place_ref, *refs):
    sems = refs[-1]
    out_ref = refs[-2]
    pieces = refs[:-2]
    copies = []
    for n, piece in enumerate(pieces):
        rows = piece.shape[0]
        start = pl.multiple_of(place_ref[n] * 16, 16)
        copies.append(pltpu.make_async_copy(piece, out_ref.at[pl.ds(start, rows)], sems.at[n]))
    for copy in copies:
        copy.start()
    for copy in copies:
        copy.wait()


def lay_rows(pieces, places):
    rows = sum(piece.shape[0] for piece in pieces)
    hbm = pl.BlockSpec(memory_space=pl.ANY)
    return pl.pallas_call(
        lay_rows_kernel,
        out_shape=jax.ShapeDtypeStruct((rows, pieces[0].shape[1]), pieces[0].dtype),
        in_specs=[pl.BlockSpec(memory_space=pltpu.SMEM)] + [hbm] * len(pieces),
        out_specs=pl.BlockSpec(memory_space=pltpu.VMEM),
        scratch_shapes=[pltpu.SemaphoreType.DMA((len(pieces),))],
        name="lay_rows",
    )(places // 16, *pieces)


def widen_kernel(columns, parts, replica_ref, *refs):
    out_ref = refs[-1]
    near, rest = replica_ref[0] & 1, replica_ref[0] >> 1
    for n, block in enumerate(refs[:-1]):
        left, count = columns[n // 2], parts[n // 2]
        rows = block.shape[0] // count
        for k in range(count):
            place = near ^ (n % 2)
            if count > 1:
                place = place * count + (rest ^ k)
            start = pl.multiple_of(place * rows, rows)
            piece = block[k * rows : (k + 1) * rows, :]
            out_ref[pl.ds(start, rows), left : left + block.shape[1]] = piece.astype(jnp.float32)


def widen_rows(chunks, parts, replica):
    flat = [block for chunk in chunks for block in chunk]
    columns, left = [], 0
    for chunk in chunks:
        columns.append(left)
        left += chunk[0].shape[1]
    rows = 2 * chunks[0][0].shape[0]
    vmem = pl.BlockSpec(memory_space=pltpu.VMEM)
    return pl.pallas_call(
        partial(widen_kernel, tuple(columns), tuple(parts)),
        out_shape=jax.ShapeDtypeStruct((rows, left), jnp.float32),
        in_specs=[pl.BlockSpec(memory_space=pltpu.SMEM)] + [vmem] * len(flat),
        out_specs=vmem,
        name="widen_rows",
    )(replica, *flat)


def swap(values, axis, mask):
    count = lax.axis_size(axis)
    return lax.ppermute(values, axis, [(i, i ^ mask) for i in range(count)])


def take(values, index, dim):
    return lax.dynamic_index_in_dim(values, index, dim, keepdims=False)


def add(first, *others):
    total = first.astype(jnp.float32)
    for other in others:
        total = total + other.astype(jnp.float32)
    return total.astype(jnp.bfloat16)


class Flow:
    def __init__(self):
        self.live = []

    def add(self, stream):
        slot = {"stream": stream, "sent": None, "left": 0, "result": None, "done": False}
        self.live.append(slot)
        self._advance(slot, None)
        return slot

    def _advance(self, slot, value):
        try:
            sent = slot["stream"].send(value)
            slot["sent"], slot["left"] = sent if isinstance(sent, tuple) else (sent, 1)
        except StopIteration as stop:
            slot["result"] = stop.value
            slot["sent"] = None
            slot["done"] = True
            self.live.remove(slot)

    def step(self, values=None, slots=None, force=False):
        slots = [slot for slot in (self.live if slots is None else slots) if not slot["done"]]
        for slot in slots:
            slot["left"] -= 1
        slots = [slot for slot in slots if slot["left"] <= 0 or force]
        values, sent = lax.optimization_barrier((values, [slot["sent"] for slot in slots]))
        for slot, came in zip(slots, sent):
            self._advance(slot, came)
        return values

    def until(self, slots, values=None, alone=False):
        while any(not slot["done"] for slot in slots):
            values = self.step(values, slots if alone else None)
        return values


def rows_stream(piece, wait=1):
    shard = lax.axis_index("shard")
    held = [(0, piece)]
    mask = lax.axis_size("shard") // 2
    first = True
    near = None
    while mask > 1:
        send = [swap(p, "shard", mask) for _, p in held]
        if first:
            send.append(swap(piece, "shard", 1))
        came = yield send, wait
        if first:
            near = came[-1]
            first = False
        held = held + [(k ^ mask, p) for (k, _), p in zip(held, came)]
        mask //= 2
    came = yield [swap(p, "shard", 1) for k, p in held[1:]]
    held = held + [(1, near)] + [(k ^ 1, p) for (k, _), p in zip(held[1:], came)]
    keys = [k for k, _ in held]
    return [p for _, p in held], jnp.stack([shard ^ k for k in keys]).astype(jnp.int32)


def weight_stream(piece, wait=1):
    rows, width = piece.shape
    shard, near = lax.axis_index("shard"), lax.axis_index("rep") & 1
    part = lax.dynamic_slice_in_dim(piece, near * (rows // 2), rows // 2, 0)
    held = [(0, part)]
    both = []
    mask = lax.axis_size("shard") // 2
    beside = None
    while mask > 1:
        send = [swap(p, "shard", mask) for _, p in held]
        if beside is None:
            send.append(swap(piece, "shard", 1))
        came = yield send, wait
        if beside is None:
            beside = came[-1]
        fresh = [(k ^ mask, p) for (k, _), p in zip(held, came)]
        passed = yield [swap(p, "rep", 1) for _, p in fresh] + [swap(p, "shard", 1) for _, p in fresh]
        count = len(fresh)
        for n, (k, p) in enumerate(fresh):
            both.append((k, 0, p))
            both.append((k ^ 1, 0, passed[count + n]))
            both.append((k, 1, passed[n]))
        held = held + fresh
        mask //= 2
    late = [(k, p) for k, side, p in both if side == 1]
    came = yield [swap(p, "shard", 1) for _, p in late]
    both = both + [(k ^ 1, 1, p) for (k, _), p in zip(late, came)]
    pieces = [piece, beside] + [p for _, _, p in both]
    places = [shard * rows, (shard ^ 1) * rows]
    places += [(shard ^ k) * rows + (near ^ side) * (rows // 2) for k, side, _ in both]
    return lay_rows(pieces, jnp.stack(places).astype(jnp.int32))


def transposed_dot(left, right):
    return lax.dot_general(left, right, (((0,), (0,)), ((), ())), preferred_element_type=jnp.float32)


def reduce_stream(left, right, waits=(1, 1, 1, 1, 1), direct=False):
    shards, replicas = lax.axis_size("shard"), lax.axis_size("rep")
    block = left.shape[1] // shards
    shard, near = lax.axis_index("shard"), lax.axis_index("rep") & 1
    core, far = shard & 1, shard >> 1

    def product(r, c, extras=(), half=None):
        start, size = ((far ^ r) * 2 + c) * block, block
        if half is not None:
            size = block // 2
            start = start + half * size
            extras = [x if x.shape[0] == size else lax.dynamic_slice_in_dim(x, half * size, size, 0) for x in extras]
        total = transposed_dot(lax.dynamic_slice_in_dim(left, start, size, 1), right)
        for extra in extras:
            total = total + extra.astype(jnp.float32)
        return total.astype(jnp.bfloat16)

    count = shards // 2
    came = yield [swap(product(r, 1 - core), "shard", 1) for r in range(count)], waits[0]
    extras = [[c] for c in came]
    while count > 1:
        count //= 2
        came = yield [swap(product(r, core, extras[r]), "shard", 2 * count) for r in range(count, 2 * count)], waits[1]
        for n, c in enumerate(came):
            extras[n].append(c)
    came = yield [swap(product(0, core, extras[0], 1 - near), "rep", 1)], waits[2]
    total = product(0, core, [*extras[0], came[0]], near)
    if direct:
        parts = lax.axis_size("rep") // 2
        rest = lax.axis_index("rep") >> 1
        split = total.reshape(parts, -1, right.shape[1])
        others = range(1, parts)
        came = yield [swap(take(split, rest ^ k, 0), "rep", 2 * k) for k in others]
        mine = add(take(split, rest, 0), *came)
        came = yield [swap(mine, "rep", 2 * k) for k in others]
        total = jnp.concatenate([mine, *came], 0)
        came = yield [swap(total, "rep", 1)]
        return total, came[0]
    mask = 2
    while mask < replicas:
        came = yield [swap(total, "rep", mask)], waits[3 if mask == 2 else 4]
        total = add(total, came[0])
        mask *= 2
    came = yield [swap(total, "rep", 1)]
    return total, came[0]


def butterfly_stream(total):
    for axis in ("shard", "rep"):
        mask = 1
        while mask < lax.axis_size(axis):
            came = yield [swap(total, axis, mask)]
            total = total + came[0]
            mask *= 2
    return total


def small_stream(flat):
    held = flat[None]
    mask = 1
    shard = lax.axis_index("shard")
    while mask < lax.axis_size("shard"):
        came = yield [swap(held, "shard", mask)]
        flag = (shard & mask) == 0
        held = jnp.concatenate([jnp.where(flag, held, came[0]), jnp.where(flag, came[0], held)], 0)
        mask *= 2
    return held


def unpack_small(every, shapes, dims):
    parts = every.shape[0]
    outputs = []
    offset = 0
    for shape, dim in zip(shapes, dims):
        length = math.prod(shape)
        block = every[:, offset : offset + length].reshape((parts,) + shape)
        offset += length
        if dim == 0:
            outputs.append(block.reshape((-1,) + shape[1:]))
        else:
            outputs.append(jnp.swapaxes(block, 0, 1).reshape(shape[0], -1))
    return outputs


def own_block(values, dim):
    size = values.shape[dim] // lax.axis_size("shard")
    return lax.dynamic_slice_in_dim(values, lax.axis_index("shard") * size, size, dim)


def group_tables(lengths, order, input_rows, device):
    count = lengths.shape[0]
    slots = jnp.arange(count, dtype=jnp.int32)
    starts = jnp.cumsum(lengths) - lengths
    pick = (order[:, None] == slots[None, :]).astype(jnp.int32)
    owner_len = jnp.sum(pick * lengths[None, :], 1)
    owner_start = jnp.cumsum(owner_len) - owner_len
    owner_src = jnp.sum(pick * starts[None, :], 1)
    first_len = jnp.sum(jnp.where(slots == 2 * device, owner_len, 0))
    first_src = jnp.sum(jnp.where(slots == 2 * device, owner_src, 0))
    second_src = jnp.sum(jnp.where(slots == 2 * device + 1, owner_src, 0))
    local = jnp.arange(input_rows, dtype=jnp.int32)
    segment = (local >= first_len).astype(jnp.int32)
    position = local - segment * first_len
    source = jnp.where(segment > 0, second_src, first_src) + position
    given = device * input_rows + local
    seq_id = jnp.sum((starts[None, :] <= given[:, None]).astype(jnp.int32), 1) - 1
    member = (seq_id[:, None] == slots[None, :]).astype(jnp.int32)
    seq_start = jnp.sum(member * starts[None, :], 1)
    seq_owner_start = jnp.sum(pick * owner_start[:, None], 0)
    target = jnp.sum(member * seq_owner_start[None, :], 1) + given - seq_start
    return (source, position, first_len.reshape(1), target)


def rms_scale(values):
    return lax.rsqrt(jnp.mean(values * values, axis=-1, keepdims=True) + EPS)


def rms_norm(values, gain):
    return values * rms_scale(values) * gain


def rope_tables(position):
    half = HEAD_SIZE // 2
    lane = jnp.arange(SIDE, dtype=jnp.int32)
    ladder = (lane % half).astype(jnp.float32) * (2.0 / HEAD_SIZE)
    angles = position.astype(jnp.float32)[:, None] * jnp.exp(-math.log(ROPE_BASE) * ladder)
    sign = jnp.where(lane % HEAD_SIZE < half, -1.0, 1.0)
    return jnp.cos(angles), jnp.sin(angles) * sign


def gated_norm(ssm_y, gate_z, gain):
    gated = ssm_y * jax.nn.silu(gate_z)
    return gated * rms_scale(gated) * gain


def swiglu(gate_up):
    half = gate_up.shape[1] // 2
    return jax.nn.silu(gate_up[:, :half]) * gate_up[:, half:]


def dot(left, right):
    return jnp.dot(left, right, preferred_element_type=jnp.float32)


def running_sum(values, reverse):
    count = values.shape[0]
    i = lax.broadcasted_iota(jnp.int32, (count, count), 0)
    j = lax.broadcasted_iota(jnp.int32, (count, count), 1)
    chosen = ((i <= j) if reverse else (j <= i)).astype(jnp.float32)
    return jnp.dot(chosen, values, precision=lax.Precision.HIGHEST)


def to_lanes(values, fill):
    count, width = values.shape
    return jnp.concatenate([values, jnp.full((count, SIDE - width), fill, values.dtype)], 1)


SMALL = (2, 3, 4, 5, 6, 7, 8, 10)
PLAN = (0, 2, 2)
WAITS = {
    "down": (1, 2, 1, 1, 1),
    "gate": (1, 2, 1, 1, 2),
    "up": (1, 2, 1, 2, 2),
    "output": (1, 3, 1, 1, 2),
    "qkvz": (1, 3, 1, 1, 1),
    "u": (1, 1, 1, 1, 1),
}


def on_device(
    tokens,
    seq_lengths,
    owner_order,
    gain_attn,
    w_input,
    w_step,
    step_bias,
    decay_log,
    skip_scale,
    conv_weight,
    conv_bias,
    gain_ssm,
    w_output,
    gain_ffn,
    w_gate_up,
    w_down,
    cotangent,
):
    input_rows = tokens.shape[0]
    shard = lax.axis_index("shard")
    flow = Flow()
    f32 = lambda v: v.astype(jnp.float32)

    slot_input = flow.add(weight_stream(w_input))
    small_args = (gain_attn, w_step, step_bias, decay_log, skip_scale, conv_weight, conv_bias, gain_ssm, gain_ffn)
    small_dims = (0, 0, 0, 0, 0, 1, 0, 0, 0)
    slot_small = flow.add(small_stream(jnp.concatenate([a.reshape(-1) for a in small_args])))
    source, position, limit, target = group_tables(seq_lengths[0], owner_order[0], input_rows, shard)
    cosine, sine = rope_tables(position)
    source, position, tokens, cosine, sine, w_output = flow.step((source, position, tokens, cosine, sine, w_output))
    slot_tokens = flow.add(rows_stream(tokens))
    source, position, w_output, w_gate_up, w_down, cotangent = flow.step(
        (source, position, w_output, w_gate_up, w_down, cotangent)
    )
    slot_output = flow.add(weight_stream(w_output, 2))
    w_gate_up_all = lax.all_gather(w_gate_up, "shard", axis=0, tiled=True)
    w_down_all = lax.all_gather(w_down, "shard", axis=0, tiled=True)
    source, position, cotangent = flow.until([slot_tokens, slot_input, slot_small], (source, position, cotangent), True)

    gain_attn_all, w_step_all, step_bias_all, decay_all, skip_all, conv_w_all, conv_b_all, gain_ssm_all, gain_ffn_all = (
        unpack_small(slot_small["result"], [a.shape for a in small_args], small_dims)
    )
    gain_attn_f, gain_ssm_f, gain_ffn_f = f32(gain_attn_all), f32(gain_ssm_all), f32(gain_ffn_all)
    conv_w_f, conv_b_f = f32(conv_w_all), f32(conv_b_all)
    skip_lanes = jnp.repeat(f32(skip_all), SSM_HD)[None]
    pieces, owners = slot_tokens["result"]
    own = f32(pick_rows(pieces, owners * input_rows, source))
    w_input_all = slot_input["result"]

    normed = rms_norm(own, gain_attn_f).astype(jnp.bfloat16)
    projected = dot(normed, w_input_all)
    step_pre = dot(normed, w_step_all) + f32(step_bias_all)
    step = jax.nn.softplus(step_pre)
    rate = -jnp.exp(f32(decay_all))
    cum = to_lanes(running_sum(step * rate, False), 0.0)
    tables = (cum, cum.T)
    step_lanes = to_lanes(step, 1.0)
    projected, normed = flow.step((projected, normed))
    conv_out, low = conv_forward(projected, position, conv_w_f, conv_b_f, step_lanes)
    inner_x = conv_out[:, :INNER]
    low, cotangent, projected = flow.step((low, cotangent, projected))
    slot_cot = flow.add(rows_stream(cotangent, 2))
    attn_out, logs = attention_forward(limit, projected, cosine, sine)
    attn_out, low = flow.step((attn_out, low))
    ssd_out = ssd_forward(limit, low, tables)
    ssd_out, projected = flow.until([slot_output], (ssd_out, projected), True)
    w_output_all = slot_output["result"]
    gate_z = projected[:, QUERY_KEY_VALUE : QUERY_KEY_VALUE + INNER]
    ssm_y = ssd_out + skip_lanes * inner_x
    ssm_out = gated_norm(ssm_y, gate_z, gain_ssm_f).astype(jnp.bfloat16)
    joined = jnp.concatenate([attn_out, ssm_out], 1)
    middle = own + dot(joined, w_output_all)
    normed_ffn = rms_norm(middle, gain_ffn_f).astype(jnp.bfloat16)
    gate_up = dot(normed_ffn, w_gate_up_all)
    hidden = swiglu(gate_up).astype(jnp.bfloat16)
    gate_up, hidden = flow.until([slot_cot], (gate_up, hidden))
    pieces, owners = slot_cot["result"]
    cot = pick_rows(pieces, owners * input_rows, source)

    def back(left, weight):
        return lax.dot_general(left, weight, (((1,), (1,)), ((), ())), preferred_element_type=jnp.float32)

    slots = {}
    slots["down"] = [flow.add(reduce_stream(hidden, cot, WAITS["down"]))]
    grad_hidden = back(cot, w_down_all)
    grad_gate_up = jax.vjp(swiglu, gate_up)[1](grad_hidden)[0].astype(jnp.bfloat16)
    grad_gate_up = flow.step(grad_gate_up)
    half = grad_gate_up.shape[1] // 2
    slots["gate_up"] = [flow.add(reduce_stream(normed_ffn, grad_gate_up[:, :half], WAITS["gate"]))]
    grad_normed_ffn = back(grad_gate_up, w_gate_up_all)
    grad_middle_norm, grad_gain_ffn = jax.vjp(rms_norm, middle, gain_ffn_f)[1](grad_normed_ffn)
    grad_middle = f32(cot) + grad_middle_norm
    grad_middle, grad_gate_up = flow.step((grad_middle, grad_gate_up))
    slots["gate_up"].append(flow.add(reduce_stream(normed_ffn, grad_gate_up[:, half:], WAITS["up"])))
    middle_low = grad_middle.astype(jnp.bfloat16)
    grad_joined = back(middle_low, w_output_all)
    grad_attn = grad_joined[:, : QUERY_HEADS * HEAD_SIZE].astype(jnp.bfloat16)
    grad_ssm_out = grad_joined[:, QUERY_HEADS * HEAD_SIZE :]
    grad_ssm_y, grad_z, grad_gain_ssm = jax.vjp(gated_norm, ssm_y, gate_z, gain_ssm_f)[1](grad_ssm_out)
    grad_z_low = grad_z.astype(jnp.bfloat16)
    grad_y_low = grad_ssm_y.astype(jnp.bfloat16)
    grad_ssm_y, grad_z_low, grad_attn, middle_low, grad_y_low = flow.step(
        (grad_ssm_y, grad_z_low, grad_attn, middle_low, grad_y_low)
    )
    slots["output"] = [flow.add(reduce_stream(joined, middle_low, WAITS["output"]))]
    first = attention_backward(0, limit, projected, cosine, sine, grad_attn, logs)
    first, grad_attn = flow.step((first, grad_attn))
    second = attention_backward(1, limit, projected, cosine, sine, grad_attn, logs, first[1])
    second, grad_y_low, grad_z_low = flow.step((second, grad_y_low, grad_z_low))
    qkvz = jnp.concatenate([first[0], second[0], second[1], grad_z_low], 1)
    slots["input"] = [flow.add(reduce_stream(normed, qkvz, WAITS["qkvz"]))]
    upper = ssd_backward(0, limit, low, grad_y_low, tables)
    upper, grad_y_low, hidden = flow.step((upper, grad_y_low, hidden))
    block_low = (middle + dot(hidden, w_down_all)).astype(jnp.bfloat16)
    lower = ssd_backward(1, limit, low, grad_y_low, tables, upper[1])
    lower, upper, block_low = flow.step((lower, upper, block_low))
    block_all = lax.all_gather(block_low, "shard", axis=0, tiled=True)
    conv_args = (projected, position, conv_w_f, conv_b_f, step_lanes, skip_lanes)
    conv_upper = conv_backward(0, *conv_args, upper[0], grad_ssm_y, ssd_out, low, lower[2])
    conv_upper, lower = flow.step((conv_upper, lower))
    conv_lower = conv_backward(1, *conv_args, lower[0], grad_ssm_y, ssd_out, low, lower[2])
    conv_upper, conv_lower = flow.step((conv_upper, conv_lower))
    grad_u_low = jnp.concatenate([conv_upper[0], conv_lower[0]], 1)
    grad_taps = jnp.concatenate([conv_upper[1], conv_lower[1]], 1)
    head_parts = conv_upper[2] + conv_lower[2]
    slots["input"].append(flow.add(reduce_stream(normed, grad_u_low, WAITS["u"], True)))
    last = slots["input"][-1:]
    grad_projected = jnp.concatenate([qkvz, grad_u_low], 1)
    heads_of = lambda offset: head_parts[:, offset : offset + SSM_HEADS]
    grad_skip = jnp.sum(heads_of(64), 0)
    grad_inc = running_sum(heads_of(32), True)
    grad_step = heads_of(0) + grad_inc * rate
    grad_decay = jnp.sum(grad_inc * step, 0) * rate
    grad_step_pre = grad_step * jax.nn.sigmoid(step_pre)
    grad_step_bias = jnp.sum(grad_step_pre, 0)
    step_low = grad_step_pre.astype(jnp.bfloat16)
    grad_w_step = transposed_dot(normed, step_low)
    small_grads = (
        grad_w_step,
        grad_step_bias,
        grad_decay,
        grad_skip,
        grad_taps[:TAPS],
        grad_taps[TAPS],
        grad_gain_ssm,
        grad_gain_ffn,
    )
    grad_projected, step_low = flow.step((grad_projected, step_low))
    flat = jnp.concatenate([g.reshape(-1) for g in small_grads])
    flat = jnp.pad(flat, (0, -flat.shape[0] % 1024)).reshape(-1, SIDE)
    slot_flat = flow.add(butterfly_stream(flat))
    grad_normed = back(grad_projected, w_input_all) + back(step_low, w_step_all)
    grad_tokens_norm, grad_gain_attn = jax.vjp(rms_norm, own, gain_attn_f)[1](grad_normed)
    grad_low = (grad_middle + grad_tokens_norm).astype(jnp.bfloat16)
    replica = lax.axis_index("rep").reshape(1).astype(jnp.int32)
    line = lax.axis_size("rep") // 2
    held = {}

    def widen(name):
        parts = [line if slot in last else 1 for slot in slots[name]]
        held[name] = widen_rows([slot["result"] for slot in slots[name]], parts, replica)

    grad_low, gain_late, block_all = flow.step((grad_low, grad_gain_attn.reshape(-1, SIDE), block_all))
    slot_grad = flow.add(rows_stream(grad_low))
    slot_late = flow.add(butterfly_stream(gain_late))
    queue = ["late", "small", "down", "gate_up", "block", "output", "tokens", "input"]

    def small_outputs():
        summed = slot_flat["result"].reshape(-1)
        offset = 0
        blocks = []
        for i, grad in zip(SMALL, small_grads):
            block = summed[offset : offset + grad.size].reshape(grad.shape)
            offset += grad.size
            blocks.append(own_block(block, 1 if i == 6 else 0))
        return blocks

    def work(limit):
        for name in list(queue):
            if limit == 0:
                return
            if name in ("late", "small"):
                if not (slot_late if name == "late" else slot_flat)["done"]:
                    continue
                held[name] = small_outputs() if name == "small" else own_block(slot_late["result"].reshape(-1), 0)
                limit += 1
            elif name == "block":
                held["block"] = pick_rows([block_all], jnp.zeros((1,), jnp.int32), target)
            elif name == "tokens":
                if not slot_grad["done"]:
                    continue
                pieces, owners = slot_grad["result"]
                held["tokens"] = pick_rows(pieces, owners * input_rows, target)
            else:
                if not all(slot["done"] for slot in slots[name]):
                    continue
                widen(name)
            queue.remove(name)
            limit -= 1

    boundary = 0
    while flow.live:
        work(PLAN[boundary] if boundary < len(PLAN) else 2)
        held = flow.step(held, [slot for slot in flow.live if slot is not slot_grad] if boundary == 0 else None)
        boundary += 1
    work(len(queue))
    block_out, grad_tokens, widened = held["block"], held["tokens"], held
    outs = [None] * 13
    outs[0] = held["late"]
    for i, name in enumerate(SMALL):
        outs[name] = held["small"][i]
    for i, name in ((1, "input"), (9, "output"), (11, "gate_up"), (12, "down")):
        outs[i] = widened[name]
    return (block_out, grad_tokens, *outs)


def solution(mesh):
    placed = (
        P(("rep", "shard"), None),
        P("rep", None),
        P("rep", None),
        P("shard"),
        P("shard", None),
        P("shard", None),
        P("shard"),
        P("shard"),
        P("shard"),
        P(None, "shard"),
        P("shard"),
        P("shard"),
        P("shard", None),
        P("shard"),
        P("shard", None),
        P("shard", None),
        P(("rep", "shard"), None),
    )
    return jax.shard_map(
        on_device,
        mesh=mesh,
        in_specs=placed,
        out_specs=(
            P(("rep", "shard"), None),
            P(("rep", "shard"), None),
            P("shard"),
            P("shard", None),
            P("shard", None),
            P("shard"),
            P("shard"),
            P("shard"),
            P(None, "shard"),
            P("shard"),
            P("shard"),
            P("shard", None),
            P("shard"),
            P("shard", None),
            P("shard", None),
        ),
        check_vma=False,
    )
```
